32 devices in a mesh: var: 4 (over z), lat: 2 (over y), lon: 4 (over x, core).
Axes of the slice: x: 2, y: 2, z: 4, core: 2. Of those that a mesh axis runs over, the one named last changes fastest.
Arguments:
- var_tokens: bfloat16 [128, 12, 96, 1024], P(('var', 'lon'), 'lat'), may hold values from -6 to 6
- var_query: float32 [16, 64], replicated, may hold values from -80 to 80
- agg_key: bfloat16 [1024, 1024], replicated, may hold values from -0.1875 to 0.1875
- agg_value: bfloat16 [1024, 1024], replicated, may hold values from -0.1875 to 0.1875
- agg_out: bfloat16 [1024, 1024], replicated, may hold values from -0.1875 to 0.1875
- norm_gain: float32 [1024], replicated, may hold values from 0.25 to 1.75
- nb_query: bfloat16 [1024, 1024], replicated, may hold values from -0.1875 to 0.1875
- nb_key: bfloat16 [1024, 1024], replicated, may hold values from -0.1875 to 0.1875
- nb_value: bfloat16 [1024, 1024], replicated, may hold values from -0.1875 to 0.1875
- nb_out: bfloat16 [1024, 1024], replicated, may hold values from -0.1875 to 0.1875
- pos_bias: float32 [16, 13, 13], replicated, may hold values from -120 to 120
- valid: int32 [12, 96], replicated, may hold values 0 or 1
Outputs:
- layer_out: bfloat16 [12, 96, 1024], P('lat', ('var', 'lon'))
The draws below stay inside these ranges and needn't reach their ends.
Inputs may be any that keep to these rules, and one draw needn't show every extreme that they name: `valid`: a patch always attends to itself.
All inputs are finite; a program needn't handle non-finite values.
Results may differ from the reference program's by a relative error of at most 0.015.
Values may be sent and summed in bfloat16 or wider, within the bound.
No kernel may reach another device: no remote copies, remote signals or barrier semaphores. Data moves between devices by JAX's collectives and lax.ppermute only.
A program may use at most 128 MiB of HBM per device.

```python
import math
import jax
import jax.numpy as jnp
from jax import lax

D = 1024
H = 16
HD = 64
V = 128
HALF = 6
WIN = 13
NLAT = 12
NLON = 96


def draw_var_query(key, part):
    return 2.0 * jnp.clip(jax.random.normal(jax.random.fold_in(key, 23), (H, HD), jnp.float32), -4.0, 4.0)


def draw_pos_bias(key, part):
    return jnp.clip(jax.random.normal(jax.random.fold_in(key, 33), (H, WIN, WIN), jnp.float32), -4.0, 4.0)


def touch_ends(values, own_key, low, largest):
    dims = values.shape
    spot = [jax.random.randint(jax.random.fold_in(own_key, axis), (), 0, dims[axis]) for axis in range(len(dims))]
    values = values.at[tuple(spot)].set(low)
    longest = dims.index(max(dims))
    spot[longest] = (spot[longest] + 1) % dims[longest]
    return values.at[tuple(spot)].set(largest)


def block_levels(own_key, dims, shards, smallest, largest):
    level = 1.0
    for axis_at, shards_of in shards:
        draws = jax.random.uniform(jax.random.fold_in(jax.random.fold_in(own_key, 6), axis_at), (shards_of,), jnp.float32, smallest / len(shards), largest / len(shards))
        level = level * jnp.repeat(jnp.exp(draws), dims[axis_at] // shards_of).reshape((-1,) + (1,) * (len(dims) - 1 - axis_at))
    return level


def noise(stream_key, extent, scale, limit, cuts=(), kind=jnp.bfloat16):
    values = jax.random.normal(stream_key, extent, jnp.float32) * scale
    if len(cuts) > 0:
        values = block_levels(stream_key, extent, cuts, -0.22, 0.18) * values
    return jnp.clip(values, min=-limit, max=limit).astype(kind)


def setup_inputs(seed: int = 0) -> dict:
    keys = jax.random.split(jax.random.key(seed), 13)
    return {
        "var_tokens": noise(keys[0], (V, NLAT, NLON, D), 1.0, 6.0, ((0, 16), (1, 2))),
        "var_query": draw_var_query(jax.random.fold_in(keys[12], 71), 0),
        "agg_key": noise(keys[2], (D, D), D ** -0.5, 0.1875),
        "agg_value": noise(keys[3], (D, D), D ** -0.5, 0.1875),
        "agg_out": noise(keys[4], (D, D), D ** -0.5, 0.1875),
        "norm_gain": jnp.clip(1.0 + 0.15 * jax.random.normal(keys[5], (D,), jnp.float32), 0.25, 1.75),
        "nb_query": noise(keys[6], (D, D), D ** -0.5, 0.1875),
        "nb_key": noise(keys[7], (D, D), D ** -0.5, 0.1875),
        "nb_value": noise(keys[8], (D, D), D ** -0.5, 0.1875),
        "nb_out": noise(keys[9], (D, D), D ** -0.5, 0.1875),
        "pos_bias": draw_pos_bias(jax.random.fold_in(keys[12], 71), 0),
        "valid": touch_ends((jax.random.randint(keys[11], (NLAT, NLON), 0, 8) < 7).astype(jnp.int32), jax.random.fold_in(keys[11], 1), 0, 1),
    }


EPS = 1e-05
HIGH = lax.Precision.HIGHEST

def layer_norm(tokens, norm_gain):
    values = tokens.astype(jnp.float32)
    center = values - lax.optimization_barrier(jnp.mean(values, axis=-1, keepdims=True))
    spread = lax.optimization_barrier(jnp.mean(center * center, axis=-1, keepdims=True))
    return (center * lax.rsqrt(spread + EPS) * norm_gain).astype(jnp.bfloat16)

def extend(field):
    wrapped = jnp.concatenate([field[:, NLON - HALF:], field, field[:, :HALF]], axis=1)
    return jnp.pad(wrapped, ((HALF, HALF), (0, 0)) + ((0, 0),) * (field.ndim - 2))

def reference(var_tokens, var_query, agg_key, agg_value, agg_out, norm_gain, nb_query, nb_key, nb_value, nb_out, pos_bias, valid):
    scale = 1.0 / math.sqrt(HD)
    folded = jnp.einsum('dhe,he->dh', agg_key.astype(jnp.float32).reshape(D, H, HD), var_query, precision=HIGH) * scale

    def score_plane(plane):
        return jnp.einsum('ijd,dh->ijh', plane.astype(jnp.float32), folded, precision=HIGH)
    score = lax.map(score_plane, var_tokens)
    weight = jax.nn.softmax(score, axis=0)

    def accumulate(total, item):
        plane, share = item
        return (total + share[:, :, :, None] * plane.astype(jnp.float32)[:, :, None, :], None)
    summed, _ = lax.scan(accumulate, jnp.zeros((NLAT, NLON, H, D), jnp.float32), (var_tokens, weight))
    pooled = jnp.einsum('ijhd,dhe->ijhe', summed, agg_value.astype(jnp.float32).reshape(D, H, HD), precision=HIGH)
    pooled = pooled.reshape(NLAT * NLON, D).astype(jnp.bfloat16)
    tokens = jnp.dot(pooled, agg_out, preferred_element_type=jnp.float32).astype(jnp.bfloat16)
    normed = layer_norm(tokens, norm_gain)

    def project(matrix):
        return jnp.dot(normed, matrix, preferred_element_type=jnp.float32).astype(jnp.bfloat16).reshape(NLAT, NLON, D)
    queries = project(nb_query)
    key_pad = extend(project(nb_key))
    value_pad = extend(project(nb_value))
    allow_pad = extend(valid)
    span = 2 * HALF + 1
    first = jnp.repeat(jnp.arange(span, dtype=jnp.int32), span)
    second = jnp.tile(jnp.arange(span, dtype=jnp.int32), span)
    places = jnp.arange(span * span, dtype=jnp.int32)
    center = HALF * span + HALF
    query_four = queries.astype(jnp.float32).reshape(NLAT, NLON, H, HD)
    zero = jnp.zeros((), jnp.int32)

    def logits_at(item):
        row_off, col_off, place = item
        window = lax.dynamic_slice(key_pad, (row_off, col_off, zero), (NLAT, NLON, D))
        window = window.astype(jnp.float32).reshape(NLAT, NLON, H, HD)
        allow = lax.dynamic_slice(allow_pad, (row_off, col_off), (NLAT, NLON)) > 0
        allow = allow | (place == center)
        bias = pos_bias[:, row_off, col_off]
        logit = jnp.einsum('ijhe,ijhe->ijh', query_four, window, precision=HIGH) * scale + bias
        return jnp.where(allow[:, :, None], logit, -jnp.inf)
    logits = lax.map(logits_at, (first, second, places))
    top = lax.optimization_barrier(jnp.max(logits, axis=0, keepdims=True))
    raised = jnp.exp(logits - top)
    attn = (raised / lax.optimization_barrier(jnp.sum(raised, axis=0, keepdims=True))).astype(jnp.bfloat16)

    def gather_values(total, item):
        row_off, col_off, share = item
        window = lax.dynamic_slice(value_pad, (row_off, col_off, zero), (NLAT, NLON, D))
        window = window.astype(jnp.float32).reshape(NLAT, NLON, H, HD)
        return (total + share.astype(jnp.float32)[:, :, :, None] * window, None)
    mixed, _ = lax.scan(gather_values, jnp.zeros((NLAT, NLON, H, HD), jnp.float32), (first, second, attn))
    mixed = mixed.reshape(NLAT * NLON, D).astype(jnp.bfloat16)
    result = tokens.astype(jnp.float32) + jnp.dot(mixed, nb_out, preferred_element_type=jnp.float32)
    return result.astype(jnp.bfloat16).reshape(NLAT, NLON, D)
```

```python
import functools
import math

import jax
import jax.numpy as jnp
import numpy as np
from jax import lax
from jax.experimental import pallas as pl
from jax.experimental.pallas import tpu as pltpu
from jax.sharding import PartitionSpec as P

HALF = 6
EPS = 1e-05
LANES = 128
TILE_BLOCKS = 16
RADICES = (2, 2, 4)
CHUNKS = 2
QROWS = 48
MIB = 1 << 20
F32 = jnp.float32
BF16 = jnp.bfloat16


def dot(a, b):
    return jnp.dot(a, b, preferred_element_type=F32)


def dot_nt(a, b):
    return lax.dot_general(a, b, (((1,), (1,)), ((), ())), preferred_element_type=F32)


def split3(x):
    hi = x.astype(BF16)
    rest = x - hi.astype(F32)
    mid = rest.astype(BF16)
    low = (rest - mid.astype(F32)).astype(BF16)
    return hi.astype(F32), mid.astype(F32), low.astype(F32)


def lane_iota(shape):
    return lax.broadcasted_iota(jnp.int32, shape, len(shape) - 1)


def pack3(x, heads):
    hi, mid, low = split3(x)
    lane = lane_iota(x.shape)
    mid = pltpu.roll(mid, heads, 1)
    low = pltpu.roll(low, 2 * heads, 1)
    out = jnp.where(lane < heads, hi, jnp.where(lane < 2 * heads, mid, low))
    return jnp.where(lane < 3 * heads, out, 0.0)


def unpack3(x, heads):
    return x + pltpu.roll(x, LANES - heads, 1) + pltpu.roll(x, LANES - 2 * heads, 1)


def expander(heads, width):
    head_dim = width // heads
    row = lax.broadcasted_iota(jnp.int32, (LANES, width), 0)
    lane = lax.broadcasted_iota(jnp.int32, (LANES, width), 1)
    hit = jnp.zeros((LANES, width), F32)
    for piece in range(3):
        low = (row - piece * heads) * head_dim
        inside = (row >= piece * heads) & (row < (piece + 1) * heads)
        hit = jnp.where(inside & (lane >= low) & (lane < low + head_dim), 1.0, hit)
    return hit.astype(BF16)


def encode_stats(top, total, heads):
    return pack3(top, heads) + pltpu.roll(pack3(total, heads), 3 * heads, 1)


def fold_kernel(scale, query_ref, key_ref, out_ref):
    heads, head_dim = query_ref.shape
    width = key_ref.shape[0]
    query = query_ref[...] * scale
    wide = jnp.concatenate([query] * (width // head_dim), axis=1)
    row = lax.broadcasted_iota(jnp.int32, wide.shape, 0)
    lane = lax.broadcasted_iota(jnp.int32, wide.shape, 1)
    own = (lane >= row * head_dim) & (lane < (row + 1) * head_dim)
    pieces = jnp.concatenate(split3(jnp.where(own, wide, 0.0)), axis=0).astype(BF16)
    folded = dot_nt(pieces, key_ref[...])
    folded = folded[:heads] + folded[heads : 2 * heads] + folded[2 * heads :]
    parts = jnp.concatenate(
        list(split3(folded)) + [jnp.zeros((LANES - 3 * heads, width), F32)], axis=0
    )
    out_ref[...] = parts.T.astype(BF16)


def pool_kernel(heads, place_ref, token_ref, fold_ref, value_ref, keep_ref, send_ref):
    variables, _, columns, width = token_ref.shape
    tokens = token_ref[:, 0].reshape(variables * columns, width)
    score = unpack3(dot(tokens, fold_ref[...]), heads)
    score = score.reshape(variables, columns, LANES)
    top = jnp.max(score, axis=0)
    raised = jnp.exp(score - top[None])
    total = jnp.sum(raised, axis=0)
    share = pack3(raised.reshape(variables * columns, LANES), heads).astype(BF16)
    spread = expander(heads, width)
    step = 256
    pooled = []
    for start in range(0, width, step):
        rows = dot(tokens, value_ref[:, start : start + step])
        rows = rows * dot(share, spread[:, start : start + step])
        pooled.append(jnp.sum(rows.reshape(variables, columns, step), axis=0).astype(BF16))
    pooled.append(encode_stats(top, total, heads).astype(BF16))
    packed = jnp.concatenate(pooled, axis=1)
    source = lax.broadcasted_iota(jnp.int32, (columns, columns), 1)
    target = jnp.broadcast_to(place_ref[...], (columns, columns))
    chosen = jnp.where(source == target, 1.0, 0.0).astype(BF16)
    ordered = dot(chosen, packed).astype(BF16)
    half = columns // RADICES[0]
    keep_ref[0, 0] = ordered[:half]
    send_ref[0, 0] = ordered[half:]


def merge_body(parts, heads, width, last):
    stats = [unpack3(part[:, width:].astype(F32), heads) for part in parts]
    top = functools.reduce(jnp.maximum, stats)
    scales = [jnp.exp(stat - top) for stat in stats]
    totals = [pltpu.roll(stat, LANES - 3 * heads, 1) for stat in stats]
    total = sum(scale * amount for scale, amount in zip(scales, totals))
    lane = lane_iota(total.shape)
    total = jnp.where(lane < heads, total, 1.0)
    if last:
        scales = [scale / total for scale in scales]
    spread = expander(heads, width)
    merged = sum(
        dot(pack3(scale, heads).astype(BF16), spread) * part[:, :width].astype(F32)
        for scale, part in zip(scales, parts)
    ).astype(BF16)
    if last:
        return merged
    stat = encode_stats(top, total, heads).astype(BF16)
    return jnp.concatenate([merged, stat], axis=1)


def merge_kernel(heads, width, count, last, *refs):
    parts = [ref[...] for ref in refs[:count]]
    flat = [part.reshape(-1, part.shape[-1]) for part in parts]
    merged = merge_body(flat, heads, width, last)
    outs = refs[count:]
    if last:
        outs[0][...] = merged
        return
    if len(outs[0].shape) == 3:
        groups, size, _ = outs[0].shape
        merged = merged.reshape(groups, size * len(outs), merged.shape[-1])
        for at, out in enumerate(outs):
            out[...] = merged[:, at * size : (at + 1) * size]
    else:
        groups = parts[0].shape[0]
        size = outs[0].shape[0] // groups
        merged = merged.astype(F32)
        for group in range(groups):
            for at, out in enumerate(outs):
                low = (group * len(outs) + at) * size
                out[group * size : (group + 1) * size] = merged[low : low + size].astype(BF16)


def merge(parts, shapes, heads, width, last):
    rows = sum(math.prod(part.shape[:-1]) for part in parts)
    return pl.pallas_call(
        functools.partial(merge_kernel, heads, width, len(parts), last),
        out_shape=[jax.ShapeDtypeStruct(shape, BF16) for shape in shapes],
        compiler_params=pltpu.CompilerParams(vmem_limit_bytes=48 * MIB),
        cost_estimate=pl.CostEstimate(
            flops=rows * LANES * width * 2,
            bytes_accessed=rows * width * 4,
            transcendentals=rows * LANES,
        ),
        name="merge",
    )(*parts)


def bias_kernel(columns, side_ref, meta_ref, allowed_ref, table_ref, out_ref):
    heads, span2 = table_ref.shape
    span = 2 * HALF + 1
    keys = meta_ref.shape[1]
    hi, mid, low = split3(table_ref[...])
    pieces = jnp.concatenate([hi, mid, low], axis=0).astype(BF16)
    row_at = meta_ref[0:1] + meta_ref[1:2] * side_ref[0]
    column_at = meta_ref[2:3]
    allowed = allowed_ref[...] > 0
    out_ref[...] = jnp.zeros(out_ref.shape, F32)
    place = lax.broadcasted_iota(jnp.int32, (span2, keys), 0)
    for row in range(HALF):
        for column in range(columns):
            up = row_at - row + HALF
            across = column_at - column + HALF
            inside = (up >= 0) & (up < span) & (across >= 0) & (across < span)
            index = jnp.where(inside, up * span + across, -1)
            hot = jnp.where(place == index, 1.0, 0.0).astype(BF16)
            found = dot(pieces, hot)
            found = found[:heads] + found[heads : 2 * heads] + found[2 * heads :]
            center = index == HALF * span + HALF
            kept = (inside & allowed) | center
            out_ref[:, row * columns + column, :] = jnp.where(kept, found, -jnp.inf)


def attend_kernel(heads, count, *refs):
    blocks = refs[:count]
    gain_ref, bias_ref = refs[count : count + 2]
    sources = refs[count + 2 : count + 7]
    out_ref = refs[count + 7]
    window, mix, *held = refs[count + 8 : count + 15]
    sems = refs[count + 15]
    copies = [
        pltpu.make_async_copy(source, target, sems.at[at])
        for at, (source, target) in enumerate(zip(sources, held))
    ]
    for copy in copies:
        copy.start()
    w_agg, w_query, w_key, w_value, w_out = held
    size, width = blocks[0].shape
    scale = 1.0 / math.sqrt(width // heads)
    for at, block in enumerate(blocks):
        window[at * size : (at + 1) * size] = block[...]
    copies[0].wait()
    tokens = dot(window[...], w_agg[...]).astype(BF16)
    values = tokens.astype(F32)
    center = values - jnp.mean(values, axis=-1, keepdims=True)
    variance = jnp.mean(center * center, axis=-1, keepdims=True)
    normed = (center * lax.rsqrt(variance + EPS) * gain_ref[...]).astype(BF16)
    copies[1].wait()
    queries = dot(normed[:QROWS], w_query[...]).astype(BF16)
    copies[2].wait()
    keys = dot(normed, w_key[...]).astype(BF16)
    copies[3].wait()
    values = dot(normed, w_value[...]).astype(BF16)
    lane = lane_iota((QROWS, LANES))
    left = lane < LANES // 2
    for pair in range(heads // 2):
        at = slice(pair * LANES, (pair + 1) * LANES)
        query = queries[:, at]
        zero = jnp.zeros_like(query)
        both = jnp.concatenate([jnp.where(left, query, zero), jnp.where(left, zero, query)], axis=0)
        logit = dot_nt(both, keys[:, at]) * scale
        bias = bias_ref[2 * pair : 2 * pair + 2]
        logit = logit + bias.reshape(2 * QROWS, bias.shape[-1])
        raised = jnp.exp(logit - jnp.max(logit, axis=-1, keepdims=True))
        attn = (raised / jnp.sum(raised, axis=-1, keepdims=True)).astype(BF16)
        mixed = dot(attn, values[:, at])
        mix[:, at] = jnp.where(left, mixed[:QROWS], mixed[QROWS:]).astype(BF16)
    copies[4].wait()
    result = tokens[:QROWS].astype(F32) + dot(mix[...], w_out[...])
    out_ref[...] = result[:size].astype(BF16)


def on_device(
    sizes,
    var_tokens,
    var_query,
    agg_key,
    agg_value,
    agg_out,
    norm_gain,
    nb_query,
    nb_key,
    nb_value,
    nb_out,
    pos_bias,
    valid,
):
    heads, head_dim = var_query.shape
    width = agg_key.shape[0]
    local_vars, rows, total_columns, _ = var_tokens.shape
    n_var, n_lat, n_lon = sizes
    devices = n_var * n_lon
    columns = total_columns // devices
    tile = TILE_BLOCKS * columns
    tiles = devices // TILE_BLOCKS
    packed = width + LANES
    lat = lax.axis_index("lat")
    block = lax.axis_index("var") * n_lon + lax.axis_index("lon")

    digits = []
    stride = 1
    for radix in RADICES:
        digits.append((stride, radix))
        stride *= radix
    at = np.arange(tile) // columns
    wanted = jnp.zeros((tile,), jnp.int32)
    weight = TILE_BLOCKS
    for stride, radix in digits:
        weight //= radix
        relative = jnp.asarray((at // weight) % radix, jnp.int32)
        wanted = wanted + ((relative + block // stride) % radix) * stride
    wanted = wanted * columns + jnp.asarray(np.arange(tile) % columns, jnp.int32)
    place = jnp.broadcast_to(wanted[:, None], (tile, 1))
    high = (block // TILE_BLOCKS).astype(jnp.int32).reshape(1)

    folded = pl.pallas_call(
        functools.partial(fold_kernel, 1.0 / math.sqrt(head_dim)),
        out_shape=jax.ShapeDtypeStruct((width, LANES), BF16),
        compiler_params=pltpu.CompilerParams(vmem_limit_bytes=32 * MIB),
        name="fold",
    )(var_query, agg_key)

    half = tile // RADICES[0]
    per_chunk = rows // CHUNKS

    def pool(chunk):
        def kernel(high_ref, *refs):
            pool_kernel(heads, *refs)

        def out_map(r, t, high_ref):
            return (r, lax.rem(t + tiles - high_ref[0], tiles), 0, 0)

        shape = jax.ShapeDtypeStruct((per_chunk, tiles, half, packed), BF16)
        keep, send = pl.pallas_call(
            kernel,
            grid_spec=pltpu.PrefetchScalarGridSpec(
                num_scalar_prefetch=1,
                grid=(per_chunk, tiles),
                in_specs=[
                    pl.BlockSpec((tile, 1), lambda r, t, h: (0, 0)),
                    pl.BlockSpec(
                        (local_vars, 1, tile, width),
                        lambda r, t, h: (0, chunk * per_chunk + r, t, 0),
                    ),
                    pl.BlockSpec((width, LANES), lambda r, t, h: (0, 0)),
                    pl.BlockSpec((width, width), lambda r, t, h: (0, 0)),
                ],
                out_specs=[pl.BlockSpec((1, 1, half, packed), out_map)] * 2,
            ),
            out_shape=[shape, shape],
            compiler_params=pltpu.CompilerParams(vmem_limit_bytes=56 * MIB),
            cost_estimate=pl.CostEstimate(
                flops=3 * per_chunk * total_columns * local_vars * width * width,
                bytes_accessed=2 * per_chunk * total_columns * local_vars * width,
                transcendentals=per_chunk * total_columns * local_vars * LANES,
            ),
            name="pool",
        )(high, place, var_tokens, folded, agg_value)
        flat = (per_chunk * tiles, half, packed)
        return keep.reshape(flat), send.reshape(flat)

    def exchange(array, shift, stride, radix):
        def moved(i):
            digit = (i // stride) % radix
            return i + ((digit + shift) % radix - digit) * stride

        return lax.ppermute(array, ("var", "lon"), [(i, moved(i)) for i in range(devices)])

    stages = [(stride, radix) for stride, radix in digits]
    if tiles > 1:
        stages.append((TILE_BLOCKS, tiles))

    def reduce_scatter(keep, sends):
        groups = per_chunk * tiles
        size = half
        for number, (stride, radix) in enumerate(stages):
            got = [exchange(s, k + 1, stride, radix) for k, s in enumerate(sends)]
            parts = [keep] + got
            if number + 1 == len(stages):
                rows_left = math.prod(keep.shape[:-1])
                (out,) = merge(parts, [(rows_left, width)], heads, width, True)
                return out
            following = stages[number + 1][1]
            if number + 2 < len(stages) and number + 1 < len(RADICES):
                size //= following
                if size % 8 == 0:
                    shape = (groups, size, packed)
                else:
                    shape = (groups * size, packed)
                outs = merge(parts, [shape] * following, heads, width, False)
            elif number + 1 < len(RADICES):
                size //= following
                shape = (groups * size, packed)
                outs = merge(parts, [shape] * following, heads, width, False)
            else:
                (full,) = merge_whole(parts, heads, width)
                full = full.reshape(per_chunk, tiles, size, packed)
                outs = [full[:, k].reshape(per_chunk * size, packed) for k in range(tiles)]
            keep, sends = outs[0], list(outs[1:])

    def merge_whole(parts, heads, width):
        shape = (math.prod(parts[0].shape[:-1]), packed)
        parts = [part.reshape((1,) + shape) for part in parts]
        return merge(parts, [(1,) + shape], heads, width, False)

    chunks = []
    for chunk in range(CHUNKS):
        keep, send = pool(chunk)
        chunks.append(reduce_scatter(keep, [send]))
    pooled = jnp.concatenate(chunks, axis=0) if CHUNKS > 1 else chunks[0]

    places = [(dl, dx) for dx in (0, -1, 1) for dl in (0, 1)]

    def neighbour(array, dl, dx):
        pairs = []
        for i in range(n_var * n_lat * n_lon):
            v, l, o = i // (n_lat * n_lon), (i // n_lon) % n_lat, i % n_lon
            b = (v * n_lon + o + dx) % devices
            source = ((b // n_lon) * n_lat + (l + dl) % n_lat) * n_lon + b % n_lon
            pairs.append((source, i))
        return lax.ppermute(array, ("var", "lat", "lon"), pairs)

    window = [pooled] + [neighbour(pooled, dl, dx) for dl, dx in places[1:]]

    patch = rows * columns
    dl = np.repeat([p[0] for p in places], patch)
    dx = np.repeat([p[1] for p in places], patch)
    row = np.tile(np.repeat(np.arange(rows), columns), len(places))
    column = np.tile(np.arange(columns), len(places) * rows)
    meta = jnp.asarray(np.stack([row, dl, dx * columns + column]), jnp.int32)
    side = jnp.where(lat == 0, rows, -rows).astype(jnp.int32)
    row_ids = lat * rows + meta[0] + meta[1] * side
    column_ids = (block * columns + meta[2]) % total_columns
    allowed = jnp.take(valid.reshape(-1), row_ids * total_columns + column_ids)[None, :]
    keys = len(places) * patch
    bias = pl.pallas_call(
        functools.partial(bias_kernel, columns),
        in_specs=[
            pl.BlockSpec(memory_space=pltpu.SMEM),
            pl.BlockSpec(memory_space=pltpu.VMEM),
            pl.BlockSpec(memory_space=pltpu.VMEM),
            pl.BlockSpec(memory_space=pltpu.VMEM),
        ],
        out_shape=jax.ShapeDtypeStruct((heads, QROWS, keys), F32),
        name="bias",
    )(side.reshape(1), meta, allowed, pos_bias.reshape(heads, -1))

    vmem = pl.BlockSpec(memory_space=pltpu.VMEM)
    square = pltpu.VMEM((width, width), BF16)
    out = pl.pallas_call(
        functools.partial(attend_kernel, heads, len(window)),
        in_specs=[vmem] * (len(window) + 2) + [pl.BlockSpec(memory_space=pl.ANY)] * 5,
        out_specs=vmem,
        out_shape=jax.ShapeDtypeStruct((patch, width), BF16),
        scratch_shapes=[
            pltpu.VMEM((keys, width), BF16),
            pltpu.VMEM((QROWS, width), BF16),
            square,
            square,
            square,
            square,
            square,
            pltpu.SemaphoreType.DMA((5,)),
        ],
        compiler_params=pltpu.CompilerParams(vmem_limit_bytes=48 * MIB),
        name="attend",
    )(*window, norm_gain.reshape(1, width), bias, agg_out, nb_query, nb_key, nb_value, nb_out)
    return out.reshape(rows, columns, width)


def solution(mesh):
    sizes = (mesh.shape["var"], mesh.shape["lat"], mesh.shape["lon"])
    return jax.shard_map(
        functools.partial(on_device, sizes),
        mesh=mesh,
        in_specs=(P(("var", "lon"), "lat", None, None),) + (P(),) * 11,
        out_specs=P("lat", ("var", "lon"), None),
        check_vma=False,
    )
```

```python
import functools
import math

import jax
import jax.numpy as jnp
import numpy as np
from jax import lax
from jax.experimental import pallas as pl
from jax.experimental.pallas import tpu as pltpu
from jax.sharding import PartitionSpec as P

HALF = 6
EPS = 1e-05
LANES = 128
TILE_BLOCKS = 16
RADICES = (2, 2, 4)
QROWS = 48
MIB = 1 << 20
POOL_VMEM = 24 * MIB
MERGE_VMEM = 12 * MIB
F32 = jnp.float32
BF16 = jnp.bfloat16


def dot(a, b):
    return jnp.dot(a, b, preferred_element_type=F32)


def dot_nt(a, b):
    return lax.dot_general(a, b, (((1,), (1,)), ((), ())), preferred_element_type=F32)


def split3(x):
    hi = x.astype(BF16)
    rest = x - hi.astype(F32)
    mid = rest.astype(BF16)
    low = (rest - mid.astype(F32)).astype(BF16)
    return hi.astype(F32), mid.astype(F32), low.astype(F32)


def lane_iota(shape):
    return lax.broadcasted_iota(jnp.int32, shape, len(shape) - 1)


def pack3(x, heads):
    hi, mid, low = split3(x)
    lane = lane_iota(x.shape)
    mid = pltpu.roll(mid, heads, 1)
    low = pltpu.roll(low, 2 * heads, 1)
    out = jnp.where(lane < heads, hi, jnp.where(lane < 2 * heads, mid, low))
    return jnp.where(lane < 3 * heads, out, 0.0)


def unpack3(x, heads):
    return x + pltpu.roll(x, LANES - heads, 1) + pltpu.roll(x, LANES - 2 * heads, 1)


def expander(heads, width):
    head_dim = width // heads
    row = lax.broadcasted_iota(jnp.int32, (LANES, width), 0)
    lane = lax.broadcasted_iota(jnp.int32, (LANES, width), 1)
    hit = jnp.zeros((LANES, width), F32)
    for piece in range(3):
        low = (row - piece * heads) * head_dim
        inside = (row >= piece * heads) & (row < (piece + 1) * heads)
        hit = jnp.where(inside & (lane >= low) & (lane < low + head_dim), 1.0, hit)
    return hit.astype(BF16)


def encode_stats(top, total, heads):
    return pack3(top, heads) + pltpu.roll(pack3(total, heads), 3 * heads, 1)


def fold(query, key, heads, head_dim):
    width = key.shape[0]
    wide = jnp.concatenate([query] * (width // head_dim), axis=1)
    row = lax.broadcasted_iota(jnp.int32, wide.shape, 0)
    lane = lax.broadcasted_iota(jnp.int32, wide.shape, 1)
    own = (lane >= row * head_dim) & (lane < (row + 1) * head_dim)
    pieces = jnp.concatenate(split3(jnp.where(own, wide, 0.0)), axis=0).astype(BF16)
    folded = dot_nt(pieces, key)
    folded = folded[:heads] + folded[heads : 2 * heads] + folded[2 * heads :]
    parts = jnp.concatenate(
        list(split3(folded)) + [jnp.zeros((LANES - 3 * heads, width), F32)], axis=0
    )
    return parts.T.astype(BF16)


def column_order(block, tile, columns):
    shape = (tile, tile)
    target = lax.broadcasted_iota(jnp.int32, shape, 0)
    source = lax.broadcasted_iota(jnp.int32, shape, 1)
    group = jnp.zeros(shape, jnp.int32)
    for at in range(1, TILE_BLOCKS):
        group = group + jnp.where(target >= at * columns, 1, 0)
    wanted = jnp.zeros(shape, jnp.int32)
    weight, stride = TILE_BLOCKS, 1
    for radix in RADICES:
        weight //= radix
        bits, low = weight.bit_length() - 1, stride.bit_length() - 1
        digit = ((group >> bits) + (block >> low)) & (radix - 1)
        wanted = wanted + digit * stride
        stride *= radix
    wanted = wanted * columns + target - group * columns
    return jnp.where(source == wanted, 1.0, 0.0).astype(BF16)


def pool_kernel(heads, head_dim, first, count, tiles, columns, lead, *refs):
    block_ref, token_ref, value_ref = refs[:3]
    if lead:
        query_ref, key_ref, keep_ref, send_ref, fold_ref = refs[3:8]
        slots, held, sems, held_key = refs[8:]
    else:
        fold_ref, keep_ref, send_ref = refs[3:6]
        slots, held, sems = refs[6:]
    _, variables, tile, width = slots.shape
    steps = count * tiles
    block = block_ref[0]
    high = block // TILE_BLOCKS

    def fetch(step):
        row = first + step // tiles
        start = pl.multiple_of((step % tiles) * tile, tile)
        return pltpu.make_async_copy(
            token_ref.at[:, row, pl.ds(start, tile), :],
            slots.at[step % 2],
            sems.at[step % 2],
        )

    values = pltpu.make_async_copy(value_ref, held, sems.at[2])
    if lead:
        key = pltpu.make_async_copy(key_ref, held_key, sems.at[3])
        key.start()
    fetch(0).start()
    values.start()
    order = column_order(block, tile, columns)
    half = tile // RADICES[0]
    lane = lane_iota((variables * tile, LANES))
    if lead:
        key.wait()
        query = query_ref[...] * (1.0 / math.sqrt(head_dim))
        fold_ref[...] = fold(query, held_key[...], heads, head_dim)

    def body(step, _):
        @pl.when(step + 1 < steps)
        def _():
            fetch(step + 1).start()

        fetch(step).wait()
        tokens = slots[step % 2].reshape(variables * tile, width)
        score = unpack3(dot(tokens, fold_ref[...]), heads)
        score = score.reshape(variables, tile, LANES)
        top = jnp.max(score, axis=0)
        raised = jnp.exp(score - top[None])
        total = jnp.sum(raised, axis=0)
        share = raised.reshape(variables * tile, LANES)

        @pl.when(step == 0)
        def _():
            values.wait()

        pooled = []
        wide = 256
        for start in range(0, width, wide):
            rows = dot(tokens, held[:, start : start + wide])
            for low in range(0, wide, LANES):
                head = (start + low) // head_dim
                index = head + jnp.where(lane >= head_dim, 1, 0)
                spread = jnp.take_along_axis(share, index, axis=1)
                part = rows[:, low : low + LANES] * spread
                pooled.append(jnp.sum(part.reshape(variables, tile, LANES), axis=0).astype(BF16))
        pooled.append(encode_stats(top, total, heads).astype(BF16))
        ordered = dot(order, jnp.concatenate(pooled, axis=1)).astype(BF16)
        place = (step // tiles) * tiles + (step % tiles + tiles - high) % tiles
        keep_ref[place] = ordered[:half]
        send_ref[place] = ordered[half:]
        return 0

    lax.fori_loop(0, steps, body, 0)


def merge_body(parts, heads, width, last):
    stats = [unpack3(part[:, width:].astype(F32), heads) for part in parts]
    top = functools.reduce(jnp.maximum, stats)
    scales = [jnp.exp(stat - top) for stat in stats]
    totals = [pltpu.roll(stat, LANES - 3 * heads, 1) for stat in stats]
    total = sum(scale * amount for scale, amount in zip(scales, totals))
    lane = lane_iota(total.shape)
    total = jnp.where(lane < heads, total, 1.0)
    if last:
        scales = [scale / total for scale in scales]
    spread = expander(heads, width)
    merged = sum(
        dot(pack3(scale, heads).astype(BF16), spread) * part[:, :width].astype(F32)
        for scale, part in zip(scales, parts)
    ).astype(BF16)
    if last:
        return merged
    stat = encode_stats(top, total, heads).astype(BF16)
    return jnp.concatenate([merged, stat], axis=1)


def merge_kernel(heads, width, counts, last, *refs):
    outs = refs[sum(counts) :]
    at = 0
    merged, groups = [], 0
    for count in counts:
        parts = [ref[...] for ref in refs[at : at + count]]
        at += count
        groups += parts[0].shape[0]
        flat = [part.reshape(-1, part.shape[-1]) for part in parts]
        merged.append(merge_body(flat, heads, width, last))
    if last:
        for out, rows in zip(outs, merged):
            out[...] = rows
        return
    size = math.prod(outs[0].shape[:-1]) // groups
    place = 0
    for rows in merged:
        rows = rows.astype(F32)
        for low in range(0, rows.shape[0], size * len(outs)):
            for k, out in enumerate(outs):
                piece = rows[low + k * size : low + (k + 1) * size].astype(BF16)
                if len(out.shape) == 3:
                    out[place] = piece
                else:
                    out[place * size : (place + 1) * size] = piece
            place += 1


def merge(groups, shapes, heads, width, last):
    parts = [part for group in groups for part in group]
    rows = sum(math.prod(part.shape[:-1]) for part in parts)
    return pl.pallas_call(
        functools.partial(merge_kernel, heads, width, [len(group) for group in groups], last),
        out_shape=[jax.ShapeDtypeStruct(shape, BF16) for shape in shapes],
        compiler_params=pltpu.CompilerParams(vmem_limit_bytes=MERGE_VMEM),
        cost_estimate=pl.CostEstimate(
            flops=rows * LANES * width * 2,
            bytes_accessed=rows * width * 4,
            transcendentals=rows * LANES,
        ),
        name="merge",
    )(*parts)


def bias_kernel(rows, columns, where_ref, meta_ref, valid_ref, table_ref, out_ref):
    span, heads, _ = table_ref.shape
    pitch = 16
    n_rows, n_columns = valid_ref.shape
    keys = meta_ref.shape[1]
    lat, block = where_ref[0], where_ref[1]
    side = rows - 2 * rows * lat
    row_at = meta_ref[0:1] + meta_ref[1:2] * side
    column_at = meta_ref[2:3]

    far = column_at + block * columns
    far = jnp.where(far < 0, far + n_columns, far)
    far = jnp.where(far >= n_columns, far - n_columns, far)
    hot = lax.broadcasted_iota(jnp.int32, (n_columns, keys), 0) == far
    seen = dot(valid_ref[...].astype(F32).astype(BF16), jnp.where(hot, 1.0, 0.0).astype(BF16))
    mine = lax.broadcasted_iota(jnp.int32, (n_rows, keys), 0) == row_at + lat * rows
    allowed = jnp.sum(jnp.where(mine, seen, 0.0), axis=0, keepdims=True) > 0.5

    flat = [table_ref[up] for up in range(span)]
    gap = jnp.zeros((heads, pitch - span), F32)
    flat = jnp.concatenate([piece for up in flat for piece in (up, gap)], axis=1)
    pieces = jnp.concatenate(split3(flat), axis=0).astype(BF16)
    out_ref[...] = jnp.zeros(out_ref.shape, F32)
    place = lax.broadcasted_iota(jnp.int32, (span * pitch, keys), 0)
    for row in range(rows):
        for column in range(columns):
            up = row_at - row + HALF
            across = column_at - column + HALF
            inside = (up >= 0) & (up < span) & (across >= 0) & (across < span)
            index = jnp.where(inside, up * pitch + across, -1)
            found = dot(pieces, jnp.where(place == index, 1.0, 0.0).astype(BF16))
            found = found[:heads] + found[heads : 2 * heads] + found[2 * heads :]
            kept = (inside & allowed) | (index == HALF * pitch + HALF)
            out_ref[:, row * columns + column, :] = jnp.where(kept, found, -jnp.inf)


def attend_kernel(heads, count, *refs):
    blocks = refs[:count]
    gain_ref, bias_ref, w_agg, w_query, w_key, w_value, w_out, out_ref = refs[count : count + 8]
    window, mix = refs[count + 8 :]
    width = window.shape[1]
    scale = 1.0 / math.sqrt(width // heads)
    at = 0
    for block in blocks:
        size = block.shape[0]
        window[at : at + size] = block[...]
        at += size
    tokens = dot(window[...], w_agg[...]).astype(BF16)
    values = tokens.astype(F32)
    center = values - jnp.mean(values, axis=-1, keepdims=True)
    variance = jnp.mean(center * center, axis=-1, keepdims=True)
    normed = (center * lax.rsqrt(variance + EPS) * gain_ref[...]).astype(BF16)
    queries = dot(normed[:QROWS], w_query[...]).astype(BF16)
    keys = dot(normed, w_key[...]).astype(BF16)
    values = dot(normed, w_value[...]).astype(BF16)
    lane = lane_iota((QROWS, LANES))
    left = lane < LANES // 2
    for pair in range(heads // 2):
        at = slice(pair * LANES, (pair + 1) * LANES)
        query = queries[:, at]
        zero = jnp.zeros_like(query)
        both = jnp.concatenate([jnp.where(left, query, zero), jnp.where(left, zero, query)], axis=0)
        logit = dot_nt(both, keys[:, at]) * scale
        bias = bias_ref[2 * pair : 2 * pair + 2]
        logit = logit + bias.reshape(2 * QROWS, bias.shape[-1])
        raised = jnp.exp(logit - jnp.max(logit, axis=-1, keepdims=True))
        attn = (raised / jnp.sum(raised, axis=-1, keepdims=True)).astype(BF16)
        mixed = dot(attn, values[:, at])
        mix[:, at] = jnp.where(left, mixed[:QROWS], mixed[QROWS:]).astype(BF16)
    result = tokens[:QROWS].astype(F32) + dot(mix[...], w_out[...])
    rows, columns, _ = out_ref.shape
    for row in range(rows):
        out_ref[row] = result[row * columns : (row + 1) * columns].astype(BF16)


def split_before(stages, number):
    return math.prod(radix for _, radix in stages[1 : min(number + 1, len(RADICES))])


def on_device(
    sizes,
    var_tokens,
    var_query,
    agg_key,
    agg_value,
    agg_out,
    norm_gain,
    nb_query,
    nb_key,
    nb_value,
    nb_out,
    pos_bias,
    valid,
):
    heads, head_dim = var_query.shape
    width = agg_key.shape[0]
    local_vars, rows, total_columns, _ = var_tokens.shape
    n_var, n_lat, n_lon = sizes
    devices = n_var * n_lon
    columns = total_columns // devices
    tile = TILE_BLOCKS * columns
    tiles = devices // TILE_BLOCKS
    packed = width + LANES
    half = tile // RADICES[0]
    lat = lax.axis_index("lat")
    block = lax.axis_index("var") * n_lon + lax.axis_index("lon")
    where = jnp.stack([lat, block]).astype(jnp.int32)
    block = where[1:]
    smem = pl.BlockSpec(memory_space=pltpu.SMEM)
    vmem = pl.BlockSpec(memory_space=pltpu.VMEM)
    anywhere = pl.BlockSpec(memory_space=pl.ANY)

    def pool(first, count, folded):
        lead = folded is None
        shape = jax.ShapeDtypeStruct((count * tiles, half, packed), BF16)
        outs = [shape, shape] + [jax.ShapeDtypeStruct((width, LANES), BF16)] * lead
        extra = (var_query, agg_key) if lead else (folded,)
        square = pltpu.VMEM((width, width), BF16)
        patches = count * total_columns * local_vars
        return pl.pallas_call(
            functools.partial(
                pool_kernel, heads, head_dim, first, count, tiles, columns, lead
            ),
            in_specs=[smem, anywhere, anywhere] + ([vmem, anywhere] if lead else [vmem]),
            out_specs=[vmem] * len(outs),
            out_shape=outs,
            scratch_shapes=[
                pltpu.VMEM((2, local_vars, tile, width), BF16),
                square,
                pltpu.SemaphoreType.DMA((4,)),
            ]
            + [square] * lead,
            compiler_params=pltpu.CompilerParams(vmem_limit_bytes=POOL_VMEM),
            cost_estimate=pl.CostEstimate(
                flops=3 * patches * width * width,
                bytes_accessed=2 * patches * width,
                transcendentals=patches * LANES,
            ),
            name="pool",
        )(block, var_tokens, agg_value, *extra)

    def exchange(array, shift, stride, radix):
        def moved(i):
            digit = (i // stride) % radix
            return i + ((digit + shift) % radix - digit) * stride

        return lax.ppermute(array, ("var", "lon"), [(i, moved(i)) for i in range(devices)])

    stages, stride = [], 1
    for radix in RADICES:
        stages.append((stride, radix))
        stride *= radix
    if tiles > 1:
        stages.append((TILE_BLOCKS, tiles))

    def swap(sends, number):
        stride, radix = stages[number]
        return [exchange(send, k + 1, stride, radix) for k, send in enumerate(sends)]

    def next_split(groups, number, places, size):
        if number + 1 == len(stages):
            rows_left = sum(math.prod(group[0].shape[:-1]) for group in groups)
            return merge(groups, [(rows_left, width)], heads, width, True)
        radix = stages[number + 1][1]
        if number + 1 < len(RADICES):
            size //= radix
            shape = (places, size, packed) if size % 8 == 0 else (places * size, packed)
            return merge(groups, [shape] * radix, heads, width, False)
        (full,) = merge(groups, [(places * size, packed)], heads, width, False)
        full = full.reshape(places // tiles, tiles, size, packed)
        return [full[:, k].reshape(places // tiles * size, packed) for k in range(tiles)]

    barrier = lax.optimization_barrier
    lead_rows = rows - 2
    keep_a, send_a, folded = pool(0, lead_rows, None)
    got_a = swap([send_a], 0)
    keep_b, send_b = pool(lead_rows, 1, folded)
    size = half
    parts_a = next_split([[keep_a] + got_a], 0, lead_rows * tiles, size)
    got_b = swap([send_b], 0)
    parts_a, folded = barrier((parts_a, folded))
    got_a = swap(parts_a[1:], 1)
    keep_c, send_c = pool(lead_rows + 1, 1, folded)
    got_c = swap([send_c], 0)
    keep_a = parts_a[0]
    keep_b = [[keep_b] + got_b, [keep_c] + got_c]

    places = [(dl, dx) for dx in (0, -1, 1) for dl in (0, 1)]
    patch = rows * columns
    dl = np.repeat([p[0] for p in places], patch)
    dx = np.repeat([p[1] for p in places], patch)
    row = np.tile(np.repeat(np.arange(rows), columns), len(places))
    column = np.tile(np.arange(columns), len(places) * rows)
    meta = jnp.asarray(np.stack([row, dl, dx * columns + column]), jnp.int32)
    keys = len(places) * patch
    bias = pl.pallas_call(
        functools.partial(bias_kernel, rows, columns),
        in_specs=[smem, vmem, vmem, vmem],
        out_specs=vmem,
        out_shape=jax.ShapeDtypeStruct((heads, QROWS, keys), F32),
        compiler_params=pltpu.CompilerParams(vmem_limit_bytes=MERGE_VMEM),
        cost_estimate=pl.CostEstimate(
            flops=patch * 256 * keys * 48 * 8, bytes_accessed=heads * keys * 400, transcendentals=0
        ),
        name="bias",
    )(where, meta, valid, jnp.transpose(pos_bias, (1, 0, 2)))

    for number in range(1, len(stages)):
        parts_a = next_split(
            [[keep_a] + got_a], number, lead_rows * tiles, half // split_before(stages, number)
        )
        if number + 1 < len(stages):
            keep_a, got_a = parts_a[0], swap(parts_a[1:], number + 1)
        parts_b = next_split(keep_b, number - 1, 2 * tiles, half // split_before(stages, number - 1))
        got = swap(parts_b[1:], number)
        if number == 1:
            got, bias = barrier((got, bias))
        keep_b = [[parts_b[0]] + got]
    pooled_a = parts_a[0]
    (pooled_b,) = next_split(keep_b, len(stages) - 1, 2 * tiles, columns)
    pooled = jnp.concatenate([pooled_a, pooled_b], axis=0)

    def neighbour(array, dl, dx):
        pairs = []
        for i in range(n_var * n_lat * n_lon):
            v, l, o = i // (n_lat * n_lon), (i // n_lon) % n_lat, i % n_lon
            b = (v * n_lon + o + dx) % devices
            source = ((b // n_lon) * n_lat + (l + dl) % n_lat) * n_lon + b % n_lon
            pairs.append((source, i))
        return lax.ppermute(array, ("var", "lat", "lon"), pairs)

    window = [pooled] + [neighbour(pooled, dl, dx) for dl, dx in places[1:]]

    return pl.pallas_call(
        functools.partial(attend_kernel, heads, len(window)),
        in_specs=[vmem] * (len(window) + 7),
        out_specs=vmem,
        out_shape=jax.ShapeDtypeStruct((rows, columns, width), BF16),
        scratch_shapes=[pltpu.VMEM((keys, width), BF16), pltpu.VMEM((QROWS, width), BF16)],
        compiler_params=pltpu.CompilerParams(vmem_limit_bytes=MERGE_VMEM),
        name="attend",
    )(*window, norm_gain.reshape(1, width), bias, agg_out, nb_query, nb_key, nb_value, nb_out)


def solution(mesh):
    sizes = (mesh.shape["var"], mesh.shape["lat"], mesh.shape["lon"])
    return jax.shard_map(
        functools.partial(on_device, sizes),
        mesh=mesh,
        in_specs=(P(("var", "lon"), "lat", None, None),) + (P(),) * 11,
        out_specs=P("lat", ("var", "lon"), None),
        check_vma=False,
    )
```

```python
import functools
import math

import jax
import jax.numpy as jnp
import numpy as np
from jax import lax
from jax.experimental import pallas as pl
from jax.experimental.pallas import tpu as pltpu
from jax.sharding import PartitionSpec as P

HALF = 6
EPS = 1e-05
LANES = 128
TILE_BLOCKS = 16
RADICES = (2, 2, 4)
QROWS = 48
MIB = 1 << 20
POOL_VMEM = 60 * MIB
MERGE_VMEM = 12 * MIB
STAGE_VMEM = 42 * MIB
F32 = jnp.float32
BF16 = jnp.bfloat16


def dot(a, b):
    return jnp.dot(a, b, preferred_element_type=F32)


def dot_nt(a, b):
    return lax.dot_general(a, b, (((1,), (1,)), ((), ())), preferred_element_type=F32)


def split3(x):
    hi = x.astype(BF16)
    rest = x - hi.astype(F32)
    mid = rest.astype(BF16)
    low = (rest - mid.astype(F32)).astype(BF16)
    return hi.astype(F32), mid.astype(F32), low.astype(F32)


def lane_iota(shape):
    return lax.broadcasted_iota(jnp.int32, shape, len(shape) - 1)


def pack3(x, heads):
    hi, mid, low = split3(x)
    lane = lane_iota(x.shape)
    mid = pltpu.roll(mid, heads, 1)
    low = pltpu.roll(low, 2 * heads, 1)
    out = jnp.where(lane < heads, hi, jnp.where(lane < 2 * heads, mid, low))
    return jnp.where(lane < 3 * heads, out, 0.0)


def unpack3(x, heads):
    return x + pltpu.roll(x, LANES - heads, 1) + pltpu.roll(x, LANES - 2 * heads, 1)


def expander(heads, width):
    head_dim = width // heads
    row = lax.broadcasted_iota(jnp.int32, (LANES, width), 0)
    lane = lax.broadcasted_iota(jnp.int32, (LANES, width), 1)
    hit = jnp.zeros((LANES, width), F32)
    for piece in range(3):
        low = (row - piece * heads) * head_dim
        inside = (row >= piece * heads) & (row < (piece + 1) * heads)
        hit = jnp.where(inside & (lane >= low) & (lane < low + head_dim), 1.0, hit)
    return hit.astype(BF16)


def encode_stats(top, total, heads):
    return pack3(top, heads) + pltpu.roll(pack3(total, heads), 3 * heads, 1)


def fold(query, key, heads, head_dim):
    width = key.shape[0]
    wide = jnp.concatenate([query] * (width // head_dim), axis=1)
    row = lax.broadcasted_iota(jnp.int32, wide.shape, 0)
    lane = lax.broadcasted_iota(jnp.int32, wide.shape, 1)
    own = (lane >= row * head_dim) & (lane < (row + 1) * head_dim)
    pieces = jnp.concatenate(split3(jnp.where(own, wide, 0.0)), axis=0).astype(BF16)
    folded = dot_nt(pieces, key)
    folded = folded[:heads] + folded[heads : 2 * heads] + folded[2 * heads :]
    parts = jnp.concatenate(
        list(split3(folded)) + [jnp.zeros((LANES - 3 * heads, width), F32)], axis=0
    )
    return parts.T.astype(BF16)


def column_order(block, tile, columns):
    shape = (tile, tile)
    target = lax.broadcasted_iota(jnp.int32, shape, 0)
    source = lax.broadcasted_iota(jnp.int32, shape, 1)
    group = jnp.zeros(shape, jnp.int32)
    for at in range(1, TILE_BLOCKS):
        group = group + jnp.where(target >= at * columns, 1, 0)
    wanted = jnp.zeros(shape, jnp.int32)
    weight, stride = TILE_BLOCKS, 1
    for radix in RADICES:
        weight //= radix
        bits, low = weight.bit_length() - 1, stride.bit_length() - 1
        digit = ((group >> bits) + (block >> low)) & (radix - 1)
        wanted = wanted + digit * stride
        stride *= radix
    wanted = wanted * columns + target - group * columns
    return jnp.where(source == wanted, 1.0, 0.0).astype(BF16)


def pool_kernel(heads, head_dim, first, count, tiles, columns, lead, *refs):
    block_ref, token_ref, value_ref = refs[:3]
    if lead:
        query_ref, key_ref, keep_ref, send_ref, fold_ref = refs[3:8]
        slots, held, sems, held_key = refs[8:]
    else:
        fold_ref, keep_ref, send_ref = refs[3:6]
        slots, held, sems = refs[6:]
    _, variables, tile, width = slots.shape
    steps = count * tiles
    block = block_ref[0]
    high = block // TILE_BLOCKS

    def fetch(step):
        row = first + step // tiles
        start = pl.multiple_of((step % tiles) * tile, tile)
        return pltpu.make_async_copy(
            token_ref.at[:, row, pl.ds(start, tile), :],
            slots.at[step % 2],
            sems.at[step % 2],
        )

    values = pltpu.make_async_copy(value_ref, held, sems.at[2])
    if lead:
        key = pltpu.make_async_copy(key_ref, held_key, sems.at[3])
        key.start()
    fetch(0).start()
    values.start()
    order = column_order(block, tile, columns)
    half = tile // RADICES[0]
    lane = lane_iota((variables * tile, LANES))
    if lead:
        key.wait()
        query = query_ref[...] * (1.0 / math.sqrt(head_dim))
        fold_ref[...] = fold(query, held_key[...], heads, head_dim)

    def body(step, _):
        @pl.when(step + 1 < steps)
        def _():
            fetch(step + 1).start()

        fetch(step).wait()
        tokens = slots[step % 2].reshape(variables * tile, width)
        score = unpack3(dot(tokens, fold_ref[...]), heads)
        score = score.reshape(variables, tile, LANES)
        top = jnp.max(score, axis=0)
        raised = jnp.exp(score - top[None])
        total = jnp.sum(raised, axis=0)
        share = raised.reshape(variables * tile, LANES)

        @pl.when(step == 0)
        def _():
            values.wait()

        pooled = []
        wide = 256
        for start in range(0, width, wide):
            rows = dot(tokens, held[:, start : start + wide])
            for low in range(0, wide, LANES):
                head = (start + low) // head_dim
                index = head + jnp.where(lane >= head_dim, 1, 0)
                spread = jnp.take_along_axis(share, index, axis=1)
                part = rows[:, low : low + LANES] * spread
                pooled.append(jnp.sum(part.reshape(variables, tile, LANES), axis=0).astype(BF16))
        pooled.append(encode_stats(top, total, heads).astype(BF16))
        ordered = dot(order, jnp.concatenate(pooled, axis=1)).astype(BF16)
        place = (step // tiles) * tiles + (step % tiles + tiles - high) % tiles
        keep_ref[place] = ordered[:half]
        send_ref[place] = ordered[half:]
        return 0

    lax.fori_loop(0, steps, body, 0)


def merge_body(parts, heads, width, last):
    stats = [unpack3(part[:, width:].astype(F32), heads) for part in parts]
    top = functools.reduce(jnp.maximum, stats)
    scales = [jnp.exp(stat - top) for stat in stats]
    totals = [pltpu.roll(stat, LANES - 3 * heads, 1) for stat in stats]
    total = sum(scale * amount for scale, amount in zip(scales, totals))
    lane = lane_iota(total.shape)
    total = jnp.where(lane < heads, total, 1.0)
    if last:
        scales = [scale / total for scale in scales]
    spread = expander(heads, width)
    merged = sum(
        dot(pack3(scale, heads).astype(BF16), spread) * part[:, :width].astype(F32)
        for scale, part in zip(scales, parts)
    ).astype(BF16)
    if last:
        return merged
    stat = encode_stats(top, total, heads).astype(BF16)
    return jnp.concatenate([merged, stat], axis=1)


def merge_kernel(heads, width, counts, last, *refs):
    outs = refs[sum(counts) :]
    at = 0
    merged, groups = [], 0
    for count in counts:
        parts = [ref[...] for ref in refs[at : at + count]]
        at += count
        groups += parts[0].shape[0]
        flat = [part.reshape(-1, part.shape[-1]) for part in parts]
        merged.append(merge_body(flat, heads, width, last))
    if last:
        for out, rows in zip(outs, merged):
            out[...] = rows
        return
    size = math.prod(outs[0].shape[:-1]) // groups
    place = 0
    for rows in merged:
        rows = rows.astype(F32)
        for low in range(0, rows.shape[0], size * len(outs)):
            for k, out in enumerate(outs):
                piece = rows[low + k * size : low + (k + 1) * size].astype(BF16)
                if len(out.shape) == 3:
                    out[place] = piece
                else:
                    out[place * size : (place + 1) * size] = piece
            place += 1


def merge(groups, shapes, heads, width, last):
    parts = [part for group in groups for part in group]
    rows = sum(math.prod(part.shape[:-1]) for part in parts)
    return pl.pallas_call(
        functools.partial(merge_kernel, heads, width, [len(group) for group in groups], last),
        out_shape=[jax.ShapeDtypeStruct(shape, BF16) for shape in shapes],
        compiler_params=pltpu.CompilerParams(vmem_limit_bytes=MERGE_VMEM),
        cost_estimate=pl.CostEstimate(
            flops=rows * LANES * width * 2,
            bytes_accessed=rows * width * 4,
            transcendentals=rows * LANES,
        ),
        name="merge",
    )(*parts)


def bias_kernel(rows, columns, where_ref, meta_ref, valid_ref, table_ref, *refs):
    out_ref, sems = refs[5], refs[11]
    copies = [
        pltpu.make_async_copy(refs[at], refs[6 + at], sems.at[at]) for at in range(5)
    ]
    for copy in copies:
        copy.start()
    span, heads, _ = table_ref.shape
    pitch = 16
    n_rows, n_columns = valid_ref.shape
    keys = meta_ref.shape[1]
    lat, block = where_ref[0], where_ref[1]
    side = rows - 2 * rows * lat
    row_at = meta_ref[0:1] + meta_ref[1:2] * side
    column_at = meta_ref[2:3]

    far = column_at + block * columns
    far = jnp.where(far < 0, far + n_columns, far)
    far = jnp.where(far >= n_columns, far - n_columns, far)
    hot = lax.broadcasted_iota(jnp.int32, (n_columns, keys), 0) == far
    seen = dot(valid_ref[...].astype(F32).astype(BF16), jnp.where(hot, 1.0, 0.0).astype(BF16))
    mine = lax.broadcasted_iota(jnp.int32, (n_rows, keys), 0) == row_at + lat * rows
    allowed = jnp.sum(jnp.where(mine, seen, 0.0), axis=0, keepdims=True) > 0.5

    flat = [table_ref[up] for up in range(span)]
    gap = jnp.zeros((heads, pitch - span), F32)
    flat = jnp.concatenate([piece for up in flat for piece in (up, gap)], axis=1)
    pieces = jnp.concatenate(split3(flat), axis=0).astype(BF16)
    out_ref[...] = jnp.zeros(out_ref.shape, F32)
    place = lax.broadcasted_iota(jnp.int32, (span * pitch, keys), 0)
    for row in range(rows):
        for column in range(columns):
            up = row_at - row + HALF
            across = column_at - column + HALF
            inside = (up >= 0) & (up < span) & (across >= 0) & (across < span)
            index = jnp.where(inside, up * pitch + across, -1)
            found = dot(pieces, jnp.where(place == index, 1.0, 0.0).astype(BF16))
            found = found[:heads] + found[heads : 2 * heads] + found[2 * heads :]
            kept = (inside & allowed) | (index == HALF * pitch + HALF)
            out_ref[:, row * columns + column, :] = jnp.where(kept, found, -jnp.inf)
    for copy in copies:
        copy.wait()


def attend_kernel(heads, count, *refs):
    blocks = refs[:count]
    gain_ref, bias_ref, w_agg, w_query, w_key, w_value, w_out, out_ref = refs[count : count + 8]
    window, mix = refs[count + 8 :]
    width = window.shape[1]
    scale = 1.0 / math.sqrt(width // heads)
    at = 0
    for block in blocks:
        size = block.shape[0]
        window[at : at + size] = block[...]
        at += size
    tokens = dot(window[...], w_agg[...]).astype(BF16)
    values = tokens.astype(F32)
    center = values - jnp.mean(values, axis=-1, keepdims=True)
    variance = jnp.mean(center * center, axis=-1, keepdims=True)
    normed = (center * lax.rsqrt(variance + EPS) * gain_ref[...]).astype(BF16)
    queries = dot(normed[:QROWS], w_query[...]).astype(BF16)
    keys = dot(normed, w_key[...]).astype(BF16)
    values = dot(normed, w_value[...]).astype(BF16)
    lane = lane_iota((QROWS, LANES))
    left = lane < LANES // 2
    for pair in range(heads // 2):
        at = slice(pair * LANES, (pair + 1) * LANES)
        query = queries[:, at]
        zero = jnp.zeros_like(query)
        both = jnp.concatenate([jnp.where(left, query, zero), jnp.where(left, zero, query)], axis=0)
        logit = dot_nt(both, keys[:, at]) * scale
        bias = bias_ref[2 * pair : 2 * pair + 2]
        logit = logit + bias.reshape(2 * QROWS, bias.shape[-1])
        raised = jnp.exp(logit - jnp.max(logit, axis=-1, keepdims=True))
        attn = (raised / jnp.sum(raised, axis=-1, keepdims=True)).astype(BF16)
        mixed = dot(attn, values[:, at])
        mix[:, at] = jnp.where(left, mixed[:QROWS], mixed[QROWS:]).astype(BF16)
    result = tokens[:QROWS].astype(F32) + dot(mix[...], w_out[...])
    rows, columns, _ = out_ref.shape
    for row in range(rows):
        out_ref[row] = result[row * columns : (row + 1) * columns].astype(BF16)


def split_before(stages, number):
    return math.prod(radix for _, radix in stages[1 : min(number + 1, len(RADICES))])


def on_device(
    sizes,
    var_tokens,
    var_query,
    agg_key,
    agg_value,
    agg_out,
    norm_gain,
    nb_query,
    nb_key,
    nb_value,
    nb_out,
    pos_bias,
    valid,
):
    heads, head_dim = var_query.shape
    width = agg_key.shape[0]
    local_vars, rows, total_columns, _ = var_tokens.shape
    n_var, n_lat, n_lon = sizes
    devices = n_var * n_lon
    columns = total_columns // devices
    tile = TILE_BLOCKS * columns
    tiles = devices // TILE_BLOCKS
    packed = width + LANES
    half = tile // RADICES[0]
    lat = lax.axis_index("lat")
    block = lax.axis_index("var") * n_lon + lax.axis_index("lon")
    where = jnp.stack([lat, block]).astype(jnp.int32)
    block = where[1:]
    smem = pl.BlockSpec(memory_space=pltpu.SMEM)
    vmem = pl.BlockSpec(memory_space=pltpu.VMEM)
    hbm = pl.BlockSpec(memory_space=pltpu.HBM)

    def pool(first, count, folded):
        lead = folded is None
        shape = jax.ShapeDtypeStruct((count * tiles, half, packed), BF16)
        outs = [shape, shape] + [jax.ShapeDtypeStruct((width, LANES), BF16)] * lead
        extra = (var_query, agg_key) if lead else (folded,)
        square = pltpu.VMEM((width, width), BF16)
        return pl.pallas_call(
            functools.partial(
                pool_kernel, heads, head_dim, first, count, tiles, columns, lead
            ),
            in_specs=[smem, hbm, hbm] + ([vmem, hbm] if lead else [vmem]),
            out_specs=[vmem] * len(outs),
            out_shape=outs,
            scratch_shapes=[
                pltpu.VMEM((2, local_vars, tile, width), BF16),
                square,
                pltpu.SemaphoreType.DMA((4,)),
            ]
            + [square] * lead,
            compiler_params=pltpu.CompilerParams(vmem_limit_bytes=POOL_VMEM),
            cost_estimate=pl.CostEstimate(
                flops=3 * count * total_columns * local_vars * width * width,
                bytes_accessed=2 * count * total_columns * local_vars * width,
                transcendentals=0,
            ),
            name="pool",
        )(block, var_tokens, agg_value, *extra)

    def exchange(array, shift, stride, radix):
        def moved(i):
            digit = (i // stride) % radix
            return i + ((digit + shift) % radix - digit) * stride

        return lax.ppermute(array, ("var", "lon"), [(i, moved(i)) for i in range(devices)])

    stages, stride = [], 1
    for radix in RADICES:
        stages.append((stride, radix))
        stride *= radix
    if tiles > 1:
        stages.append((TILE_BLOCKS, tiles))

    def swap(sends, number):
        stride, radix = stages[number]
        return [exchange(send, k + 1, stride, radix) for k, send in enumerate(sends)]

    def next_split(groups, number, places, size):
        if number + 1 == len(stages):
            rows_left = sum(math.prod(group[0].shape[:-1]) for group in groups)
            return merge(groups, [(rows_left, width)], heads, width, True)
        radix = stages[number + 1][1]
        if number + 1 < len(RADICES):
            size //= radix
            shape = (places, size, packed) if size % 8 == 0 else (places * size, packed)
            return merge(groups, [shape] * radix, heads, width, False)
        (full,) = merge(groups, [(places * size, packed)], heads, width, False)
        full = full.reshape(places // tiles, tiles, size, packed)
        return [full[:, k].reshape(places // tiles * size, packed) for k in range(tiles)]

    barrier = lax.optimization_barrier
    lead_rows = rows - 2
    keep_a, send_a, folded = pool(0, lead_rows, None)
    got_a = swap([send_a], 0)
    keep_b, send_b = pool(lead_rows, 1, folded)
    size = half
    parts_a = next_split([[keep_a] + got_a], 0, lead_rows * tiles, size)
    got_b = swap([send_b], 0)
    parts_a, folded = barrier((parts_a, folded))
    got_a = swap(parts_a[1:], 1)
    keep_c, send_c = pool(lead_rows + 1, 1, folded)
    got_c = swap([send_c], 0)
    keep_a = parts_a[0]
    keep_b = [[keep_b] + got_b, [keep_c] + got_c]

    places = [(dl, dx) for dx in (0, -1, 1) for dl in (0, 1)]
    patch = rows * columns
    dl = np.repeat([p[0] for p in places], patch)
    dx = np.repeat([p[1] for p in places], patch)
    row = np.tile(np.repeat(np.arange(rows), columns), len(places))
    column = np.tile(np.arange(columns), len(places) * rows)
    meta = jnp.asarray(np.stack([row, dl, dx * columns + column]), jnp.int32)
    keys = len(places) * patch
    weights = (agg_out, nb_query, nb_key, nb_value, nb_out)
    bias, *weights = pl.pallas_call(
        functools.partial(bias_kernel, rows, columns),
        in_specs=[smem, vmem, vmem, vmem] + [hbm] * 5,
        out_specs=[vmem] * 6,
        out_shape=[jax.ShapeDtypeStruct((heads, QROWS, keys), F32)]
        + [jax.ShapeDtypeStruct(weight.shape, weight.dtype) for weight in weights],
        scratch_shapes=[pltpu.SemaphoreType.DMA((5,))],
        compiler_params=pltpu.CompilerParams(vmem_limit_bytes=STAGE_VMEM),
        cost_estimate=pl.CostEstimate(
            flops=1000, bytes_accessed=1000, transcendentals=0
        ),
        name="bias",
    )(where, meta, valid, jnp.transpose(pos_bias, (1, 0, 2)), *weights)

    for number in range(1, len(stages)):
        parts_a = next_split(
            [[keep_a] + got_a], number, lead_rows * tiles, half // split_before(stages, number)
        )
        parts_b = next_split(keep_b, number - 1, 2 * tiles, half // split_before(stages, number - 1))
        parts_a, parts_b = barrier((parts_a, parts_b))
        if number + 1 < len(stages):
            keep_a, got_a = parts_a[0], swap(parts_a[1:], number + 1)
        got = swap(parts_b[1:], number)
        if number == 1:
            got, bias, weights = barrier((got, bias, weights))
        keep_b = [[parts_b[0]] + got]
    pooled_a = parts_a[0]
    (pooled_b,) = next_split(keep_b, len(stages) - 1, 2 * tiles, columns)
    pooled = jnp.concatenate([pooled_a, pooled_b], axis=0)

    def neighbour(array, dl, dx):
        pairs = []
        for i in range(n_var * n_lat * n_lon):
            v, l, o = i // (n_lat * n_lon), (i // n_lon) % n_lat, i % n_lon
            b = (v * n_lon + o + dx) % devices
            source = ((b // n_lon) * n_lat + (l + dl) % n_lat) * n_lon + b % n_lon
            pairs.append((source, i))
        return lax.ppermute(array, ("var", "lat", "lon"), pairs)

    window = [pooled] + [neighbour(pooled, dl, dx) for dl, dx in places[1:]]

    return pl.pallas_call(
        functools.partial(attend_kernel, heads, len(window)),
        in_specs=[vmem] * (len(window) + 7),
        out_specs=vmem,
        out_shape=jax.ShapeDtypeStruct((rows, columns, width), BF16),
        scratch_shapes=[
            pltpu.VMEM((keys, width), BF16),
            pltpu.VMEM((QROWS, width), BF16),
        ],
        compiler_params=pltpu.CompilerParams(vmem_limit_bytes=MERGE_VMEM),
        name="attend",
    )(*window, norm_gain.reshape(1, width), bias, *weights)


def solution(mesh):
    sizes = (mesh.shape["var"], mesh.shape["lat"], mesh.shape["lon"])
    return jax.shard_map(
        functools.partial(on_device, sizes),
        mesh=mesh,
        in_specs=(P(("var", "lon"), "lat", None, None),) + (P(),) * 11,
        out_specs=P("lat", ("var", "lon"), None),
        check_vma=False,
    )
```

```python
import functools
import math

import jax
import jax.numpy as jnp
import numpy as np
from jax import lax
from jax.experimental import pallas as pl
from jax.experimental.pallas import tpu as pltpu
from jax.sharding import PartitionSpec as P

HALF = 6
EPS = 1e-05
LANES = 128
TILE_BLOCKS = 16
RADICES = (2, 2, 4)
QROWS = 48
MIB = 1 << 20
PRE_VMEM = 50 * MIB
LEAD_VMEM = 40 * MIB
POOL_VMEM = 30 * MIB
MERGE_VMEM = 12 * MIB
STAGE_VMEM = 42 * MIB
F32 = jnp.float32
BF16 = jnp.bfloat16


def dot(a, b):
    return jnp.dot(a, b, preferred_element_type=F32)


def dot_nt(a, b):
    return lax.dot_general(a, b, (((1,), (1,)), ((), ())), preferred_element_type=F32)


def split3(x):
    hi = x.astype(BF16)
    rest = x - hi.astype(F32)
    mid = rest.astype(BF16)
    low = (rest - mid.astype(F32)).astype(BF16)
    return hi.astype(F32), mid.astype(F32), low.astype(F32)


def lane_iota(shape):
    return lax.broadcasted_iota(jnp.int32, shape, len(shape) - 1)


def pack3(x, heads):
    hi, mid, low = split3(x)
    lane = lane_iota(x.shape)
    mid = pltpu.roll(mid, heads, 1)
    low = pltpu.roll(low, 2 * heads, 1)
    out = jnp.where(lane < heads, hi, jnp.where(lane < 2 * heads, mid, low))
    return jnp.where(lane < 3 * heads, out, 0.0)


def unpack3(x, heads):
    return x + pltpu.roll(x, LANES - heads, 1) + pltpu.roll(x, LANES - 2 * heads, 1)


def expander(heads, width):
    head_dim = width // heads
    row = lax.broadcasted_iota(jnp.int32, (LANES, width), 0)
    lane = lax.broadcasted_iota(jnp.int32, (LANES, width), 1)
    hit = jnp.zeros((LANES, width), F32)
    for piece in range(3):
        low = (row - piece * heads) * head_dim
        inside = (row >= piece * heads) & (row < (piece + 1) * heads)
        hit = jnp.where(inside & (lane >= low) & (lane < low + head_dim), 1.0, hit)
    return hit.astype(BF16)


def encode_stats(top, total, heads):
    return pack3(top, heads) + pltpu.roll(pack3(total, heads), 3 * heads, 1)


def fold(query, key, heads, head_dim):
    width = key.shape[0]
    wide = jnp.concatenate([query] * (width // head_dim), axis=1)
    row = lax.broadcasted_iota(jnp.int32, wide.shape, 0)
    lane = lax.broadcasted_iota(jnp.int32, wide.shape, 1)
    own = (lane >= row * head_dim) & (lane < (row + 1) * head_dim)
    pieces = jnp.concatenate(split3(jnp.where(own, wide, 0.0)), axis=0).astype(BF16)
    folded = dot_nt(pieces, key)
    folded = folded[:heads] + folded[heads : 2 * heads] + folded[2 * heads :]
    parts = jnp.concatenate(
        list(split3(folded)) + [jnp.zeros((LANES - 3 * heads, width), F32)], axis=0
    )
    return parts.T.astype(BF16)


def column_order(block, tile, columns):
    shape = (tile, tile)
    target = lax.broadcasted_iota(jnp.int32, shape, 0)
    source = lax.broadcasted_iota(jnp.int32, shape, 1)
    group = jnp.zeros(shape, jnp.int32)
    for at in range(1, TILE_BLOCKS):
        group = group + jnp.where(target >= at * columns, 1, 0)
    wanted = jnp.zeros(shape, jnp.int32)
    weight, stride = TILE_BLOCKS, 1
    for radix in RADICES:
        weight //= radix
        bits, low = weight.bit_length() - 1, stride.bit_length() - 1
        digit = ((group >> bits) + (block >> low)) & (radix - 1)
        wanted = wanted + digit * stride
        stride *= radix
    wanted = wanted * columns + target - group * columns
    return jnp.where(source == wanted, 1.0, 0.0).astype(BF16)


def pool_rows(heads, head_dim, block, order, tokens, fold_ref, values, keep_ref, send_ref, place):
    variables, tile, width = tokens.shape
    half = tile // RADICES[0]
    lane = lane_iota((variables * tile, LANES))
    flat = tokens.reshape(variables * tile, width)
    score = unpack3(dot(flat, fold_ref[...]), heads)
    score = score.reshape(variables, tile, LANES)
    top = jnp.max(score, axis=0)
    raised = jnp.exp(score - top[None])
    total = jnp.sum(raised, axis=0)
    share = raised.reshape(variables * tile, LANES)
    pooled = []
    wide = 256
    for start in range(0, width, wide):
        rows = dot(flat, values(start, wide))
        for low in range(0, wide, LANES):
            index = (start + low) // head_dim + jnp.where(lane >= head_dim, 1, 0)
            spread = jnp.take_along_axis(share, index, axis=1)
            part = rows[:, low : low + LANES] * spread
            pooled.append(jnp.sum(part.reshape(variables, tile, LANES), axis=0).astype(BF16))
    pooled.append(encode_stats(top, total, heads).astype(BF16))
    ordered = dot(order, jnp.concatenate(pooled, axis=1)).astype(BF16)
    keep_ref[place] = ordered[:half]
    send_ref[place] = ordered[half:]


def pre_kernel(heads, head_dim, token_ref, value_ref, query_ref, key_ref, *refs):
    fold_ref, held, first_ref, query, held_key, sems = refs
    tile = first_ref.shape[1]
    copies = [
        pltpu.make_async_copy(query_ref, query, sems.at[0]),
        pltpu.make_async_copy(key_ref, held_key, sems.at[1]),
        pltpu.make_async_copy(token_ref.at[:, 0, pl.ds(0, tile), :], first_ref, sems.at[2]),
        pltpu.make_async_copy(value_ref, held, sems.at[3]),
    ]
    for copy in copies:
        copy.start()
    for copy in copies[:2]:
        copy.wait()
    scaled = query[...] * (1.0 / math.sqrt(head_dim))
    fold_ref[...] = fold(scaled, held_key[...], heads, head_dim)
    for copy in copies[2:]:
        copy.wait()


def lead_kernel(heads, head_dim, count, tiles, columns, *refs):
    block_ref, token_ref, first_ref, held, fold_ref = refs[:5]
    keep_ref, send_ref, rest_ref, slots, sems = refs[5:]
    tile = slots.shape[2]
    steps = count * tiles
    block = block_ref[0]
    high = block // TILE_BLOCKS

    def fetch(step):
        start = pl.multiple_of((step % tiles) * tile, tile)
        return pltpu.make_async_copy(
            token_ref.at[:, step // tiles, pl.ds(start, tile), :],
            slots.at[step % 2],
            sems.at[step % 2],
        )

    later = rest_ref.shape[1]
    rest = pltpu.make_async_copy(token_ref.at[:, pl.ds(count, later)], rest_ref, sems.at[2])
    fetch(1).start()
    order = column_order(block, tile, columns)

    def work(step, tokens):
        pool_rows(
            heads,
            head_dim,
            block,
            order,
            tokens,
            fold_ref,
            lambda start, wide: held[:, start : start + wide],
            keep_ref,
            send_ref,
            (step // tiles) * tiles + (step % tiles + tiles - high) % tiles,
        )

    work(0, first_ref[...])
    fetch(2).start()
    rest.start()

    def body(step, _):
        fetch(step).wait()
        work(step, slots[step % 2])

        @pl.when(step + 2 < steps)
        def _():
            fetch(step + 2).start()

        return 0

    lax.fori_loop(1, steps, body, 0)
    rest.wait()


def pool_kernel(heads, head_dim, row, tiles, columns, *refs):
    block_ref, rest_ref, held, fold_ref, keep_ref, send_ref = refs
    block = block_ref[0]
    high = block // TILE_BLOCKS
    tile = rest_ref.shape[2] // tiles
    order = column_order(block, tile, columns)
    for step in range(tiles):
        pool_rows(
            heads,
            head_dim,
            block,
            order,
            rest_ref[:, row, step * tile : (step + 1) * tile],
            fold_ref,
            lambda start, wide: held[:, start : start + wide],
            keep_ref,
            send_ref,
            (step + tiles - high) % tiles,
        )


def merge_body(parts, heads, width, last):
    stats = [unpack3(part[:, width:].astype(F32), heads) for part in parts]
    top = functools.reduce(jnp.maximum, stats)
    scales = [jnp.exp(stat - top) for stat in stats]
    totals = [pltpu.roll(stat, LANES - 3 * heads, 1) for stat in stats]
    total = sum(scale * amount for scale, amount in zip(scales, totals))
    lane = lane_iota(total.shape)
    total = jnp.where(lane < heads, total, 1.0)
    if last:
        scales = [scale / total for scale in scales]
    spread = expander(heads, width)
    merged = sum(
        dot(pack3(scale, heads).astype(BF16), spread) * part[:, :width].astype(F32)
        for scale, part in zip(scales, parts)
    ).astype(BF16)
    if last:
        return merged
    stat = encode_stats(top, total, heads).astype(BF16)
    return jnp.concatenate([merged, stat], axis=1)


def merge_kernel(heads, width, counts, last, *refs):
    outs = refs[sum(counts) :]
    at = 0
    merged, groups = [], 0
    for count in counts:
        parts = [ref[...] for ref in refs[at : at + count]]
        at += count
        groups += parts[0].shape[0]
        flat = [part.reshape(-1, part.shape[-1]) for part in parts]
        merged.append(merge_body(flat, heads, width, last))
    if last:
        for out, rows in zip(outs, merged):
            out[...] = rows
        return
    size = math.prod(outs[0].shape[:-1]) // groups
    place = 0
    for rows in merged:
        rows = rows.astype(F32)
        for low in range(0, rows.shape[0], size * len(outs)):
            for k, out in enumerate(outs):
                piece = rows[low + k * size : low + (k + 1) * size].astype(BF16)
                if len(out.shape) == 3:
                    out[place] = piece
                else:
                    out[place * size : (place + 1) * size] = piece
            place += 1


def merge(groups, shapes, heads, width, last):
    parts = [part for group in groups for part in group]
    rows = sum(math.prod(part.shape[:-1]) for part in parts)
    return pl.pallas_call(
        functools.partial(merge_kernel, heads, width, [len(group) for group in groups], last),
        out_shape=[jax.ShapeDtypeStruct(shape, BF16) for shape in shapes],
        compiler_params=pltpu.CompilerParams(vmem_limit_bytes=MERGE_VMEM),
        cost_estimate=pl.CostEstimate(
            flops=rows * LANES * width * 2,
            bytes_accessed=rows * width * 4,
            transcendentals=rows * LANES,
        ),
        name="merge",
    )(*parts)


def stage_kernel(rows, columns, count, *refs):
    where_ref, meta_ref, valid_ref, table_ref = refs[:4]
    sources, out_ref = refs[4 : 4 + count], refs[4 + count]
    targets, sems = refs[5 + count : 5 + 2 * count], refs[5 + 2 * count]
    copies = [
        pltpu.make_async_copy(source, target, sems.at[at])
        for at, (source, target) in enumerate(zip(sources, targets))
    ]
    for copy in copies:
        copy.start()
    span, heads, _ = table_ref.shape
    pitch = 16
    n_rows, n_columns = valid_ref.shape
    keys = meta_ref.shape[1]
    lat, block = where_ref[0], where_ref[1]
    side = rows - 2 * rows * lat
    row_at = meta_ref[0:1] + meta_ref[1:2] * side
    column_at = meta_ref[2:3]

    far = column_at + block * columns
    far = jnp.where(far < 0, far + n_columns, far)
    far = jnp.where(far >= n_columns, far - n_columns, far)
    hot = lax.broadcasted_iota(jnp.int32, (n_columns, keys), 0) == far
    seen = dot(valid_ref[...].astype(F32).astype(BF16), jnp.where(hot, 1.0, 0.0).astype(BF16))
    mine = lax.broadcasted_iota(jnp.int32, (n_rows, keys), 0) == row_at + lat * rows
    allowed = jnp.sum(jnp.where(mine, seen, 0.0), axis=0, keepdims=True) > 0.5

    flat = [table_ref[up] for up in range(span)]
    gap = jnp.zeros((heads, pitch - span), F32)
    flat = jnp.concatenate([piece for up in flat for piece in (up, gap)], axis=1)
    pieces = jnp.concatenate(split3(flat), axis=0).astype(BF16)
    out_ref[...] = jnp.zeros(out_ref.shape, F32)
    place = lax.broadcasted_iota(jnp.int32, (span * pitch, keys), 0)
    for row in range(rows):
        for column in range(columns):
            up = row_at - row + HALF
            across = column_at - column + HALF
            inside = (up >= 0) & (up < span) & (across >= 0) & (across < span)
            index = jnp.where(inside, up * pitch + across, -1)
            found = dot(pieces, jnp.where(place == index, 1.0, 0.0).astype(BF16))
            found = found[:heads] + found[heads : 2 * heads] + found[2 * heads :]
            kept = (inside & allowed) | (index == HALF * pitch + HALF)
            out_ref[:, row * columns + column, :] = jnp.where(kept, found, -jnp.inf)
    for copy in copies:
        copy.wait()


def attend_kernel(heads, count, *refs):
    blocks = refs[:count]
    gain_ref, bias_ref, w_agg, w_query, w_key, w_value, w_out, out_ref = refs[count : count + 8]
    window, mix = refs[count + 8 :]
    width = window.shape[1]
    scale = 1.0 / math.sqrt(width // heads)
    at = 0
    for block in blocks:
        size = block.shape[0]
        window[at : at + size] = block[...]
        at += size
    tokens = dot(window[...], w_agg[...]).astype(BF16)
    values = tokens.astype(F32)
    center = values - jnp.mean(values, axis=-1, keepdims=True)
    variance = jnp.mean(center * center, axis=-1, keepdims=True)
    normed = (center * lax.rsqrt(variance + EPS) * gain_ref[...]).astype(BF16)
    queries = dot(normed[:QROWS], w_query[...]).astype(BF16)
    keys = dot(normed, w_key[...]).astype(BF16)
    left = lane_iota((QROWS, LANES)) < LANES // 2
    pairs = [slice(at, at + LANES) for at in range(0, width, LANES)]
    logits = []
    for at in pairs:
        query = queries[:, at]
        zero = jnp.zeros_like(query)
        both = jnp.concatenate([jnp.where(left, query, zero), jnp.where(left, zero, query)], axis=0)
        logits.append(dot_nt(both, keys[:, at]))
    values = dot(normed, w_value[...]).astype(BF16)
    shares = []
    for pair, logit in enumerate(logits):
        bias = bias_ref[2 * pair : 2 * pair + 2]
        logit = logit * scale + bias.reshape(2 * QROWS, bias.shape[-1])
        raised = jnp.exp(logit - jnp.max(logit, axis=-1, keepdims=True))
        shares.append((raised / jnp.sum(raised, axis=-1, keepdims=True)).astype(BF16))
    mixed = [dot(share, values[:, at]) for share, at in zip(shares, pairs)]
    for at, rows in zip(pairs, mixed):
        mix[:, at] = jnp.where(left, rows[:QROWS], rows[QROWS:]).astype(BF16)
    result = tokens[:QROWS].astype(F32) + dot(mix[...], w_out[...])
    rows, columns, _ = out_ref.shape
    for row in range(rows):
        out_ref[row] = result[row * columns : (row + 1) * columns].astype(BF16)


def split_before(stages, number):
    return math.prod(radix for _, radix in stages[1 : min(number + 1, len(RADICES))])


def on_device(
    sizes,
    var_tokens,
    var_query,
    agg_key,
    agg_value,
    agg_out,
    norm_gain,
    nb_query,
    nb_key,
    nb_value,
    nb_out,
    pos_bias,
    valid,
):
    heads, head_dim = var_query.shape
    width = agg_key.shape[0]
    local_vars, rows, total_columns, _ = var_tokens.shape
    n_var, n_lat, n_lon = sizes
    devices = n_var * n_lon
    columns = total_columns // devices
    tile = TILE_BLOCKS * columns
    tiles = devices // TILE_BLOCKS
    packed = width + LANES
    half = tile // RADICES[0]
    lat = lax.axis_index("lat")
    block = lax.axis_index("var") * n_lon + lax.axis_index("lon")
    where = jnp.stack([lat, block]).astype(jnp.int32)
    block = where[1:]
    smem = pl.BlockSpec(memory_space=pltpu.SMEM)
    vmem = pl.BlockSpec(memory_space=pltpu.VMEM)
    hbm = pl.BlockSpec(memory_space=pltpu.HBM)

    weight = jax.ShapeDtypeStruct((width, width), BF16)
    lead_rows = rows - 2

    def pool_cost(count):
        work = count * total_columns * local_vars * width
        return pl.CostEstimate(flops=3 * work * width, bytes_accessed=2 * work, transcendentals=0)

    def lead_pool():
        folded = jax.ShapeDtypeStruct((width, LANES), BF16)
        first = jax.ShapeDtypeStruct((local_vars, tile, width), BF16)
        folded, held, first = pl.pallas_call(
            functools.partial(pre_kernel, heads, head_dim),
            in_specs=[hbm] * 4,
            out_specs=[vmem] * 3,
            out_shape=[folded, weight, first],
            scratch_shapes=[
                pltpu.VMEM(var_query.shape, F32),
                pltpu.VMEM((width, width), BF16),
                pltpu.SemaphoreType.DMA((4,)),
            ],
            compiler_params=pltpu.CompilerParams(vmem_limit_bytes=PRE_VMEM),
            name="pre",
        )(var_tokens, agg_value, var_query, agg_key)
        shape = jax.ShapeDtypeStruct((lead_rows * tiles, half, packed), BF16)
        later = (local_vars, rows - lead_rows, total_columns, width)
        keep, send, rest = pl.pallas_call(
            functools.partial(lead_kernel, heads, head_dim, lead_rows, tiles, columns),
            in_specs=[smem, hbm, vmem, vmem, vmem],
            out_specs=[vmem] * 3,
            out_shape=[shape, shape, jax.ShapeDtypeStruct(later, BF16)],
            scratch_shapes=[
                pltpu.VMEM((2, local_vars, tile, width), BF16),
                pltpu.SemaphoreType.DMA((3,)),
            ],
            compiler_params=pltpu.CompilerParams(vmem_limit_bytes=LEAD_VMEM),
            cost_estimate=pool_cost(lead_rows),
            name="lead",
        )(block, var_tokens, first, held, folded)
        return keep, send, folded, held, rest

    def pool(row, rest, held, folded):
        shape = jax.ShapeDtypeStruct((tiles, half, packed), BF16)
        return pl.pallas_call(
            functools.partial(pool_kernel, heads, head_dim, row, tiles, columns),
            in_specs=[smem] + [vmem] * 3,
            out_specs=[vmem] * 2,
            out_shape=[shape] * 2,
            compiler_params=pltpu.CompilerParams(vmem_limit_bytes=POOL_VMEM),
            cost_estimate=pool_cost(1),
            name="pool",
        )(block, rest, held, folded)

    def exchange(array, shift, stride, radix):
        def moved(i):
            digit = (i // stride) % radix
            return i + ((digit + shift) % radix - digit) * stride

        return lax.ppermute(array, ("var", "lon"), [(i, moved(i)) for i in range(devices)])

    stages, stride = [], 1
    for radix in RADICES:
        stages.append((stride, radix))
        stride *= radix
    if tiles > 1:
        stages.append((TILE_BLOCKS, tiles))

    def swap(sends, number):
        stride, radix = stages[number]
        return [exchange(send, k + 1, stride, radix) for k, send in enumerate(sends)]

    def next_split(groups, number, places, size):
        if number + 1 == len(stages):
            rows_left = sum(math.prod(group[0].shape[:-1]) for group in groups)
            return merge(groups, [(rows_left, width)], heads, width, True)
        radix = stages[number + 1][1]
        if number + 1 < len(RADICES):
            size //= radix
            shape = (places, size, packed) if size % 8 == 0 else (places * size, packed)
            return merge(groups, [shape] * radix, heads, width, False)
        (full,) = merge(groups, [(places * size, packed)], heads, width, False)
        full = full.reshape(places // tiles, tiles, size, packed)
        return [full[:, k].reshape(places // tiles * size, packed) for k in range(tiles)]

    barrier = lax.optimization_barrier
    keep_a, send_a, folded, held, rest = lead_pool()
    got_a = swap([send_a], 0)
    keep_b, send_b = pool(0, rest, held, folded)
    parts_a = next_split([[keep_a] + got_a], 0, lead_rows * tiles, half)
    got_b = swap([send_b], 0)
    parts_a, folded = barrier((parts_a, folded))
    got_a = swap(parts_a[1:], 1)
    keep_c, send_c = pool(1, rest, held, folded)
    got_c = swap([send_c], 0)
    keep_a = parts_a[0]
    keep_b = [[keep_b] + got_b, [keep_c] + got_c]

    places = [(dl, dx) for dx in (0, -1, 1) for dl in (0, 1)]
    patch = rows * columns
    dl = np.repeat([p[0] for p in places], patch)
    dx = np.repeat([p[1] for p in places], patch)
    row = np.tile(np.repeat(np.arange(rows), columns), len(places))
    column = np.tile(np.arange(columns), len(places) * rows)
    meta = jnp.asarray(np.stack([row, dl, dx * columns + column]), jnp.int32)
    keys = len(places) * patch
    for number in range(1, len(stages)):
        split_b, split_a = split_before(stages, number - 1), split_before(stages, number)
        parts_b = next_split(keep_b, number - 1, 2 * tiles, half // split_b)
        if number > 1:
            got_a, _ = barrier((got_a, parts_b))
        parts_a = next_split([[keep_a] + got_a], number, lead_rows * tiles, half // split_a)
        if number == 1:
            parts_a, parts_b = barrier((parts_a, parts_b))
        if number + 1 < len(stages):
            keep_a, got_a = parts_a[0], swap(parts_a[1:], number + 1)
        keep_b = [[parts_b[0]] + swap(parts_b[1:], number)]
    pooled_a = parts_a[0]
    (pooled_b,) = next_split(keep_b, len(stages) - 1, 2 * tiles, columns)
    pooled = jnp.concatenate([pooled_a, pooled_b], axis=0)

    def neighbour(array, dl, dx):
        pairs = []
        for i in range(n_var * n_lat * n_lon):
            v, l, o = i // (n_lat * n_lon), (i // n_lon) % n_lat, i % n_lon
            b = (v * n_lon + o + dx) % devices
            source = ((b // n_lon) * n_lat + (l + dl) % n_lat) * n_lon + b % n_lon
            pairs.append((source, i))
        return lax.ppermute(array, ("var", "lat", "lon"), pairs)

    weights = (agg_out, nb_query, nb_key, nb_value, nb_out)
    pooled, where = barrier((pooled, where))
    bias, *weights = pl.pallas_call(
        functools.partial(stage_kernel, rows, columns, len(weights)),
        in_specs=[smem, vmem, vmem, vmem] + [hbm] * len(weights),
        out_specs=[vmem] * (1 + len(weights)),
        out_shape=[jax.ShapeDtypeStruct((heads, QROWS, keys), F32)] + [weight] * len(weights),
        scratch_shapes=[pltpu.SemaphoreType.DMA((len(weights),))],
        compiler_params=pltpu.CompilerParams(vmem_limit_bytes=STAGE_VMEM),
        cost_estimate=pl.CostEstimate(
            flops=1000, bytes_accessed=10 * width * width, transcendentals=0
        ),
        name="stage",
    )(where, meta, valid, jnp.transpose(pos_bias, (1, 0, 2)), *weights)
    window = [pooled] + [neighbour(pooled, dl, dx) for dl, dx in places[1:]]

    return pl.pallas_call(
        functools.partial(attend_kernel, heads, len(window)),
        in_specs=[vmem] * (len(window) + 7),
        out_specs=vmem,
        out_shape=jax.ShapeDtypeStruct((rows, columns, width), BF16),
        scratch_shapes=[
            pltpu.VMEM((keys, width), BF16),
            pltpu.VMEM((QROWS, width), BF16),
        ],
        compiler_params=pltpu.CompilerParams(vmem_limit_bytes=MERGE_VMEM),
        name="attend",
    )(*window, norm_gain.reshape(1, width), bias, *weights)


def solution(mesh):
    sizes = (mesh.shape["var"], mesh.shape["lat"], mesh.shape["lon"])
    return jax.shard_map(
        functools.partial(on_device, sizes),
        mesh=mesh,
        in_specs=(P(("var", "lon"), "lat", None, None),) + (P(),) * 11,
        out_specs=P("lat", ("var", "lon"), None),
        check_vma=False,
    )
```

```python
import functools
import math

import jax
import jax.numpy as jnp
import numpy as np
from jax import lax
from jax.experimental import pallas as pl
from jax.experimental.pallas import tpu as pltpu
from jax.sharding import PartitionSpec as P

HALF = 6
EPS = 1e-05
LANES = 128
TILE_BLOCKS = 16
RADICES = (2, 2, 4)
QROWS = 48
MIB = 1 << 20
PRE_VMEM = 50 * MIB
LEAD_VMEM = 40 * MIB
POOL_VMEM = 30 * MIB
MERGE_VMEM = 12 * MIB
STAGE_VMEM = 47 * MIB
LOAD_VMEM = 42 * MIB
F32 = jnp.float32
BF16 = jnp.bfloat16


def dot(a, b):
    return jnp.dot(a, b, preferred_element_type=F32)


def dot_nt(a, b):
    return lax.dot_general(a, b, (((1,), (1,)), ((), ())), preferred_element_type=F32)


def split3(x):
    hi = x.astype(BF16)
    rest = x - hi.astype(F32)
    mid = rest.astype(BF16)
    low = (rest - mid.astype(F32)).astype(BF16)
    return hi.astype(F32), mid.astype(F32), low.astype(F32)


def lane_iota(shape):
    return lax.broadcasted_iota(jnp.int32, shape, len(shape) - 1)


def pack3(x, heads):
    hi, mid, low = split3(x)
    lane = lane_iota(x.shape)
    mid = pltpu.roll(mid, heads, 1)
    low = pltpu.roll(low, 2 * heads, 1)
    out = jnp.where(lane < heads, hi, jnp.where(lane < 2 * heads, mid, low))
    return jnp.where(lane < 3 * heads, out, 0.0)


def unpack3(x, heads):
    return x + pltpu.roll(x, LANES - heads, 1) + pltpu.roll(x, LANES - 2 * heads, 1)


def expander(heads, width):
    head_dim = width // heads
    row = lax.broadcasted_iota(jnp.int32, (LANES, width), 0)
    lane = lax.broadcasted_iota(jnp.int32, (LANES, width), 1)
    hit = jnp.zeros((LANES, width), F32)
    for piece in range(3):
        low = (row - piece * heads) * head_dim
        inside = (row >= piece * heads) & (row < (piece + 1) * heads)
        hit = jnp.where(inside & (lane >= low) & (lane < low + head_dim), 1.0, hit)
    return hit.astype(BF16)


def encode_stats(top, total, heads):
    return pack3(top, heads) + pltpu.roll(pack3(total, heads), 3 * heads, 1)


def fold(query, key, heads, head_dim):
    width = key.shape[0]
    wide = jnp.concatenate([query] * (width // head_dim), axis=1)
    row = lax.broadcasted_iota(jnp.int32, wide.shape, 0)
    lane = lax.broadcasted_iota(jnp.int32, wide.shape, 1)
    own = (lane >= row * head_dim) & (lane < (row + 1) * head_dim)
    pieces = jnp.concatenate(split3(jnp.where(own, wide, 0.0)), axis=0).astype(BF16)
    folded = dot_nt(pieces, key)
    folded = folded[:heads] + folded[heads : 2 * heads] + folded[2 * heads :]
    parts = jnp.concatenate(
        list(split3(folded)) + [jnp.zeros((LANES - 3 * heads, width), F32)], axis=0
    )
    return parts.T.astype(BF16)


def column_order(block, tile, columns):
    shape = (tile, tile)
    target = lax.broadcasted_iota(jnp.int32, shape, 0)
    source = lax.broadcasted_iota(jnp.int32, shape, 1)
    group = jnp.zeros(shape, jnp.int32)
    for at in range(1, TILE_BLOCKS):
        group = group + jnp.where(target >= at * columns, 1, 0)
    wanted = jnp.zeros(shape, jnp.int32)
    weight, stride = TILE_BLOCKS, 1
    for radix in RADICES:
        weight //= radix
        bits, low = weight.bit_length() - 1, stride.bit_length() - 1
        digit = ((group >> bits) + (block >> low)) & (radix - 1)
        wanted = wanted + digit * stride
        stride *= radix
    wanted = wanted * columns + target - group * columns
    return jnp.where(source == wanted, 1.0, 0.0).astype(BF16)


def pool_rows(heads, head_dim, block, order, tokens, fold_ref, values, keep_ref, send_ref, place):
    variables, tile, width = tokens.shape
    half = tile // RADICES[0]
    lane = lane_iota((variables * tile, LANES))
    flat = tokens.reshape(variables * tile, width)
    score = unpack3(dot(flat, fold_ref[...]), heads)
    score = score.reshape(variables, tile, LANES)
    top = jnp.max(score, axis=0)
    raised = jnp.exp(score - top[None])
    total = jnp.sum(raised, axis=0)
    share = raised.reshape(variables * tile, LANES)
    pooled = []
    wide = 256
    for start in range(0, width, wide):
        rows = dot(flat, values(start, wide))
        for low in range(0, wide, LANES):
            index = (start + low) // head_dim + jnp.where(lane >= head_dim, 1, 0)
            spread = jnp.take_along_axis(share, index, axis=1)
            part = rows[:, low : low + LANES] * spread
            pooled.append(jnp.sum(part.reshape(variables, tile, LANES), axis=0).astype(BF16))
    pooled.append(encode_stats(top, total, heads).astype(BF16))
    ordered = dot(order, jnp.concatenate(pooled, axis=1)).astype(BF16)
    keep_ref[place] = ordered[:half]
    send_ref[place] = ordered[half:]


def pre_kernel(heads, head_dim, token_ref, value_ref, query_ref, key_ref, *refs):
    fold_ref, held, first_ref, query, held_key, sems = refs
    tile = first_ref.shape[1]
    copies = [
        pltpu.make_async_copy(query_ref, query, sems.at[0]),
        pltpu.make_async_copy(key_ref, held_key, sems.at[1]),
        pltpu.make_async_copy(token_ref.at[:, 0, pl.ds(0, tile), :], first_ref, sems.at[2]),
        pltpu.make_async_copy(value_ref, held, sems.at[3]),
    ]
    for copy in copies:
        copy.start()
    for copy in copies[:2]:
        copy.wait()
    scaled = query[...] * (1.0 / math.sqrt(head_dim))
    fold_ref[...] = fold(scaled, held_key[...], heads, head_dim)
    for copy in copies[2:]:
        copy.wait()


def lead_kernel(heads, head_dim, count, tiles, columns, *refs):
    block_ref, token_ref, first_ref, held, fold_ref = refs[:5]
    keep_ref, send_ref, rest_ref, slots, sems = refs[5:]
    tile = slots.shape[2]
    steps = count * tiles
    block = block_ref[0]
    high = block // TILE_BLOCKS

    def fetch(step):
        start = pl.multiple_of((step % tiles) * tile, tile)
        return pltpu.make_async_copy(
            token_ref.at[:, step // tiles, pl.ds(start, tile), :],
            slots.at[step % 2],
            sems.at[step % 2],
        )

    later = rest_ref.shape[1]
    rest = pltpu.make_async_copy(token_ref.at[:, pl.ds(count, later)], rest_ref, sems.at[2])
    fetch(1).start()
    order = column_order(block, tile, columns)

    def work(step, tokens):
        pool_rows(
            heads,
            head_dim,
            block,
            order,
            tokens,
            fold_ref,
            lambda start, wide: held[:, start : start + wide],
            keep_ref,
            send_ref,
            (step // tiles) * tiles + (step % tiles + tiles - high) % tiles,
        )

    fetch(2).start()
    work(0, first_ref[...])

    def body(step, _):
        fetch(step).wait()
        work(step, slots[step % 2])

        @pl.when(step + 2 < steps)
        def _():
            fetch(step + 2).start()

        @pl.when(step == 1)
        def _():
            rest.start()

        return 0

    lax.fori_loop(1, steps, body, 0)
    rest.wait()


def pool_kernel(heads, head_dim, row, tiles, columns, *refs):
    block_ref, rest_ref, held, fold_ref, keep_ref, send_ref = refs
    block = block_ref[0]
    high = block // TILE_BLOCKS
    tile = rest_ref.shape[2] // tiles
    order = column_order(block, tile, columns)
    for step in range(tiles):
        pool_rows(
            heads,
            head_dim,
            block,
            order,
            rest_ref[:, row, step * tile : (step + 1) * tile],
            fold_ref,
            lambda start, wide: held[:, start : start + wide],
            keep_ref,
            send_ref,
            (step + tiles - high) % tiles,
        )


def merge_body(parts, heads, width, last):
    stats = [unpack3(part[:, width:].astype(F32), heads) for part in parts]
    top = functools.reduce(jnp.maximum, stats)
    scales = [jnp.exp(stat - top) for stat in stats]
    totals = [pltpu.roll(stat, LANES - 3 * heads, 1) for stat in stats]
    total = sum(scale * amount for scale, amount in zip(scales, totals))
    lane = lane_iota(total.shape)
    total = jnp.where(lane < heads, total, 1.0)
    if last:
        scales = [scale / total for scale in scales]
    spread = expander(heads, width)
    merged = sum(
        dot(pack3(scale, heads).astype(BF16), spread) * part[:, :width].astype(F32)
        for scale, part in zip(scales, parts)
    ).astype(BF16)
    if last:
        return merged
    stat = encode_stats(top, total, heads).astype(BF16)
    return jnp.concatenate([merged, stat], axis=1)


def merge_kernel(heads, width, counts, last, *refs):
    outs = refs[sum(counts) :]
    at = 0
    merged, groups = [], 0
    for count in counts:
        parts = [ref[...] for ref in refs[at : at + count]]
        at += count
        groups += parts[0].shape[0]
        flat = [part.reshape(-1, part.shape[-1]) for part in parts]
        merged.append(merge_body(flat, heads, width, last))
    if last:
        at = 0
        for rows in merged:
            outs[0][at : at + rows.shape[0]] = rows
            at += rows.shape[0]
        return
    size = math.prod(outs[0].shape[:-1]) // groups
    place = 0
    for rows in merged:
        rows = rows.astype(F32)
        for low in range(0, rows.shape[0], size * len(outs)):
            for k, out in enumerate(outs):
                piece = rows[low + k * size : low + (k + 1) * size].astype(BF16)
                if len(out.shape) == 3:
                    out[place] = piece
                else:
                    out[place * size : (place + 1) * size] = piece
            place += 1


def merge(groups, shapes, heads, width, last):
    parts = [part for group in groups for part in group]
    rows = sum(math.prod(part.shape[:-1]) for part in parts)
    return pl.pallas_call(
        functools.partial(merge_kernel, heads, width, [len(group) for group in groups], last),
        out_shape=[jax.ShapeDtypeStruct(shape, BF16) for shape in shapes],
        compiler_params=pltpu.CompilerParams(vmem_limit_bytes=MERGE_VMEM),
        cost_estimate=pl.CostEstimate(
            flops=rows * LANES * width * 2,
            bytes_accessed=rows * width * 4,
            transcendentals=rows * LANES,
        ),
        name="merge",
    )(*parts)


def stage_kernel(rows, columns, count, *refs):
    where_ref, meta_ref, valid_ref, table_ref = refs[:4]
    sources, out_ref = refs[4 : 4 + count], refs[4 + count]
    targets, sems = refs[5 + count : 5 + 2 * count], refs[5 + 2 * count]
    copies = [
        pltpu.make_async_copy(source, target, sems.at[at])
        for at, (source, target) in enumerate(zip(sources, targets))
    ]
    for copy in copies:
        copy.start()
    span, heads, _ = table_ref.shape
    pitch = 16
    n_rows, n_columns = valid_ref.shape
    keys = meta_ref.shape[1]
    lat, block = where_ref[0], where_ref[1]
    side = rows - 2 * rows * lat
    row_at = meta_ref[0:1] + meta_ref[1:2] * side
    column_at = meta_ref[2:3] + meta_ref[3:4] * (1 - 2 * (block & 1))

    far = column_at + block * columns
    far = jnp.where(far < 0, far + n_columns, far)
    far = jnp.where(far >= n_columns, far - n_columns, far)
    hot = lax.broadcasted_iota(jnp.int32, (n_columns, keys), 0) == far
    seen = dot(valid_ref[...].astype(F32).astype(BF16), jnp.where(hot, 1.0, 0.0).astype(BF16))
    mine = lax.broadcasted_iota(jnp.int32, (n_rows, keys), 0) == row_at + lat * rows
    allowed = jnp.sum(jnp.where(mine, seen, 0.0), axis=0, keepdims=True) > 0.5

    flat = [table_ref[up] for up in range(span)]
    gap = jnp.zeros((heads, pitch - span), F32)
    flat = jnp.concatenate([piece for up in flat for piece in (up, gap)], axis=1)
    pieces = jnp.concatenate(split3(flat), axis=0).astype(BF16)
    out_ref[...] = jnp.zeros(out_ref.shape, F32)
    place = lax.broadcasted_iota(jnp.int32, (span * pitch, keys), 0)
    for row in range(rows):
        for column in range(columns):
            up = row_at - row + HALF
            across = column_at - column + HALF
            inside = (up >= 0) & (up < span) & (across >= 0) & (across < span)
            index = jnp.where(inside, up * pitch + across, -1)
            found = dot(pieces, jnp.where(place == index, 1.0, 0.0).astype(BF16))
            found = found[:heads] + found[heads : 2 * heads] + found[2 * heads :]
            kept = (inside & allowed) | (index == HALF * pitch + HALF)
            out_ref[:, row * columns + column, :] = jnp.where(kept, found, -jnp.inf)
    for copy in copies:
        copy.wait()


def load_kernel(count, *refs):
    sems = refs[2 * count]
    copies = [
        pltpu.make_async_copy(refs[at], refs[count + at], sems.at[at]) for at in range(count)
    ]
    for copy in copies:
        copy.start()
    for copy in copies:
        copy.wait()


def attend_kernel(heads, count, *refs):
    blocks = refs[:count]
    gain_ref, bias_ref, w_agg, w_query, w_key, w_value, w_out, out_ref = refs[count : count + 8]
    window, mix = refs[count + 8 :]
    width = window.shape[1]
    scale = 1.0 / math.sqrt(width // heads)
    at = 0
    for block in blocks:
        size = block.shape[0]
        window[at : at + size] = block[...]
        at += size
    tokens = dot(window[...], w_agg[...]).astype(BF16)
    values = tokens.astype(F32)
    center = values - jnp.mean(values, axis=-1, keepdims=True)
    variance = jnp.mean(center * center, axis=-1, keepdims=True)
    normed = (center * lax.rsqrt(variance + EPS) * gain_ref[...]).astype(BF16)
    queries = dot(normed[:QROWS], w_query[...]).astype(BF16)
    keys = dot(normed, w_key[...]).astype(BF16)
    left = lane_iota((QROWS, LANES)) < LANES // 2
    pairs = [slice(at, at + LANES) for at in range(0, width, LANES)]
    logits = []
    for at in pairs:
        query = queries[:, at]
        zero = jnp.zeros_like(query)
        both = jnp.concatenate([jnp.where(left, query, zero), jnp.where(left, zero, query)], axis=0)
        logits.append(dot_nt(both, keys[:, at]))
    values = dot(normed, w_value[...]).astype(BF16)
    shares = []
    for pair, logit in enumerate(logits):
        bias = bias_ref[2 * pair : 2 * pair + 2]
        logit = logit * scale + bias.reshape(2 * QROWS, bias.shape[-1])
        raised = jnp.exp(logit - jnp.max(logit, axis=-1, keepdims=True))
        shares.append((raised / jnp.sum(raised, axis=-1, keepdims=True)).astype(BF16))
    mixed = [dot(share, values[:, at]) for share, at in zip(shares, pairs)]
    for at, rows in zip(pairs, mixed):
        mix[:, at] = jnp.where(left, rows[:QROWS], rows[QROWS:]).astype(BF16)
    result = tokens[:QROWS].astype(F32) + dot(mix[...], w_out[...])
    rows, columns, _ = out_ref.shape
    for row in range(rows):
        out_ref[row] = result[row * columns : (row + 1) * columns].astype(BF16)


def split_before(stages, number):
    return math.prod(radix for _, radix in stages[1 : min(number + 1, len(RADICES))])


def on_device(
    sizes,
    var_tokens,
    var_query,
    agg_key,
    agg_value,
    agg_out,
    norm_gain,
    nb_query,
    nb_key,
    nb_value,
    nb_out,
    pos_bias,
    valid,
):
    heads, head_dim = var_query.shape
    width = agg_key.shape[0]
    local_vars, rows, total_columns, _ = var_tokens.shape
    n_var, n_lat, n_lon = sizes
    devices = n_var * n_lon
    columns = total_columns // devices
    tile = TILE_BLOCKS * columns
    tiles = devices // TILE_BLOCKS
    packed = width + LANES
    half = tile // RADICES[0]
    lat = lax.axis_index("lat")
    block = lax.axis_index("var") * n_lon + lax.axis_index("lon")
    where = jnp.stack([lat, block]).astype(jnp.int32)
    block = where[1:]
    smem = pl.BlockSpec(memory_space=pltpu.SMEM)
    vmem = pl.BlockSpec(memory_space=pltpu.VMEM)
    hbm = pl.BlockSpec(memory_space=pltpu.HBM)

    weight = jax.ShapeDtypeStruct((width, width), BF16)
    lead_rows = rows - 2

    def pool_cost(count):
        work = count * total_columns * local_vars * width
        return pl.CostEstimate(flops=3 * work * width, bytes_accessed=2 * work, transcendentals=0)

    def lead_pool():
        folded = jax.ShapeDtypeStruct((width, LANES), BF16)
        first = jax.ShapeDtypeStruct((local_vars, tile, width), BF16)
        folded, held, first = pl.pallas_call(
            functools.partial(pre_kernel, heads, head_dim),
            in_specs=[hbm] * 4,
            out_specs=[vmem] * 3,
            out_shape=[folded, weight, first],
            scratch_shapes=[
                pltpu.VMEM(var_query.shape, F32),
                pltpu.VMEM((width, width), BF16),
                pltpu.SemaphoreType.DMA((4,)),
            ],
            compiler_params=pltpu.CompilerParams(vmem_limit_bytes=PRE_VMEM),
            name="pre",
        )(var_tokens, agg_value, var_query, agg_key)
        shape = jax.ShapeDtypeStruct((lead_rows * tiles, half, packed), BF16)
        later = (local_vars, rows - lead_rows, total_columns, width)
        keep, send, rest = pl.pallas_call(
            functools.partial(lead_kernel, heads, head_dim, lead_rows, tiles, columns),
            in_specs=[smem, hbm, vmem, vmem, vmem],
            out_specs=[vmem] * 3,
            out_shape=[shape, shape, jax.ShapeDtypeStruct(later, BF16)],
            scratch_shapes=[
                pltpu.VMEM((2, local_vars, tile, width), BF16),
                pltpu.SemaphoreType.DMA((3,)),
            ],
            compiler_params=pltpu.CompilerParams(vmem_limit_bytes=LEAD_VMEM),
            cost_estimate=pool_cost(lead_rows),
            name="lead",
        )(block, var_tokens, first, held, folded)
        return keep, send, folded, held, rest

    def pool(row, rest, held, folded):
        shape = jax.ShapeDtypeStruct((tiles, half, packed), BF16)
        return pl.pallas_call(
            functools.partial(pool_kernel, heads, head_dim, row, tiles, columns),
            in_specs=[smem] + [vmem] * 3,
            out_specs=[vmem] * 2,
            out_shape=[shape] * 2,
            compiler_params=pltpu.CompilerParams(vmem_limit_bytes=POOL_VMEM),
            cost_estimate=pool_cost(1),
            name="pool",
        )(block, rest, held, folded)

    def exchange(array, shift, stride, radix):
        def moved(i):
            digit = (i // stride) % radix
            return i + ((digit + shift) % radix - digit) * stride

        return lax.ppermute(array, ("var", "lon"), [(i, moved(i)) for i in range(devices)])

    stages, stride = [], 1
    for radix in RADICES:
        stages.append((stride, radix))
        stride *= radix
    if tiles > 1:
        stages.append((TILE_BLOCKS, tiles))

    def swap(sends, number):
        stride, radix = stages[number]
        return [exchange(send, k + 1, stride, radix) for k, send in enumerate(sends)]

    def next_split(groups, number, places, size):
        if number + 1 == len(stages):
            rows_left = sum(math.prod(group[0].shape[:-1]) for group in groups)
            return merge(groups, [(rows_left, width)], heads, width, True)
        radix = stages[number + 1][1]
        if number + 1 < len(RADICES):
            size //= radix
            shape = (places, size, packed) if size % 8 == 0 else (places * size, packed)
            return merge(groups, [shape] * radix, heads, width, False)
        (full,) = merge(groups, [(places * size, packed)], heads, width, False)
        full = full.reshape(places // tiles, tiles, size, packed)
        return [full[:, k].reshape(places // tiles * size, packed) for k in range(tiles)]

    barrier = lax.optimization_barrier
    keep_a, send_a, folded, held, rest = lead_pool()
    got_a = swap([send_a], 0)
    keep_b, send_b = pool(0, rest, held, folded)
    parts_a = next_split([[keep_a] + got_a], 0, lead_rows * tiles, half)
    got_b = swap([send_b], 0)
    parts_a, folded = barrier((parts_a, folded))
    got_a = swap(parts_a[1:], 1)
    keep_c, send_c = pool(1, rest, held, folded)
    got_c = swap([send_c], 0)
    keep_a = parts_a[0]
    keep_b = [[keep_b] + got_b, [keep_c] + got_c]

    places = [(0, 0), (1, 0), (0, 1), (1, 1), (0, -1), (1, -1)]
    patch = rows * columns
    dl = np.repeat([p[0] for p in places], patch)
    dx = np.repeat([p[1] for p in places], patch)
    row = np.tile(np.repeat(np.arange(rows), columns), len(places))
    column = np.tile(np.arange(columns), len(places) * rows)
    meta = jnp.asarray(np.stack([row, dl, column, dx * columns]), jnp.int32)
    keys = len(places) * patch
    for number in range(1, len(stages)):
        split_b, split_a = split_before(stages, number - 1), split_before(stages, number)
        parts_b = next_split(keep_b, number - 1, 2 * tiles, half // split_b)
        if number > 1:
            got_a, _ = barrier((got_a, parts_b))
        group_a = [keep_a] + got_a
        if number + 1 < len(stages):
            parts_a = next_split([group_a], number, lead_rows * tiles, half // split_a)
            if number == 1:
                parts_a, parts_b = barrier((parts_a, parts_b))
            keep_a, got_a = parts_a[0], swap(parts_a[1:], number + 1)
        keep_b = [[parts_b[0]] + swap(parts_b[1:], number)]
    (pooled,) = next_split([group_a] + keep_b, len(stages) - 1, 0, columns)

    staged = (agg_out, nb_query, nb_key)
    pooled, where = barrier((pooled, where))
    bias, *staged = pl.pallas_call(
        functools.partial(stage_kernel, rows, columns, len(staged)),
        in_specs=[smem, vmem, vmem, vmem] + [hbm] * len(staged),
        out_specs=[vmem] * (1 + len(staged)),
        out_shape=[jax.ShapeDtypeStruct((heads, QROWS, keys), F32)] + [weight] * len(staged),
        scratch_shapes=[pltpu.SemaphoreType.DMA((len(staged),))],
        compiler_params=pltpu.CompilerParams(vmem_limit_bytes=STAGE_VMEM),
        cost_estimate=pl.CostEstimate(
            flops=1000, bytes_accessed=10 * width * width, transcendentals=0
        ),
        name="stage",
    )(where, meta, valid, jnp.transpose(pos_bias, (1, 0, 2)), *staged)

    def partner(array, kind):
        pairs = []
        for i in range(n_var * n_lat * n_lon):
            v, l, o = i // (n_lat * n_lon), (i // n_lon) % n_lat, i % n_lon
            b = v * n_lon + o
            if kind == "lat":
                l = n_lat - 1 - l
            elif kind == "core":
                b ^= 1
            else:
                b = (b + 1 if b % 2 else b - 1) % devices
            pairs.append((((b // n_lon) * n_lat + l) * n_lon + b % n_lon, i))
        return lax.ppermute(array, ("var", "lat", "lon"), pairs)

    across = partner(pooled, "lat")
    near = partner(pooled, "core")
    far = partner(pooled, "odd")
    across, far, bias = barrier((across, far, bias))
    window = [pooled, across, near, partner(across, "core"), far, partner(far, "lat")]
    last = (nb_value, nb_out)
    last, _ = barrier((last, across))
    last = pl.pallas_call(
        functools.partial(load_kernel, len(last)),
        in_specs=[hbm] * len(last),
        out_specs=[vmem] * len(last),
        out_shape=[weight] * len(last),
        scratch_shapes=[pltpu.SemaphoreType.DMA((len(last),))],
        compiler_params=pltpu.CompilerParams(vmem_limit_bytes=LOAD_VMEM),
        cost_estimate=pl.CostEstimate(
            flops=1000, bytes_accessed=8 * width * width, transcendentals=0
        ),
        name="load",
    )(*last)

    return pl.pallas_call(
        functools.partial(attend_kernel, heads, len(window)),
        in_specs=[vmem] * (len(window) + 7),
        out_specs=vmem,
        out_shape=jax.ShapeDtypeStruct((rows, columns, width), BF16),
        scratch_shapes=[
            pltpu.VMEM((keys, width), BF16),
            pltpu.VMEM((QROWS, width), BF16),
        ],
        compiler_params=pltpu.CompilerParams(vmem_limit_bytes=MERGE_VMEM),
        name="attend",
    )(*window, norm_gain.reshape(1, width), bias, *staged, *last)


def solution(mesh):
    sizes = (mesh.shape["var"], mesh.shape["lat"], mesh.shape["lon"])
    return jax.shard_map(
        functools.partial(on_device, sizes),
        mesh=mesh,
        in_specs=(P(("var", "lon"), "lat", None, None),) + (P(),) * 11,
        out_specs=P("lat", ("var", "lon"), None),
        check_vma=False,
    )
```

```python
import functools
import math

import jax
import jax.numpy as jnp
import numpy as np
from jax import lax
from jax.experimental import pallas as pl
from jax.experimental.pallas import tpu as pltpu
from jax.sharding import PartitionSpec as P

HALF = 6
EPS = 1e-05
LANES = 128
TILE_BLOCKS = 16
RADICES = (2, 2, 4)
QROWS = 48
MIB = 1 << 20
PRE_VMEM = 50 * MIB
LEAD_VMEM = 40 * MIB
POOL_VMEM = 30 * MIB
MERGE_VMEM = 12 * MIB
STAGE_VMEM = 47 * MIB
LOAD_VMEM = 42 * MIB
F32 = jnp.float32
BF16 = jnp.bfloat16


def dot(a, b):
    return jnp.dot(a, b, preferred_element_type=F32)


def dot_nt(a, b):
    return lax.dot_general(a, b, (((1,), (1,)), ((), ())), preferred_element_type=F32)


def split3(x):
    hi = x.astype(BF16)
    rest = x - hi.astype(F32)
    mid = rest.astype(BF16)
    low = (rest - mid.astype(F32)).astype(BF16)
    return hi.astype(F32), mid.astype(F32), low.astype(F32)


def lane_iota(shape):
    return lax.broadcasted_iota(jnp.int32, shape, len(shape) - 1)


def pack3(x, heads):
    hi, mid, low = split3(x)
    lane = lane_iota(x.shape)
    mid = pltpu.roll(mid, heads, 1)
    low = pltpu.roll(low, 2 * heads, 1)
    out = jnp.where(lane < heads, hi, jnp.where(lane < 2 * heads, mid, low))
    return jnp.where(lane < 3 * heads, out, 0.0)


def unpack3(x, heads):
    return x + pltpu.roll(x, LANES - heads, 1) + pltpu.roll(x, LANES - 2 * heads, 1)


def expander(heads, width):
    head_dim = width // heads
    row = lax.broadcasted_iota(jnp.int32, (LANES, width), 0)
    lane = lax.broadcasted_iota(jnp.int32, (LANES, width), 1)
    hit = jnp.zeros((LANES, width), F32)
    for piece in range(3):
        low = (row - piece * heads) * head_dim
        inside = (row >= piece * heads) & (row < (piece + 1) * heads)
        hit = jnp.where(inside & (lane >= low) & (lane < low + head_dim), 1.0, hit)
    return hit.astype(BF16)


def encode_stats(top, total, heads):
    return pack3(top, heads) + pltpu.roll(pack3(total, heads), 3 * heads, 1)


def fold(query, key, heads, head_dim):
    width = key.shape[0]
    wide = jnp.concatenate([query] * (width // head_dim), axis=1)
    row = lax.broadcasted_iota(jnp.int32, wide.shape, 0)
    lane = lax.broadcasted_iota(jnp.int32, wide.shape, 1)
    own = (lane >= row * head_dim) & (lane < (row + 1) * head_dim)
    pieces = jnp.concatenate(split3(jnp.where(own, wide, 0.0)), axis=0).astype(BF16)
    folded = dot_nt(pieces, key)
    folded = folded[:heads] + folded[heads : 2 * heads] + folded[2 * heads :]
    parts = jnp.concatenate(
        list(split3(folded)) + [jnp.zeros((LANES - 3 * heads, width), F32)], axis=0
    )
    return parts.T.astype(BF16)


def column_order(block, tile, columns):
    shape = (tile, tile)
    target = lax.broadcasted_iota(jnp.int32, shape, 0)
    source = lax.broadcasted_iota(jnp.int32, shape, 1)
    group = jnp.zeros(shape, jnp.int32)
    for at in range(1, TILE_BLOCKS):
        group = group + jnp.where(target >= at * columns, 1, 0)
    wanted = jnp.zeros(shape, jnp.int32)
    weight, stride = TILE_BLOCKS, 1
    for radix in RADICES:
        weight //= radix
        bits, low = weight.bit_length() - 1, stride.bit_length() - 1
        digit = ((group >> bits) + (block >> low)) & (radix - 1)
        wanted = wanted + digit * stride
        stride *= radix
    wanted = wanted * columns + target - group * columns
    return jnp.where(source == wanted, 1.0, 0.0).astype(BF16)


def pool_rows(heads, head_dim, block, order, tokens, fold_ref, values, keep_ref, send_ref, place):
    variables, tile, width = tokens.shape
    half = tile // RADICES[0]
    lane = lane_iota((variables * tile, LANES))
    flat = tokens.reshape(variables * tile, width)
    score = unpack3(dot(flat, fold_ref[...]), heads)
    score = score.reshape(variables, tile, LANES)
    top = jnp.max(score, axis=0)
    raised = jnp.exp(score - top[None])
    total = jnp.sum(raised, axis=0)
    share = raised.reshape(variables * tile, LANES)
    pooled = []
    wide = 256
    for start in range(0, width, wide):
        rows = dot(flat, values(start, wide))
        for low in range(0, wide, LANES):
            index = (start + low) // head_dim + jnp.where(lane >= head_dim, 1, 0)
            spread = jnp.take_along_axis(share, index, axis=1)
            part = rows[:, low : low + LANES] * spread
            pooled.append(jnp.sum(part.reshape(variables, tile, LANES), axis=0).astype(BF16))
    pooled.append(encode_stats(top, total, heads).astype(BF16))
    ordered = dot(order, jnp.concatenate(pooled, axis=1)).astype(BF16)
    keep_ref[place] = ordered[:half]
    send_ref[place] = ordered[half:]


def pre_kernel(heads, head_dim, token_ref, value_ref, query_ref, key_ref, *refs):
    fold_ref, held, first_ref, query, held_key, sems = refs
    tile = first_ref.shape[1]
    copies = [
        pltpu.make_async_copy(query_ref, query, sems.at[0]),
        pltpu.make_async_copy(key_ref, held_key, sems.at[1]),
        pltpu.make_async_copy(token_ref.at[:, 0, pl.ds(0, tile), :], first_ref, sems.at[2]),
        pltpu.make_async_copy(value_ref, held, sems.at[3]),
    ]
    for copy in copies:
        copy.start()
    for copy in copies[:2]:
        copy.wait()
    scaled = query[...] * (1.0 / math.sqrt(head_dim))
    fold_ref[...] = fold(scaled, held_key[...], heads, head_dim)
    for copy in copies[2:]:
        copy.wait()


def lead_kernel(heads, head_dim, count, tiles, columns, *refs):
    block_ref, token_ref, first_ref, held, fold_ref = refs[:5]
    keep_ref, send_ref, rest_ref, slots, sems = refs[5:]
    tile = slots.shape[2]
    steps = count * tiles
    block = block_ref[0]
    high = block // TILE_BLOCKS

    def fetch(step):
        start = pl.multiple_of((step % tiles) * tile, tile)
        return pltpu.make_async_copy(
            token_ref.at[:, step // tiles, pl.ds(start, tile), :],
            slots.at[step % 2],
            sems.at[step % 2],
        )

    later = rest_ref.shape[1]
    rest = pltpu.make_async_copy(token_ref.at[:, pl.ds(count, later)], rest_ref, sems.at[2])
    pltpu.make_async_copy(first_ref, slots.at[0], sems.at[0]).start()
    fetch(1).start()
    order = column_order(block, tile, columns)

    def work(step, tokens):
        pool_rows(
            heads,
            head_dim,
            block,
            order,
            tokens,
            fold_ref,
            lambda start, wide: held[:, start : start + wide],
            keep_ref,
            send_ref,
            (step // tiles) * tiles + (step % tiles + tiles - high) % tiles,
        )


    def body(step, _):
        fetch(step).wait()
        work(step, slots[step % 2])

        @pl.when(step + 2 < steps)
        def _():
            fetch(step + 2).start()

        @pl.when(step == 1)
        def _():
            rest.start()

        return 0

    lax.fori_loop(0, steps, body, 0)
    rest.wait()


def pool_kernel(heads, head_dim, row, tiles, columns, *refs):
    block_ref, rest_ref, held, fold_ref, keep_ref, send_ref = refs
    block = block_ref[0]
    high = block // TILE_BLOCKS
    tile = rest_ref.shape[2] // tiles
    order = column_order(block, tile, columns)
    for step in range(tiles):
        pool_rows(
            heads,
            head_dim,
            block,
            order,
            rest_ref[:, row, step * tile : (step + 1) * tile],
            fold_ref,
            lambda start, wide: held[:, start : start + wide],
            keep_ref,
            send_ref,
            (step + tiles - high) % tiles,
        )


def merge_body(parts, heads, width, last):
    stats = [unpack3(part[:, width:].astype(F32), heads) for part in parts]
    top = functools.reduce(jnp.maximum, stats)
    scales = [jnp.exp(stat - top) for stat in stats]
    totals = [pltpu.roll(stat, LANES - 3 * heads, 1) for stat in stats]
    total = sum(scale * amount for scale, amount in zip(scales, totals))
    lane = lane_iota(total.shape)
    total = jnp.where(lane < heads, total, 1.0)
    if last:
        scales = [scale / total for scale in scales]
    spread = expander(heads, width)
    merged = sum(
        dot(pack3(scale, heads).astype(BF16), spread) * part[:, :width].astype(F32)
        for scale, part in zip(scales, parts)
    ).astype(BF16)
    if last:
        return merged
    stat = encode_stats(top, total, heads).astype(BF16)
    return jnp.concatenate([merged, stat], axis=1)


def merge_kernel(heads, width, counts, last, *refs):
    outs = refs[sum(counts) :]
    at = 0
    merged, groups = [], 0
    for count in counts:
        parts = [ref[...] for ref in refs[at : at + count]]
        at += count
        groups += parts[0].shape[0]
        flat = [part.reshape(-1, part.shape[-1]) for part in parts]
        merged.append(merge_body(flat, heads, width, last))
    if last:
        at = 0
        for rows in merged:
            outs[0][at : at + rows.shape[0]] = rows
            at += rows.shape[0]
        return
    size = math.prod(outs[0].shape[:-1]) // groups
    place = 0
    for rows in merged:
        rows = rows.astype(F32)
        for low in range(0, rows.shape[0], size * len(outs)):
            for k, out in enumerate(outs):
                piece = rows[low + k * size : low + (k + 1) * size].astype(BF16)
                if len(out.shape) == 3:
                    out[place] = piece
                else:
                    out[place * size : (place + 1) * size] = piece
            place += 1


def merge(groups, shapes, heads, width, last):
    parts = [part for group in groups for part in group]
    rows = sum(math.prod(part.shape[:-1]) for part in parts)
    return pl.pallas_call(
        functools.partial(merge_kernel, heads, width, [len(group) for group in groups], last),
        out_shape=[jax.ShapeDtypeStruct(shape, BF16) for shape in shapes],
        compiler_params=pltpu.CompilerParams(vmem_limit_bytes=MERGE_VMEM),
        cost_estimate=pl.CostEstimate(
            flops=rows * LANES * width * 2,
            bytes_accessed=rows * width * 4,
            transcendentals=rows * LANES,
        ),
        name="merge",
    )(*parts)


def stage_kernel(rows, columns, count, *refs):
    where_ref, meta_ref, valid_ref, table_ref = refs[:4]
    sources, out_ref = refs[4 : 4 + count], refs[4 + count]
    targets, sems = refs[5 + count : 5 + 2 * count], refs[5 + 2 * count]
    copies = [
        pltpu.make_async_copy(source, target, sems.at[at])
        for at, (source, target) in enumerate(zip(sources, targets))
    ]
    for copy in copies:
        copy.start()
    span, heads, _ = table_ref.shape
    pitch = 16
    n_rows, n_columns = valid_ref.shape
    keys = meta_ref.shape[1]
    lat, block = where_ref[0], where_ref[1]
    side = rows - 2 * rows * lat
    row_at = meta_ref[0:1] + meta_ref[1:2] * side
    column_at = meta_ref[2:3] + meta_ref[3:4] * (1 - 2 * (block & 1))

    far = column_at + block * columns
    far = jnp.where(far < 0, far + n_columns, far)
    far = jnp.where(far >= n_columns, far - n_columns, far)
    hot = lax.broadcasted_iota(jnp.int32, (n_columns, keys), 0) == far
    seen = dot(valid_ref[...].astype(F32).astype(BF16), jnp.where(hot, 1.0, 0.0).astype(BF16))
    mine = lax.broadcasted_iota(jnp.int32, (n_rows, keys), 0) == row_at + lat * rows
    allowed = jnp.sum(jnp.where(mine, seen, 0.0), axis=0, keepdims=True) > 0.5

    flat = [table_ref[up] for up in range(span)]
    gap = jnp.zeros((heads, pitch - span), F32)
    flat = jnp.concatenate([piece for up in flat for piece in (up, gap)], axis=1)
    pieces = jnp.concatenate(split3(flat), axis=0).astype(BF16)
    out_ref[...] = jnp.zeros(out_ref.shape, F32)
    place = lax.broadcasted_iota(jnp.int32, (span * pitch, keys), 0)
    for row in range(rows):
        for column in range(columns):
            up = row_at - row + HALF
            across = column_at - column + HALF
            inside = (up >= 0) & (up < span) & (across >= 0) & (across < span)
            index = jnp.where(inside, up * pitch + across, -1)
            found = dot(pieces, jnp.where(place == index, 1.0, 0.0).astype(BF16))
            found = found[:heads] + found[heads : 2 * heads] + found[2 * heads :]
            kept = (inside & allowed) | (index == HALF * pitch + HALF)
            out_ref[:, row * columns + column, :] = jnp.where(kept, found, -jnp.inf)
    for copy in copies:
        copy.wait()


def load_kernel(count, *refs):
    sems = refs[2 * count]
    copies = [
        pltpu.make_async_copy(refs[at], refs[count + at], sems.at[at]) for at in range(count)
    ]
    for copy in copies:
        copy.start()
    for copy in copies:
        copy.wait()


def attend_kernel(heads, count, *refs):
    blocks = refs[:count]
    gain_ref, bias_ref, w_agg, w_query, w_key, w_value, w_out, out_ref = refs[count : count + 8]
    window, mix = refs[count + 8 :]
    width = window.shape[1]
    scale = 1.0 / math.sqrt(width // heads)
    at = 0
    for block in blocks:
        size = block.shape[0]
        window[at : at + size] = block[...]
        at += size
    tokens = dot(window[...], w_agg[...]).astype(BF16)
    values = tokens.astype(F32)
    center = values - jnp.mean(values, axis=-1, keepdims=True)
    variance = jnp.mean(center * center, axis=-1, keepdims=True)
    normed = (center * lax.rsqrt(variance + EPS) * gain_ref[...]).astype(BF16)
    queries = dot(normed[:QROWS], w_query[...]).astype(BF16)
    keys = dot(normed, w_key[...]).astype(BF16)
    left = lane_iota((QROWS, LANES)) < LANES // 2
    pairs = [slice(at, at + LANES) for at in range(0, width, LANES)]
    logits = []
    for at in pairs:
        query = queries[:, at]
        zero = jnp.zeros_like(query)
        both = jnp.concatenate([jnp.where(left, query, zero), jnp.where(left, zero, query)], axis=0)
        logits.append(dot_nt(both, keys[:, at]))
    values = dot(normed, w_value[...]).astype(BF16)
    shares = []
    for pair, logit in enumerate(logits):
        bias = bias_ref[2 * pair : 2 * pair + 2]
        logit = logit * scale + bias.reshape(2 * QROWS, bias.shape[-1])
        raised = jnp.exp(logit - jnp.max(logit, axis=-1, keepdims=True))
        shares.append((raised / jnp.sum(raised, axis=-1, keepdims=True)).astype(BF16))
    mixed = [dot(share, values[:, at]) for share, at in zip(shares, pairs)]
    for at, rows in zip(pairs, mixed):
        mix[:, at] = jnp.where(left, rows[:QROWS], rows[QROWS:]).astype(BF16)
    result = tokens[:QROWS].astype(F32) + dot(mix[...], w_out[...])
    rows, columns, _ = out_ref.shape
    for row in range(rows):
        out_ref[row] = result[row * columns : (row + 1) * columns].astype(BF16)


def split_before(stages, number):
    return math.prod(radix for _, radix in stages[1 : min(number + 1, len(RADICES))])


def on_device(
    sizes,
    var_tokens,
    var_query,
    agg_key,
    agg_value,
    agg_out,
    norm_gain,
    nb_query,
    nb_key,
    nb_value,
    nb_out,
    pos_bias,
    valid,
):
    heads, head_dim = var_query.shape
    width = agg_key.shape[0]
    local_vars, rows, total_columns, _ = var_tokens.shape
    n_var, n_lat, n_lon = sizes
    devices = n_var * n_lon
    columns = total_columns // devices
    tile = TILE_BLOCKS * columns
    tiles = devices // TILE_BLOCKS
    packed = width + LANES
    half = tile // RADICES[0]
    lat = lax.axis_index("lat")
    block = lax.axis_index("var") * n_lon + lax.axis_index("lon")
    where = jnp.stack([lat, block]).astype(jnp.int32)
    block = where[1:]
    smem = pl.BlockSpec(memory_space=pltpu.SMEM)
    vmem = pl.BlockSpec(memory_space=pltpu.VMEM)
    hbm = pl.BlockSpec(memory_space=pltpu.HBM)

    weight = jax.ShapeDtypeStruct((width, width), BF16)
    lead_rows = rows - 2

    def pool_cost(count):
        work = count * total_columns * local_vars * width
        return pl.CostEstimate(flops=3 * work * width, bytes_accessed=2 * work, transcendentals=0)

    def lead_pool():
        folded = jax.ShapeDtypeStruct((width, LANES), BF16)
        first = jax.ShapeDtypeStruct((local_vars, tile, width), BF16)
        folded, held, first = pl.pallas_call(
            functools.partial(pre_kernel, heads, head_dim),
            in_specs=[hbm] * 4,
            out_specs=[vmem] * 3,
            out_shape=[folded, weight, first],
            scratch_shapes=[
                pltpu.VMEM(var_query.shape, F32),
                pltpu.VMEM((width, width), BF16),
                pltpu.SemaphoreType.DMA((4,)),
            ],
            compiler_params=pltpu.CompilerParams(vmem_limit_bytes=PRE_VMEM),
            name="pre",
        )(var_tokens, agg_value, var_query, agg_key)
        shape = jax.ShapeDtypeStruct((lead_rows * tiles, half, packed), BF16)
        later = (local_vars, rows - lead_rows, total_columns, width)
        keep, send, rest = pl.pallas_call(
            functools.partial(lead_kernel, heads, head_dim, lead_rows, tiles, columns),
            in_specs=[smem, hbm, vmem, vmem, vmem],
            out_specs=[vmem] * 3,
            out_shape=[shape, shape, jax.ShapeDtypeStruct(later, BF16)],
            scratch_shapes=[
                pltpu.VMEM((2, local_vars, tile, width), BF16),
                pltpu.SemaphoreType.DMA((3,)),
            ],
            compiler_params=pltpu.CompilerParams(vmem_limit_bytes=LEAD_VMEM),
            cost_estimate=pool_cost(lead_rows),
            name="lead",
        )(block, var_tokens, first, held, folded)
        return keep, send, folded, held, rest

    def pool(row, rest, held, folded):
        shape = jax.ShapeDtypeStruct((tiles, half, packed), BF16)
        return pl.pallas_call(
            functools.partial(pool_kernel, heads, head_dim, row, tiles, columns),
            in_specs=[smem] + [vmem] * 3,
            out_specs=[vmem] * 2,
            out_shape=[shape] * 2,
            compiler_params=pltpu.CompilerParams(vmem_limit_bytes=POOL_VMEM),
            cost_estimate=pool_cost(1),
            name="pool",
        )(block, rest, held, folded)

    def exchange(array, shift, stride, radix):
        def moved(i):
            digit = (i // stride) % radix
            return i + ((digit + shift) % radix - digit) * stride

        return lax.ppermute(array, ("var", "lon"), [(i, moved(i)) for i in range(devices)])

    stages, stride = [], 1
    for radix in RADICES:
        stages.append((stride, radix))
        stride *= radix
    if tiles > 1:
        stages.append((TILE_BLOCKS, tiles))

    def swap(sends, number):
        stride, radix = stages[number]
        return [exchange(send, k + 1, stride, radix) for k, send in enumerate(sends)]

    def next_split(groups, number, places, size):
        if number + 1 == len(stages):
            rows_left = sum(math.prod(group[0].shape[:-1]) for group in groups)
            return merge(groups, [(rows_left, width)], heads, width, True)
        radix = stages[number + 1][1]
        if number + 1 < len(RADICES):
            size //= radix
            shape = (places, size, packed) if size % 8 == 0 else (places * size, packed)
            return merge(groups, [shape] * radix, heads, width, False)
        (full,) = merge(groups, [(places * size, packed)], heads, width, False)
        full = full.reshape(places // tiles, tiles, size, packed)
        return [full[:, k].reshape(places // tiles * size, packed) for k in range(tiles)]

    barrier = lax.optimization_barrier
    keep_a, send_a, folded, held, rest = lead_pool()
    got_a = swap([send_a], 0)
    keep_b, send_b = pool(0, rest, held, folded)
    parts_a = next_split([[keep_a] + got_a], 0, lead_rows * tiles, half)
    got_b = swap([send_b], 0)
    parts_a, folded = barrier((parts_a, folded))
    got_a = swap(parts_a[1:], 1)
    keep_c, send_c = pool(1, rest, held, folded)
    got_c = swap([send_c], 0)
    keep_a = parts_a[0]
    keep_b = [[keep_b] + got_b, [keep_c] + got_c]

    places = [(0, 0), (1, 0), (0, 1), (1, 1), (0, -1), (1, -1)]
    patch = rows * columns
    dl = np.repeat([p[0] for p in places], patch)
    dx = np.repeat([p[1] for p in places], patch)
    row = np.tile(np.repeat(np.arange(rows), columns), len(places))
    column = np.tile(np.arange(columns), len(places) * rows)
    meta = jnp.asarray(np.stack([row, dl, column, dx * columns]), jnp.int32)
    keys = len(places) * patch
    for number in range(1, len(stages)):
        split_b, split_a = split_before(stages, number - 1), split_before(stages, number)
        parts_b = next_split(keep_b, number - 1, 2 * tiles, half // split_b)
        if number > 1:
            got_a, _ = barrier((got_a, parts_b))
        group_a = [keep_a] + got_a
        if number + 1 < len(stages):
            parts_a = next_split([group_a], number, lead_rows * tiles, half // split_a)
            if number == 1:
                parts_a, parts_b = barrier((parts_a, parts_b))
            keep_a, got_a = parts_a[0], swap(parts_a[1:], number + 1)
        keep_b = [[parts_b[0]] + swap(parts_b[1:], number)]
    (pooled,) = next_split([group_a] + keep_b, len(stages) - 1, 0, columns)

    staged = (agg_out, nb_query, nb_key)
    pooled, where = barrier((pooled, where))
    bias, *staged = pl.pallas_call(
        functools.partial(stage_kernel, rows, columns, len(staged)),
        in_specs=[smem, vmem, vmem, vmem] + [hbm] * len(staged),
        out_specs=[vmem] * (1 + len(staged)),
        out_shape=[jax.ShapeDtypeStruct((heads, QROWS, keys), F32)] + [weight] * len(staged),
        scratch_shapes=[pltpu.SemaphoreType.DMA((len(staged),))],
        compiler_params=pltpu.CompilerParams(vmem_limit_bytes=STAGE_VMEM),
        cost_estimate=pl.CostEstimate(
            flops=1000, bytes_accessed=10 * width * width, transcendentals=0
        ),
        name="stage",
    )(where, meta, valid, jnp.transpose(pos_bias, (1, 0, 2)), *staged)

    def partner(array, kind):
        pairs = []
        for i in range(n_var * n_lat * n_lon):
            v, l, o = i // (n_lat * n_lon), (i // n_lon) % n_lat, i % n_lon
            b = v * n_lon + o
            if kind == "lat":
                l = n_lat - 1 - l
            elif kind == "core":
                b ^= 1
            else:
                b = (b + 1 if b % 2 else b - 1) % devices
            pairs.append((((b // n_lon) * n_lat + l) * n_lon + b % n_lon, i))
        return lax.ppermute(array, ("var", "lat", "lon"), pairs)

    across = partner(pooled, "lat")
    near = partner(pooled, "core")
    far = partner(pooled, "odd")
    across, far, bias = barrier((across, far, bias))
    window = [pooled, across, near, partner(across, "core"), far, partner(far, "lat")]
    last = (nb_value, nb_out)
    last, _ = barrier((last, across))
    last = pl.pallas_call(
        functools.partial(load_kernel, len(last)),
        in_specs=[hbm] * len(last),
        out_specs=[vmem] * len(last),
        out_shape=[weight] * len(last),
        scratch_shapes=[pltpu.SemaphoreType.DMA((len(last),))],
        compiler_params=pltpu.CompilerParams(vmem_limit_bytes=LOAD_VMEM),
        cost_estimate=pl.CostEstimate(
            flops=1000, bytes_accessed=8 * width * width, transcendentals=0
        ),
        name="load",
    )(*last)

    return pl.pallas_call(
        functools.partial(attend_kernel, heads, len(window)),
        in_specs=[vmem] * (len(window) + 7),
        out_specs=vmem,
        out_shape=jax.ShapeDtypeStruct((rows, columns, width), BF16),
        scratch_shapes=[
            pltpu.VMEM((keys, width), BF16),
            pltpu.VMEM((QROWS, width), BF16),
        ],
        compiler_params=pltpu.CompilerParams(vmem_limit_bytes=MERGE_VMEM),
        name="attend",
    )(*window, norm_gain.reshape(1, width), bias, *staged, *last)


def solution(mesh):
    sizes = (mesh.shape["var"], mesh.shape["lat"], mesh.shape["lon"])
    return jax.shard_map(
        functools.partial(on_device, sizes),
        mesh=mesh,
        in_specs=(P(("var", "lon"), "lat", None, None),) + (P(),) * 11,
        out_specs=P("lat", ("var", "lon"), None),
        check_vma=False,
    )
```

```python
import functools
import math

import jax
import jax.numpy as jnp
import numpy as np
from jax import lax
from jax.experimental import pallas as pl
from jax.experimental.pallas import tpu as pltpu
from jax.sharding import PartitionSpec as P

HALF = 6
EPS = 1e-05
LANES = 128
TILE_BLOCKS = 16
RADICES = (2, 2, 4)
QROWS = 48
MIB = 1 << 20
PRE_VMEM = 50 * MIB
LEAD_VMEM = 40 * MIB
POOL_VMEM = 30 * MIB
MERGE_VMEM = 12 * MIB
STAGE_VMEM = 47 * MIB
LOAD_VMEM = 42 * MIB
F32 = jnp.float32
BF16 = jnp.bfloat16


def dot(a, b):
    return jnp.dot(a, b, preferred_element_type=F32)


def dot_nt(a, b):
    return lax.dot_general(a, b, (((1,), (1,)), ((), ())), preferred_element_type=F32)


def split3(x):
    hi = x.astype(BF16)
    rest = x - hi.astype(F32)
    mid = rest.astype(BF16)
    low = (rest - mid.astype(F32)).astype(BF16)
    return hi.astype(F32), mid.astype(F32), low.astype(F32)


def lane_iota(shape):
    return lax.broadcasted_iota(jnp.int32, shape, len(shape) - 1)


def pack3(x, heads):
    hi, mid, low = split3(x)
    lane = lane_iota(x.shape)
    mid = pltpu.roll(mid, heads, 1)
    low = pltpu.roll(low, 2 * heads, 1)
    out = jnp.where(lane < heads, hi, jnp.where(lane < 2 * heads, mid, low))
    return jnp.where(lane < 3 * heads, out, 0.0)


def unpack3(x, heads):
    return x + pltpu.roll(x, LANES - heads, 1) + pltpu.roll(x, LANES - 2 * heads, 1)


def expander(heads, width):
    head_dim = width // heads
    row = lax.broadcasted_iota(jnp.int32, (LANES, width), 0)
    lane = lax.broadcasted_iota(jnp.int32, (LANES, width), 1)
    hit = jnp.zeros((LANES, width), F32)
    for piece in range(3):
        low = (row - piece * heads) * head_dim
        inside = (row >= piece * heads) & (row < (piece + 1) * heads)
        hit = jnp.where(inside & (lane >= low) & (lane < low + head_dim), 1.0, hit)
    return hit.astype(BF16)


def encode_stats(top, total, heads):
    return pack3(top, heads) + pltpu.roll(pack3(total, heads), 3 * heads, 1)


def fold(query, key, heads, head_dim):
    width = key.shape[0]
    wide = jnp.concatenate([query] * (width // head_dim), axis=1)
    row = lax.broadcasted_iota(jnp.int32, wide.shape, 0)
    lane = lax.broadcasted_iota(jnp.int32, wide.shape, 1)
    own = (lane >= row * head_dim) & (lane < (row + 1) * head_dim)
    pieces = jnp.concatenate(split3(jnp.where(own, wide, 0.0)), axis=0).astype(BF16)
    folded = dot_nt(pieces, key)
    folded = folded[:heads] + folded[heads : 2 * heads] + folded[2 * heads :]
    parts = jnp.concatenate(
        list(split3(folded)) + [jnp.zeros((LANES - 3 * heads, width), F32)], axis=0
    )
    return parts.T.astype(BF16)


def column_order(block, tile, columns, turned=False):
    shape = (tile, tile)
    target = lax.broadcasted_iota(jnp.int32, shape, 0)
    source = lax.broadcasted_iota(jnp.int32, shape, 1)
    group = jnp.zeros(shape, jnp.int32)
    for at in range(1, TILE_BLOCKS):
        group = group + jnp.where(target >= at * columns, 1, 0)
    wanted = jnp.zeros(shape, jnp.int32)
    weight, stride = TILE_BLOCKS, 1
    for radix in RADICES:
        weight //= radix
        bits, low = weight.bit_length() - 1, stride.bit_length() - 1
        place = (group >> bits) & (radix - 1)
        if turned and radix == 4:
            place = jnp.where(place == 0, 0, jnp.where(place == 3, 1, place + 1))
        digit = (place + (block >> low)) & (radix - 1)
        wanted = wanted + digit * stride
        stride *= radix
    wanted = wanted * columns + target - group * columns
    return jnp.where(source == wanted, 1.0, 0.0).astype(BF16)


def pool_rows(heads, head_dim, block, order, tokens, fold_ref, values, keep_ref, send_ref, place):
    variables, tile, width = tokens.shape
    half = tile // RADICES[0]
    lane = lane_iota((variables * tile, LANES))
    flat = tokens.reshape(variables * tile, width)
    score = unpack3(dot(flat, fold_ref[...]), heads)
    score = score.reshape(variables, tile, LANES)
    top = jnp.max(score, axis=0)
    raised = jnp.exp(score - top[None])
    total = jnp.sum(raised, axis=0)
    share = raised.reshape(variables * tile, LANES)
    pooled = []
    wide = 256
    for start in range(0, width, wide):
        rows = dot(flat, values(start, wide))
        for low in range(0, wide, LANES):
            index = (start + low) // head_dim + jnp.where(lane >= head_dim, 1, 0)
            spread = jnp.take_along_axis(share, index, axis=1)
            part = rows[:, low : low + LANES] * spread
            pooled.append(jnp.sum(part.reshape(variables, tile, LANES), axis=0).astype(BF16))
    pooled.append(encode_stats(top, total, heads).astype(BF16))
    ordered = dot(order, jnp.concatenate(pooled, axis=1)).astype(BF16)
    keep_ref[place] = ordered[:half]
    send_ref[place] = ordered[half:]


def pre_kernel(heads, head_dim, token_ref, value_ref, query_ref, key_ref, *refs):
    fold_ref, held, first_ref, query, held_key, sems = refs
    tile = first_ref.shape[1]
    copies = [
        pltpu.make_async_copy(query_ref, query, sems.at[0]),
        pltpu.make_async_copy(key_ref, held_key, sems.at[1]),
        pltpu.make_async_copy(token_ref.at[:, 0, pl.ds(0, tile), :], first_ref, sems.at[2]),
        pltpu.make_async_copy(value_ref, held, sems.at[3]),
    ]
    for copy in copies:
        copy.start()
    for copy in copies[:2]:
        copy.wait()
    scaled = query[...] * (1.0 / math.sqrt(head_dim))
    fold_ref[...] = fold(scaled, held_key[...], heads, head_dim)
    for copy in copies[2:]:
        copy.wait()


def lead_kernel(heads, head_dim, count, tiles, columns, *refs):
    block_ref, token_ref, first_ref, held, fold_ref = refs[:5]
    keep_ref, send_ref, rest_ref, slots, sems = refs[5:]
    tile = slots.shape[2]
    steps = count * tiles
    block = block_ref[0]
    high = block // TILE_BLOCKS

    def fetch(step):
        start = pl.multiple_of((step % tiles) * tile, tile)
        return pltpu.make_async_copy(
            token_ref.at[:, step // tiles, pl.ds(start, tile), :],
            slots.at[step % 2],
            sems.at[step % 2],
        )

    later = rest_ref.shape[1]
    rest = pltpu.make_async_copy(token_ref.at[:, pl.ds(count, later)], rest_ref, sems.at[2])
    pltpu.make_async_copy(first_ref, slots.at[0], sems.at[0]).start()
    fetch(1).start()
    order = column_order(block, tile, columns)

    def work(step, tokens):
        pool_rows(
            heads,
            head_dim,
            block,
            order,
            tokens,
            fold_ref,
            lambda start, wide: held[:, start : start + wide],
            keep_ref,
            send_ref,
            (step // tiles) * tiles + (step % tiles + tiles - high) % tiles,
        )


    def body(step, _):
        fetch(step).wait()
        work(step, slots[step % 2])

        @pl.when(step + 2 < steps)
        def _():
            fetch(step + 2).start()

        @pl.when(step == 1)
        def _():
            rest.start()

        return 0

    lax.fori_loop(0, steps, body, 0)
    rest.wait()


def pool_kernel(heads, head_dim, row, tiles, columns, *refs):
    block_ref, rest_ref, held, fold_ref, keep_ref, send_ref = refs
    block = block_ref[0]
    high = block // TILE_BLOCKS
    tile = rest_ref.shape[2] // tiles
    order = column_order(block, tile, columns, turned=True)
    for step in range(tiles):
        pool_rows(
            heads,
            head_dim,
            block,
            order,
            rest_ref[:, row, step * tile : (step + 1) * tile],
            fold_ref,
            lambda start, wide: held[:, start : start + wide],
            keep_ref,
            send_ref,
            (step + tiles - high) % tiles,
        )


def merge_body(parts, heads, width, last):
    stats = [unpack3(part[:, width:].astype(F32), heads) for part in parts]
    top = functools.reduce(jnp.maximum, stats)
    scales = [jnp.exp(stat - top) for stat in stats]
    totals = [pltpu.roll(stat, LANES - 3 * heads, 1) for stat in stats]
    total = sum(scale * amount for scale, amount in zip(scales, totals))
    lane = lane_iota(total.shape)
    total = jnp.where(lane < heads, total, 1.0)
    if last:
        scales = [scale / total for scale in scales]
    spread = expander(heads, width)
    merged = sum(
        dot(pack3(scale, heads).astype(BF16), spread) * part[:, :width].astype(F32)
        for scale, part in zip(scales, parts)
    ).astype(BF16)
    if last:
        return merged
    stat = encode_stats(top, total, heads).astype(BF16)
    return jnp.concatenate([merged, stat], axis=1)


def merge_kernel(heads, width, counts, last, *refs):
    outs = refs[sum(counts) :]
    at = 0
    merged, groups = [], 0
    for count in counts:
        parts = [ref[...] for ref in refs[at : at + count]]
        at += count
        groups += parts[0].shape[0]
        flat = [part.reshape(-1, part.shape[-1]) for part in parts]
        merged.append(merge_body(flat, heads, width, last))
    if last:
        at = 0
        for rows in merged:
            outs[0][at : at + rows.shape[0]] = rows
            at += rows.shape[0]
        return
    size = math.prod(outs[0].shape[:-1]) // groups
    place = 0
    for rows in merged:
        rows = rows.astype(F32)
        for low in range(0, rows.shape[0], size * len(outs)):
            for k, out in enumerate(outs):
                piece = rows[low + k * size : low + (k + 1) * size].astype(BF16)
                if len(out.shape) == 3:
                    out[place] = piece
                else:
                    out[place * size : (place + 1) * size] = piece
            place += 1


def merge(groups, shapes, heads, width, last):
    parts = [part for group in groups for part in group]
    rows = sum(math.prod(part.shape[:-1]) for part in parts)
    return pl.pallas_call(
        functools.partial(merge_kernel, heads, width, [len(group) for group in groups], last),
        out_shape=[jax.ShapeDtypeStruct(shape, BF16) for shape in shapes],
        compiler_params=pltpu.CompilerParams(vmem_limit_bytes=MERGE_VMEM),
        cost_estimate=pl.CostEstimate(
            flops=rows * LANES * width * 2,
            bytes_accessed=rows * width * 4,
            transcendentals=rows * LANES,
        ),
        name="merge",
    )(*parts)


def stage_kernel(rows, columns, count, *refs):
    where_ref, meta_ref, valid_ref, table_ref = refs[:4]
    sources, out_ref = refs[4 : 4 + count], refs[4 + count]
    targets, sems = refs[5 + count : 5 + 2 * count], refs[5 + 2 * count]
    copies = [
        pltpu.make_async_copy(source, target, sems.at[at])
        for at, (source, target) in enumerate(zip(sources, targets))
    ]
    for copy in copies:
        copy.start()
    span, heads, _ = table_ref.shape
    pitch = 16
    n_rows, n_columns = valid_ref.shape
    keys = meta_ref.shape[1]
    lat, block = where_ref[0], where_ref[1]
    side = rows - 2 * rows * lat
    row_at = meta_ref[0:1] + meta_ref[1:2] * side
    column_at = meta_ref[2:3] + meta_ref[3:4] * (1 - 2 * (block & 1))

    far = column_at + block * columns
    far = jnp.where(far < 0, far + n_columns, far)
    far = jnp.where(far >= n_columns, far - n_columns, far)
    hot = lax.broadcasted_iota(jnp.int32, (n_columns, keys), 0) == far
    seen = dot(valid_ref[...].astype(F32).astype(BF16), jnp.where(hot, 1.0, 0.0).astype(BF16))
    mine = lax.broadcasted_iota(jnp.int32, (n_rows, keys), 0) == row_at + lat * rows
    allowed = jnp.sum(jnp.where(mine, seen, 0.0), axis=0, keepdims=True) > 0.5

    flat = [table_ref[up] for up in range(span)]
    gap = jnp.zeros((heads, pitch - span), F32)
    flat = jnp.concatenate([piece for up in flat for piece in (up, gap)], axis=1)
    pieces = jnp.concatenate(split3(flat), axis=0).astype(BF16)
    out_ref[...] = jnp.zeros(out_ref.shape, F32)
    place = lax.broadcasted_iota(jnp.int32, (span * pitch, keys), 0)
    for row in range(rows):
        for column in range(columns):
            up = row_at - row + HALF
            across = column_at - column + HALF
            inside = (up >= 0) & (up < span) & (across >= 0) & (across < span)
            index = jnp.where(inside, up * pitch + across, -1)
            found = dot(pieces, jnp.where(place == index, 1.0, 0.0).astype(BF16))
            found = found[:heads] + found[heads : 2 * heads] + found[2 * heads :]
            kept = (inside & allowed) | (index == HALF * pitch + HALF)
            out_ref[:, row * columns + column, :] = jnp.where(kept, found, -jnp.inf)
    for copy in copies:
        copy.wait()


def load_kernel(count, *refs):
    sems = refs[2 * count]
    copies = [
        pltpu.make_async_copy(refs[at], refs[count + at], sems.at[at]) for at in range(count)
    ]
    for copy in copies:
        copy.start()
    for copy in copies:
        copy.wait()


def project(window, gain_ref, w_agg, w_key, w_value):
    tokens = dot(window, w_agg[...]).astype(BF16)
    values = tokens.astype(F32)
    center = values - jnp.mean(values, axis=-1, keepdims=True)
    variance = jnp.mean(center * center, axis=-1, keepdims=True)
    normed = (center * lax.rsqrt(variance + EPS) * gain_ref[...]).astype(BF16)
    keys = dot(normed, w_key[...]).astype(BF16)
    values = dot(normed, w_value[...]).astype(BF16)
    return tokens, normed, keys, values


def gather_blocks(blocks, window):
    at = 0
    for block in blocks:
        size = block.shape[0]
        window[at : at + size] = block[...]
        at += size


def project_kernel(count, *refs):
    gain_ref, w_agg, w_query, w_key, w_value = refs[count : count + 5]
    token_ref, query_ref, near_key, near_value, window = refs[count + 5 :]
    gather_blocks(refs[:count], window)
    tokens, normed, keys, values = project(window[...], gain_ref, w_agg, w_key, w_value)
    token_ref[...] = tokens[:QROWS]
    query_ref[...] = dot(normed[:QROWS], w_query[...]).astype(BF16)
    near_key[...] = keys
    near_value[...] = values


def attend_kernel(heads, count, *refs):
    gain_ref, w_agg, w_key, w_value, w_out, bias_ref = refs[count : count + 6]
    token_ref, query_ref, near_key, near_value, out_ref = refs[count + 6 : count + 11]
    window, key_ref, value_ref, mix = refs[count + 11 :]
    width = window.shape[1]
    scale = 1.0 / math.sqrt(width // heads)
    near = near_key.shape[0]
    gather_blocks(refs[:count], window)
    _, _, keys, values = project(window[...], gain_ref, w_agg, w_key, w_value)
    key_ref[:near] = near_key[...]
    key_ref[near:] = keys
    value_ref[:near] = near_value[...]
    value_ref[near:] = values
    left = lane_iota((QROWS, LANES)) < LANES // 2
    pairs = [slice(at, at + LANES) for at in range(0, width, LANES)]
    logits = []
    for at in pairs:
        query = query_ref[:, at]
        zero = jnp.zeros_like(query)
        both = jnp.concatenate([jnp.where(left, query, zero), jnp.where(left, zero, query)], axis=0)
        logits.append(dot_nt(both, key_ref[:, at]))
    shares = []
    for pair, logit in enumerate(logits):
        bias = bias_ref[2 * pair : 2 * pair + 2]
        logit = logit * scale + bias.reshape(2 * QROWS, bias.shape[-1])
        raised = jnp.exp(logit - jnp.max(logit, axis=-1, keepdims=True))
        shares.append((raised / jnp.sum(raised, axis=-1, keepdims=True)).astype(BF16))
    mixed = [dot(share, value_ref[:, at]) for share, at in zip(shares, pairs)]
    for at, rows in zip(pairs, mixed):
        mix[:, at] = jnp.where(left, rows[:QROWS], rows[QROWS:]).astype(BF16)
    result = token_ref[...].astype(F32) + dot(mix[...], w_out[...])
    rows, columns, _ = out_ref.shape
    for row in range(rows):
        out_ref[row] = result[row * columns : (row + 1) * columns].astype(BF16)


def split_before(stages, number):
    return math.prod(radix for _, radix in stages[1 : min(number + 1, len(RADICES))])


def on_device(
    sizes,
    var_tokens,
    var_query,
    agg_key,
    agg_value,
    agg_out,
    norm_gain,
    nb_query,
    nb_key,
    nb_value,
    nb_out,
    pos_bias,
    valid,
):
    heads, head_dim = var_query.shape
    width = agg_key.shape[0]
    local_vars, rows, total_columns, _ = var_tokens.shape
    n_var, n_lat, n_lon = sizes
    devices = n_var * n_lon
    columns = total_columns // devices
    tile = TILE_BLOCKS * columns
    tiles = devices // TILE_BLOCKS
    packed = width + LANES
    half = tile // RADICES[0]
    lat = lax.axis_index("lat")
    block = lax.axis_index("var") * n_lon + lax.axis_index("lon")
    where = jnp.stack([lat, block]).astype(jnp.int32)
    block = where[1:]
    smem = pl.BlockSpec(memory_space=pltpu.SMEM)
    vmem = pl.BlockSpec(memory_space=pltpu.VMEM)
    hbm = pl.BlockSpec(memory_space=pltpu.HBM)

    weight = jax.ShapeDtypeStruct((width, width), BF16)
    lead_rows = rows - 2

    def pool_cost(count):
        work = count * total_columns * local_vars * width
        return pl.CostEstimate(flops=3 * work * width, bytes_accessed=2 * work, transcendentals=0)

    def lead_pool():
        folded = jax.ShapeDtypeStruct((width, LANES), BF16)
        first = jax.ShapeDtypeStruct((local_vars, tile, width), BF16)
        folded, held, first = pl.pallas_call(
            functools.partial(pre_kernel, heads, head_dim),
            in_specs=[hbm] * 4,
            out_specs=[vmem] * 3,
            out_shape=[folded, weight, first],
            scratch_shapes=[
                pltpu.VMEM(var_query.shape, F32),
                pltpu.VMEM((width, width), BF16),
                pltpu.SemaphoreType.DMA((4,)),
            ],
            compiler_params=pltpu.CompilerParams(vmem_limit_bytes=PRE_VMEM),
            name="pre",
        )(var_tokens, agg_value, var_query, agg_key)
        shape = jax.ShapeDtypeStruct((lead_rows * tiles, half, packed), BF16)
        later = (local_vars, rows - lead_rows, total_columns, width)
        keep, send, rest = pl.pallas_call(
            functools.partial(lead_kernel, heads, head_dim, lead_rows, tiles, columns),
            in_specs=[smem, hbm, vmem, vmem, vmem],
            out_specs=[vmem] * 3,
            out_shape=[shape, shape, jax.ShapeDtypeStruct(later, BF16)],
            scratch_shapes=[
                pltpu.VMEM((2, local_vars, tile, width), BF16),
                pltpu.SemaphoreType.DMA((3,)),
            ],
            compiler_params=pltpu.CompilerParams(vmem_limit_bytes=LEAD_VMEM),
            cost_estimate=pool_cost(lead_rows),
            name="lead",
        )(block, var_tokens, first, held, folded)
        return keep, send, folded, held, rest

    def pool(row, rest, held, folded):
        shape = jax.ShapeDtypeStruct((tiles, half, packed), BF16)
        return pl.pallas_call(
            functools.partial(pool_kernel, heads, head_dim, row, tiles, columns),
            in_specs=[smem] + [vmem] * 3,
            out_specs=[vmem] * 2,
            out_shape=[shape] * 2,
            compiler_params=pltpu.CompilerParams(vmem_limit_bytes=POOL_VMEM),
            cost_estimate=pool_cost(1),
            name="pool",
        )(block, rest, held, folded)

    def exchange(array, shift, stride, radix):
        def moved(i):
            digit = (i // stride) % radix
            return i + ((digit + shift) % radix - digit) * stride

        return lax.ppermute(array, ("var", "lon"), [(i, moved(i)) for i in range(devices)])

    stages, stride = [], 1
    for radix in RADICES:
        stages.append((stride, radix))
        stride *= radix
    if tiles > 1:
        stages.append((TILE_BLOCKS, tiles))

    def swap(sends, number, turned=False):
        stride, radix = stages[number]
        shifts = range(1, radix)
        if turned and number < len(RADICES) and radix == 4:
            shifts = (2, 3, 1)
        return [exchange(send, shift, stride, radix) for send, shift in zip(sends, shifts)]

    def next_split(groups, number, places, size):
        if number + 1 == len(stages):
            rows_left = sum(math.prod(group[0].shape[:-1]) for group in groups)
            return merge(groups, [(rows_left, width)], heads, width, True)
        radix = stages[number + 1][1]
        if number + 1 < len(RADICES):
            size //= radix
            shape = (places, size, packed) if size % 8 == 0 else (places * size, packed)
            return merge(groups, [shape] * radix, heads, width, False)
        (full,) = merge(groups, [(places * size, packed)], heads, width, False)
        full = full.reshape(places // tiles, tiles, size, packed)
        return [full[:, k].reshape(places // tiles * size, packed) for k in range(tiles)]

    barrier = lax.optimization_barrier
    keep_a, send_a, folded, held, rest = lead_pool()
    got_a = swap([send_a], 0)
    keep_b, send_b = pool(0, rest, held, folded)
    parts_a = next_split([[keep_a] + got_a], 0, lead_rows * tiles, half)
    got_b = swap([send_b], 0)
    parts_a, folded = barrier((parts_a, folded))
    got_a = swap(parts_a[1:], 1)
    keep_c, send_c = pool(1, rest, held, folded)
    got_c = swap([send_c], 0)
    keep_a = parts_a[0]
    keep_b = [[keep_b] + got_b, [keep_c] + got_c]

    places = [(0, 0), (0, -1), (0, 1), (1, 0), (1, -1), (1, 1)]
    patch = rows * columns
    dl = np.repeat([p[0] for p in places], patch)
    dx = np.repeat([p[1] for p in places], patch)
    row = np.tile(np.repeat(np.arange(rows), columns), len(places))
    column = np.tile(np.arange(columns), len(places) * rows)
    meta = jnp.asarray(np.stack([row, dl, column, dx * columns]), jnp.int32)
    keys = len(places) * patch
    for number in range(1, len(stages)):
        split_b, split_a = split_before(stages, number - 1), split_before(stages, number)
        parts_b = next_split(keep_b, number - 1, 2 * tiles, half // split_b)
        if number > 1:
            got_a, _ = barrier((got_a, parts_b))
        group_a = [keep_a] + got_a
        if number + 1 < len(stages):
            parts_a = next_split([group_a], number, lead_rows * tiles, half // split_a)
            if number == 1:
                parts_a, parts_b = barrier((parts_a, parts_b))
            keep_a, got_a = parts_a[0], swap(parts_a[1:], number + 1)
        keep_b = [[parts_b[0]] + swap(parts_b[1:], number, True)]
    (pooled,) = next_split([group_a] + keep_b, len(stages) - 1, 0, columns)

    staged = (agg_out, nb_query, nb_key)
    pooled, where = barrier((pooled, where))
    bias, *staged = pl.pallas_call(
        functools.partial(stage_kernel, rows, columns, len(staged)),
        in_specs=[smem, vmem, vmem, vmem] + [hbm] * len(staged),
        out_specs=[vmem] * (1 + len(staged)),
        out_shape=[jax.ShapeDtypeStruct((heads, QROWS, keys), F32)] + [weight] * len(staged),
        scratch_shapes=[pltpu.SemaphoreType.DMA((len(staged),))],
        compiler_params=pltpu.CompilerParams(vmem_limit_bytes=STAGE_VMEM),
        cost_estimate=pl.CostEstimate(
            flops=1000, bytes_accessed=10 * width * width, transcendentals=0
        ),
        name="stage",
    )(where, meta, valid, jnp.transpose(pos_bias, (1, 0, 2)), *staged)

    def partner(array, kind):
        pairs = []
        for i in range(n_var * n_lat * n_lon):
            v, l, o = i // (n_lat * n_lon), (i // n_lon) % n_lat, i % n_lon
            b = v * n_lon + o
            if kind == "lat":
                l = n_lat - 1 - l
            elif kind == "core":
                b ^= 1
            else:
                b = (b + 1 if b % 2 else b - 1) % devices
            pairs.append((((b // n_lon) * n_lat + l) * n_lon + b % n_lon, i))
        return lax.ppermute(array, ("var", "lat", "lon"), pairs)

    far = partner(pooled, "odd")
    across = partner(pooled, "lat")
    near = partner(pooled, "core")
    far, across, bias = barrier((far, across, bias))
    window = [pooled, far, near, across]
    far_late = partner(far, "lat")
    last = (nb_value, nb_out)
    last, _ = barrier((last, far))
    last = pl.pallas_call(
        functools.partial(load_kernel, len(last)),
        in_specs=[hbm] * len(last),
        out_specs=[vmem] * len(last),
        out_shape=[weight] * len(last),
        scratch_shapes=[pltpu.SemaphoreType.DMA((len(last),))],
        compiler_params=pltpu.CompilerParams(vmem_limit_bytes=LOAD_VMEM),
        cost_estimate=pl.CostEstimate(
            flops=1000, bytes_accessed=8 * width * width, transcendentals=0
        ),
        name="load",
    )(*last)

    gain = norm_gain.reshape(1, width)
    w_agg, w_query, w_key = staged
    across, last = barrier((across, last))
    w_value, w_out = last
    late = [far_late, partner(across, "core")]
    early = len(window) * patch
    tall = jax.ShapeDtypeStruct((QROWS, width), BF16)
    side = jax.ShapeDtypeStruct((early, width), BF16)
    projected = pl.pallas_call(
        functools.partial(project_kernel, len(window)),
        in_specs=[vmem] * (len(window) + 5),
        out_specs=[vmem] * 4,
        out_shape=[tall, tall, side, side],
        scratch_shapes=[pltpu.VMEM((early, width), BF16)],
        compiler_params=pltpu.CompilerParams(vmem_limit_bytes=MERGE_VMEM),
        cost_estimate=pl.CostEstimate(
            flops=6 * early * width * width, bytes_accessed=8 * width * width, transcendentals=0
        ),
        name="project",
    )(*window, gain, w_agg, w_query, w_key, w_value)
    return pl.pallas_call(
        functools.partial(attend_kernel, heads, len(late)),
        in_specs=[vmem] * (len(late) + 10),
        out_specs=vmem,
        out_shape=jax.ShapeDtypeStruct((rows, columns, width), BF16),
        scratch_shapes=[
            pltpu.VMEM((keys - early, width), BF16),
            pltpu.VMEM((keys, width), BF16),
            pltpu.VMEM((keys, width), BF16),
            pltpu.VMEM((QROWS, width), BF16),
        ],
        compiler_params=pltpu.CompilerParams(vmem_limit_bytes=MERGE_VMEM),
        name="attend",
    )(*late, gain, w_agg, w_key, w_value, w_out, bias, *projected)


def solution(mesh):
    sizes = (mesh.shape["var"], mesh.shape["lat"], mesh.shape["lon"])
    return jax.shard_map(
        functools.partial(on_device, sizes),
        mesh=mesh,
        in_specs=(P(("var", "lon"), "lat", None, None),) + (P(),) * 11,
        out_specs=P("lat", ("var", "lon"), None),
        check_vma=False,
    )
```

```python
import functools
import math

import jax
import jax.numpy as jnp
import numpy as np
from jax import lax
from jax.experimental import pallas as pl
from jax.experimental.pallas import tpu as pltpu
from jax.sharding import PartitionSpec as P

HALF = 6
EPS = 1e-05
LANES = 128
TILE_BLOCKS = 16
RADICES = (2, 2, 4)
QROWS = 48
MIB = 1 << 20
PRE_VMEM = 50 * MIB
LEAD_VMEM = 40 * MIB
POOL_VMEM = 30 * MIB
MERGE_VMEM = 12 * MIB
STAGE_VMEM = 49 * MIB
LOAD_VMEM = 36 * MIB
F32 = jnp.float32
BF16 = jnp.bfloat16


def dot(a, b):
    return jnp.dot(a, b, preferred_element_type=F32)


def dot_nt(a, b):
    return lax.dot_general(a, b, (((1,), (1,)), ((), ())), preferred_element_type=F32)


def split3(x):
    hi = x.astype(BF16)
    rest = x - hi.astype(F32)
    mid = rest.astype(BF16)
    low = (rest - mid.astype(F32)).astype(BF16)
    return hi.astype(F32), mid.astype(F32), low.astype(F32)


def lane_iota(shape):
    return lax.broadcasted_iota(jnp.int32, shape, len(shape) - 1)


def pack3(x, heads):
    hi, mid, low = split3(x)
    lane = lane_iota(x.shape)
    mid = pltpu.roll(mid, heads, 1)
    low = pltpu.roll(low, 2 * heads, 1)
    out = jnp.where(lane < heads, hi, jnp.where(lane < 2 * heads, mid, low))
    return jnp.where(lane < 3 * heads, out, 0.0)


def unpack3(x, heads):
    return x + pltpu.roll(x, LANES - heads, 1) + pltpu.roll(x, LANES - 2 * heads, 1)


def expander(heads, width):
    head_dim = width // heads
    row = lax.broadcasted_iota(jnp.int32, (LANES, width), 0)
    lane = lax.broadcasted_iota(jnp.int32, (LANES, width), 1)
    hit = jnp.zeros((LANES, width), F32)
    for piece in range(3):
        low = (row - piece * heads) * head_dim
        inside = (row >= piece * heads) & (row < (piece + 1) * heads)
        hit = jnp.where(inside & (lane >= low) & (lane < low + head_dim), 1.0, hit)
    return hit.astype(BF16)


def encode_stats(top, total, heads):
    return pack3(top, heads) + pltpu.roll(pack3(total, heads), 3 * heads, 1)


def fold(query, key, heads, head_dim):
    width = key.shape[0]
    wide = jnp.concatenate([query] * (width // head_dim), axis=1)
    row = lax.broadcasted_iota(jnp.int32, wide.shape, 0)
    lane = lax.broadcasted_iota(jnp.int32, wide.shape, 1)
    own = (lane >= row * head_dim) & (lane < (row + 1) * head_dim)
    pieces = jnp.concatenate(split3(jnp.where(own, wide, 0.0)), axis=0).astype(BF16)
    folded = dot_nt(pieces, key)
    folded = folded[:heads] + folded[heads : 2 * heads] + folded[2 * heads :]
    parts = jnp.concatenate(
        list(split3(folded)) + [jnp.zeros((LANES - 3 * heads, width), F32)], axis=0
    )
    return parts.T.astype(BF16)


def column_order(block, tile, columns, turned=False):
    shape = (tile, tile)
    target = lax.broadcasted_iota(jnp.int32, shape, 0)
    source = lax.broadcasted_iota(jnp.int32, shape, 1)
    group = jnp.zeros(shape, jnp.int32)
    for at in range(1, TILE_BLOCKS):
        group = group + jnp.where(target >= at * columns, 1, 0)
    wanted = jnp.zeros(shape, jnp.int32)
    weight, stride = TILE_BLOCKS, 1
    for radix in RADICES:
        weight //= radix
        bits, low = weight.bit_length() - 1, stride.bit_length() - 1
        place = (group >> bits) & (radix - 1)
        if turned and radix == 4:
            place = jnp.where(place == 0, 0, jnp.where(place == 3, 1, place + 1))
        digit = (place + (block >> low)) & (radix - 1)
        wanted = wanted + digit * stride
        stride *= radix
    wanted = wanted * columns + target - group * columns
    return jnp.where(source == wanted, 1.0, 0.0).astype(BF16)


def pool_rows(heads, head_dim, block, order, tokens, fold_ref, values, keep_ref, send_ref, place):
    variables, tile, width = tokens.shape
    half = tile // RADICES[0]
    lane = lane_iota((variables * tile, LANES))
    flat = tokens.reshape(variables * tile, width)
    score = unpack3(dot(flat, fold_ref[...]), heads)
    score = score.reshape(variables, tile, LANES)
    top = jnp.max(score, axis=0)
    raised = jnp.exp(score - top[None])
    total = jnp.sum(raised, axis=0)
    share = raised.reshape(variables * tile, LANES)
    pooled = []
    wide = 256
    for start in range(0, width, wide):
        rows = dot(flat, values(start, wide))
        for low in range(0, wide, LANES):
            index = (start + low) // head_dim + jnp.where(lane >= head_dim, 1, 0)
            spread = jnp.take_along_axis(share, index, axis=1)
            part = rows[:, low : low + LANES] * spread
            pooled.append(jnp.sum(part.reshape(variables, tile, LANES), axis=0).astype(BF16))
    pooled.append(encode_stats(top, total, heads).astype(BF16))
    ordered = dot(order, jnp.concatenate(pooled, axis=1)).astype(BF16)
    keep_ref[place] = ordered[:half]
    send_ref[place] = ordered[half:]


def pre_kernel(heads, head_dim, token_ref, value_ref, query_ref, key_ref, *refs):
    fold_ref, held, first_ref, query, held_key, sems = refs
    tile = first_ref.shape[1]
    copies = [
        pltpu.make_async_copy(query_ref, query, sems.at[0]),
        pltpu.make_async_copy(key_ref, held_key, sems.at[1]),
        pltpu.make_async_copy(token_ref.at[:, 0, pl.ds(0, tile), :], first_ref, sems.at[2]),
        pltpu.make_async_copy(value_ref, held, sems.at[3]),
    ]
    for copy in copies:
        copy.start()
    for copy in copies[:2]:
        copy.wait()
    scaled = query[...] * (1.0 / math.sqrt(head_dim))
    fold_ref[...] = fold(scaled, held_key[...], heads, head_dim)
    for copy in copies[2:]:
        copy.wait()


def lead_kernel(heads, head_dim, count, tiles, columns, *refs):
    block_ref, token_ref, first_ref, held, fold_ref = refs[:5]
    keep_ref, send_ref, rest_ref, slots, sems = refs[5:]
    tile = slots.shape[2]
    steps = count * tiles
    block = block_ref[0]
    high = block // TILE_BLOCKS

    def fetch(step):
        start = pl.multiple_of((step % tiles) * tile, tile)
        return pltpu.make_async_copy(
            token_ref.at[:, step // tiles, pl.ds(start, tile), :],
            slots.at[step % 2],
            sems.at[step % 2],
        )

    later = rest_ref.shape[1]
    rest = pltpu.make_async_copy(token_ref.at[:, pl.ds(count, later)], rest_ref, sems.at[2])
    pltpu.make_async_copy(first_ref, slots.at[0], sems.at[0]).start()
    fetch(1).start()
    order = column_order(block, tile, columns)

    def work(step, tokens):
        pool_rows(
            heads,
            head_dim,
            block,
            order,
            tokens,
            fold_ref,
            lambda start, wide: held[:, start : start + wide],
            keep_ref,
            send_ref,
            (step // tiles) * tiles + (step % tiles + tiles - high) % tiles,
        )


    def body(step, _):
        fetch(step).wait()
        work(step, slots[step % 2])

        @pl.when(step + 2 < steps)
        def _():
            fetch(step + 2).start()

        @pl.when(step == 1)
        def _():
            rest.start()

        return 0

    lax.fori_loop(0, steps, body, 0)
    rest.wait()


def pool_kernel(heads, head_dim, row, tiles, columns, *refs):
    block_ref, rest_ref, held, fold_ref, keep_ref, send_ref = refs
    block = block_ref[0]
    high = block // TILE_BLOCKS
    tile = rest_ref.shape[2] // tiles
    order = column_order(block, tile, columns, turned=True)
    for step in range(tiles):
        pool_rows(
            heads,
            head_dim,
            block,
            order,
            rest_ref[:, row, step * tile : (step + 1) * tile],
            fold_ref,
            lambda start, wide: held[:, start : start + wide],
            keep_ref,
            send_ref,
            (step + tiles - high) % tiles,
        )


def merge_body(parts, heads, width, last):
    stats = [unpack3(part[:, width:].astype(F32), heads) for part in parts]
    top = functools.reduce(jnp.maximum, stats)
    scales = [jnp.exp(stat - top) for stat in stats]
    totals = [pltpu.roll(stat, LANES - 3 * heads, 1) for stat in stats]
    total = sum(scale * amount for scale, amount in zip(scales, totals))
    lane = lane_iota(total.shape)
    total = jnp.where(lane < heads, total, 1.0)
    if last:
        scales = [scale / total for scale in scales]
    spread = expander(heads, width)
    merged = sum(
        dot(pack3(scale, heads).astype(BF16), spread) * part[:, :width].astype(F32)
        for scale, part in zip(scales, parts)
    ).astype(BF16)
    if last:
        return merged
    stat = encode_stats(top, total, heads).astype(BF16)
    return jnp.concatenate([merged, stat], axis=1)


def merge_kernel(heads, width, counts, last, *refs):
    outs = refs[sum(counts) :]
    at = 0
    merged, groups = [], 0
    for count in counts:
        parts = [ref[...] for ref in refs[at : at + count]]
        at += count
        groups += parts[0].shape[0]
        flat = [part.reshape(-1, part.shape[-1]) for part in parts]
        merged.append(merge_body(flat, heads, width, last))
    if last:
        at = 0
        for rows in merged:
            outs[0][at : at + rows.shape[0]] = rows
            at += rows.shape[0]
        return
    size = math.prod(outs[0].shape[:-1]) // groups
    place = 0
    for rows in merged:
        rows = rows.astype(F32)
        for low in range(0, rows.shape[0], size * len(outs)):
            for k, out in enumerate(outs):
                piece = rows[low + k * size : low + (k + 1) * size].astype(BF16)
                if len(out.shape) == 3:
                    out[place] = piece
                else:
                    out[place * size : (place + 1) * size] = piece
            place += 1


def merge(groups, shapes, heads, width, last):
    parts = [part for group in groups for part in group]
    rows = sum(math.prod(part.shape[:-1]) for part in parts)
    return pl.pallas_call(
        functools.partial(merge_kernel, heads, width, [len(group) for group in groups], last),
        out_shape=[jax.ShapeDtypeStruct(shape, BF16) for shape in shapes],
        compiler_params=pltpu.CompilerParams(vmem_limit_bytes=MERGE_VMEM),
        cost_estimate=pl.CostEstimate(
            flops=rows * LANES * width * 2,
            bytes_accessed=rows * width * 4,
            transcendentals=rows * LANES,
        ),
        name="merge",
    )(*parts)


def stage_kernel(rows, columns, count, *refs):
    where_ref, meta_ref, valid_ref, table_ref = refs[:4]
    sources, out_ref = refs[4 : 4 + count], refs[4 + count]
    targets, sems = refs[5 + count : 5 + 2 * count], refs[5 + 2 * count]
    copies = [
        pltpu.make_async_copy(source, target, sems.at[at])
        for at, (source, target) in enumerate(zip(sources, targets))
    ]
    for copy in copies:
        copy.start()
    span, heads, _ = table_ref.shape
    pitch = 16
    n_rows, n_columns = valid_ref.shape
    keys = meta_ref.shape[1]
    lat, block = where_ref[0], where_ref[1]
    side = rows - 2 * rows * lat
    row_at = meta_ref[0:1] + meta_ref[1:2] * side
    column_at = meta_ref[2:3] + meta_ref[3:4] * (1 - 2 * (block & 1))

    far = column_at + block * columns
    far = jnp.where(far < 0, far + n_columns, far)
    far = jnp.where(far >= n_columns, far - n_columns, far)
    hot = lax.broadcasted_iota(jnp.int32, (n_columns, keys), 0) == far
    seen = dot(valid_ref[...].astype(F32).astype(BF16), jnp.where(hot, 1.0, 0.0).astype(BF16))
    mine = lax.broadcasted_iota(jnp.int32, (n_rows, keys), 0) == row_at + lat * rows
    allowed = jnp.sum(jnp.where(mine, seen, 0.0), axis=0, keepdims=True) > 0.5

    flat = [table_ref[up] for up in range(span)]
    gap = jnp.zeros((heads, pitch - span), F32)
    flat = jnp.concatenate([piece for up in flat for piece in (up, gap)], axis=1)
    pieces = jnp.concatenate(split3(flat), axis=0).astype(BF16)
    out_ref[...] = jnp.zeros(out_ref.shape, F32)
    place = lax.broadcasted_iota(jnp.int32, (span * pitch, keys), 0)
    for row in range(rows):
        for column in range(columns):
            up = row_at - row + HALF
            across = column_at - column + HALF
            inside = (up >= 0) & (up < span) & (across >= 0) & (across < span)
            index = jnp.where(inside, up * pitch + across, -1)
            found = dot(pieces, jnp.where(place == index, 1.0, 0.0).astype(BF16))
            found = found[:heads] + found[heads : 2 * heads] + found[2 * heads :]
            kept = (inside & allowed) | (index == HALF * pitch + HALF)
            out_ref[:, row * columns + column, :] = jnp.where(kept, found, -jnp.inf)
    for copy in copies:
        copy.wait()


def load_kernel(count, *refs):
    sems = refs[2 * count]
    copies = [
        pltpu.make_async_copy(refs[at], refs[count + at], sems.at[at]) for at in range(count)
    ]
    for copy in copies:
        copy.start()
    for copy in copies:
        copy.wait()


def project(window, gain_ref, w_agg, w_key, w_value):
    tokens = dot(window, w_agg[...]).astype(BF16)
    values = tokens.astype(F32)
    center = values - jnp.mean(values, axis=-1, keepdims=True)
    variance = jnp.mean(center * center, axis=-1, keepdims=True)
    normed = (center * lax.rsqrt(variance + EPS) * gain_ref[...]).astype(BF16)
    keys = dot(normed, w_key[...]).astype(BF16)
    values = dot(normed, w_value[...]).astype(BF16)
    return tokens, normed, keys, values


def gather_blocks(blocks, window):
    at = 0
    for block in blocks:
        size = block.shape[0]
        window[at : at + size] = block[...]
        at += size


def project_kernel(count, *refs):
    gain_ref, w_agg, w_query, w_key, w_value = refs[count : count + 5]
    token_ref, query_ref, near_key, near_value, window = refs[count + 5 :]
    gather_blocks(refs[:count], window)
    tokens, normed, keys, values = project(window[...], gain_ref, w_agg, w_key, w_value)
    token_ref[...] = tokens[:QROWS]
    query_ref[...] = dot(normed[:QROWS], w_query[...]).astype(BF16)
    near_key[...] = keys
    near_value[...] = values


def attend_kernel(heads, count, *refs):
    gain_ref, w_agg, w_key, w_value, w_out, bias_ref = refs[count : count + 6]
    token_ref, query_ref, near_key, near_value, out_ref = refs[count + 6 : count + 11]
    window, key_ref, value_ref, mix = refs[count + 11 :]
    width = window.shape[1]
    scale = 1.0 / math.sqrt(width // heads)
    near = near_key.shape[0]
    gather_blocks(refs[:count], window)
    _, _, keys, values = project(window[...], gain_ref, w_agg, w_key, w_value)
    key_ref[:near] = near_key[...]
    key_ref[near:] = keys
    value_ref[:near] = near_value[...]
    value_ref[near:] = values
    left = lane_iota((QROWS, LANES)) < LANES // 2
    pairs = [slice(at, at + LANES) for at in range(0, width, LANES)]
    logits = []
    for at in pairs:
        query = query_ref[:, at]
        zero = jnp.zeros_like(query)
        both = jnp.concatenate([jnp.where(left, query, zero), jnp.where(left, zero, query)], axis=0)
        logits.append(dot_nt(both, key_ref[:, at]))
    shares = []
    for pair, logit in enumerate(logits):
        bias = bias_ref[2 * pair : 2 * pair + 2]
        logit = logit * scale + bias.reshape(2 * QROWS, bias.shape[-1])
        raised = jnp.exp(logit - jnp.max(logit, axis=-1, keepdims=True))
        shares.append((raised / jnp.sum(raised, axis=-1, keepdims=True)).astype(BF16))
    mixed = [dot(share, value_ref[:, at]) for share, at in zip(shares, pairs)]
    for at, rows in zip(pairs, mixed):
        mix[:, at] = jnp.where(left, rows[:QROWS], rows[QROWS:]).astype(BF16)
    result = token_ref[...].astype(F32) + dot(mix[...], w_out[...])
    rows, columns, _ = out_ref.shape
    for row in range(rows):
        out_ref[row] = result[row * columns : (row + 1) * columns].astype(BF16)


def split_before(stages, number):
    return math.prod(radix for _, radix in stages[1 : min(number + 1, len(RADICES))])


def on_device(
    sizes,
    var_tokens,
    var_query,
    agg_key,
    agg_value,
    agg_out,
    norm_gain,
    nb_query,
    nb_key,
    nb_value,
    nb_out,
    pos_bias,
    valid,
):
    heads, head_dim = var_query.shape
    width = agg_key.shape[0]
    local_vars, rows, total_columns, _ = var_tokens.shape
    n_var, n_lat, n_lon = sizes
    devices = n_var * n_lon
    columns = total_columns // devices
    tile = TILE_BLOCKS * columns
    tiles = devices // TILE_BLOCKS
    packed = width + LANES
    half = tile // RADICES[0]
    lat = lax.axis_index("lat")
    block = lax.axis_index("var") * n_lon + lax.axis_index("lon")
    where = jnp.stack([lat, block]).astype(jnp.int32)
    block = where[1:]
    smem = pl.BlockSpec(memory_space=pltpu.SMEM)
    vmem = pl.BlockSpec(memory_space=pltpu.VMEM)
    hbm = pl.BlockSpec(memory_space=pltpu.HBM)

    weight = jax.ShapeDtypeStruct((width, width), BF16)
    lead_rows = rows - 2

    def pool_cost(count):
        work = count * total_columns * local_vars * width
        return pl.CostEstimate(flops=3 * work * width, bytes_accessed=2 * work, transcendentals=0)

    def lead_pool():
        folded = jax.ShapeDtypeStruct((width, LANES), BF16)
        first = jax.ShapeDtypeStruct((local_vars, tile, width), BF16)
        folded, held, first = pl.pallas_call(
            functools.partial(pre_kernel, heads, head_dim),
            in_specs=[hbm] * 4,
            out_specs=[vmem] * 3,
            out_shape=[folded, weight, first],
            scratch_shapes=[
                pltpu.VMEM(var_query.shape, F32),
                pltpu.VMEM((width, width), BF16),
                pltpu.SemaphoreType.DMA((4,)),
            ],
            compiler_params=pltpu.CompilerParams(vmem_limit_bytes=PRE_VMEM),
            name="pre",
        )(var_tokens, agg_value, var_query, agg_key)
        shape = jax.ShapeDtypeStruct((lead_rows * tiles, half, packed), BF16)
        later = (local_vars, rows - lead_rows, total_columns, width)
        keep, send, rest = pl.pallas_call(
            functools.partial(lead_kernel, heads, head_dim, lead_rows, tiles, columns),
            in_specs=[smem, hbm, vmem, vmem, vmem],
            out_specs=[vmem] * 3,
            out_shape=[shape, shape, jax.ShapeDtypeStruct(later, BF16)],
            scratch_shapes=[
                pltpu.VMEM((2, local_vars, tile, width), BF16),
                pltpu.SemaphoreType.DMA((3,)),
            ],
            compiler_params=pltpu.CompilerParams(vmem_limit_bytes=LEAD_VMEM),
            cost_estimate=pool_cost(lead_rows),
            name="lead",
        )(block, var_tokens, first, held, folded)
        return keep, send, folded, held, rest

    def pool(row, rest, held, folded):
        shape = jax.ShapeDtypeStruct((tiles, half, packed), BF16)
        return pl.pallas_call(
            functools.partial(pool_kernel, heads, head_dim, row, tiles, columns),
            in_specs=[smem] + [vmem] * 3,
            out_specs=[vmem] * 2,
            out_shape=[shape] * 2,
            compiler_params=pltpu.CompilerParams(vmem_limit_bytes=POOL_VMEM),
            cost_estimate=pool_cost(1),
            name="pool",
        )(block, rest, held, folded)

    def exchange(array, shift, stride, radix):
        def moved(i):
            digit = (i // stride) % radix
            return i + ((digit + shift) % radix - digit) * stride

        return lax.ppermute(array, ("var", "lon"), [(i, moved(i)) for i in range(devices)])

    stages, stride = [], 1
    for radix in RADICES:
        stages.append((stride, radix))
        stride *= radix
    if tiles > 1:
        stages.append((TILE_BLOCKS, tiles))

    def swap(sends, number, turned=False):
        stride, radix = stages[number]
        shifts = range(1, radix)
        if turned and number < len(RADICES) and radix == 4:
            shifts = (2, 3, 1)
        return [exchange(send, shift, stride, radix) for send, shift in zip(sends, shifts)]

    def next_split(groups, number, places, size):
        if number + 1 == len(stages):
            rows_left = sum(math.prod(group[0].shape[:-1]) for group in groups)
            return merge(groups, [(rows_left, width)], heads, width, True)
        radix = stages[number + 1][1]
        if number + 1 < len(RADICES):
            size //= radix
            shape = (places, size, packed) if size % 8 == 0 else (places * size, packed)
            return merge(groups, [shape] * radix, heads, width, False)
        (full,) = merge(groups, [(places * size, packed)], heads, width, False)
        full = full.reshape(places // tiles, tiles, size, packed)
        return [full[:, k].reshape(places // tiles * size, packed) for k in range(tiles)]

    barrier = lax.optimization_barrier
    keep_a, send_a, folded, held, rest = lead_pool()
    got_a = swap([send_a], 0)
    keep_b, send_b = pool(0, rest, held, folded)
    parts_a = next_split([[keep_a] + got_a], 0, lead_rows * tiles, half)
    got_b = swap([send_b], 0)
    parts_a, folded = barrier((parts_a, folded))
    got_a = swap(parts_a[1:], 1)
    keep_c, send_c = pool(1, rest, held, folded)
    got_c = swap([send_c], 0)
    keep_a = parts_a[0]
    keep_b = [[keep_b] + got_b, [keep_c] + got_c]

    places = [(0, 0), (0, -1), (0, 1), (1, 0), (1, -1), (1, 1)]
    patch = rows * columns
    dl = np.repeat([p[0] for p in places], patch)
    dx = np.repeat([p[1] for p in places], patch)
    row = np.tile(np.repeat(np.arange(rows), columns), len(places))
    column = np.tile(np.arange(columns), len(places) * rows)
    meta = jnp.asarray(np.stack([row, dl, column, dx * columns]), jnp.int32)
    keys = len(places) * patch
    for number in range(1, len(stages)):
        split_b, split_a = split_before(stages, number - 1), split_before(stages, number)
        parts_b = next_split(keep_b, number - 1, 2 * tiles, half // split_b)
        if number > 1:
            got_a, _ = barrier((got_a, parts_b))
        group_a = [keep_a] + got_a
        if number + 1 < len(stages):
            parts_a = next_split([group_a], number, lead_rows * tiles, half // split_a)
            if number == 1:
                parts_a, parts_b = barrier((parts_a, parts_b))
            keep_a, got_a = parts_a[0], swap(parts_a[1:], number + 1)
        keep_b = [[parts_b[0]] + swap(parts_b[1:], number, True)]
    (pooled,) = next_split([group_a] + keep_b, len(stages) - 1, 0, columns)

    staged = (agg_out, nb_query)
    pooled, where = barrier((pooled, where))
    bias, *staged = pl.pallas_call(
        functools.partial(stage_kernel, rows, columns, len(staged)),
        in_specs=[smem, vmem, vmem, vmem] + [hbm] * len(staged),
        out_specs=[vmem] * (1 + len(staged)),
        out_shape=[jax.ShapeDtypeStruct((heads, QROWS, keys), F32)] + [weight] * len(staged),
        scratch_shapes=[pltpu.SemaphoreType.DMA((len(staged),))],
        compiler_params=pltpu.CompilerParams(vmem_limit_bytes=STAGE_VMEM),
        cost_estimate=pl.CostEstimate(
            flops=1000, bytes_accessed=10 * width * width, transcendentals=0
        ),
        name="stage",
    )(where, meta, valid, jnp.transpose(pos_bias, (1, 0, 2)), *staged)

    def partner(array, kind):
        pairs = []
        for i in range(n_var * n_lat * n_lon):
            v, l, o = i // (n_lat * n_lon), (i // n_lon) % n_lat, i % n_lon
            b = v * n_lon + o
            if kind == "lat":
                l = n_lat - 1 - l
            elif kind == "core":
                b ^= 1
            else:
                b = (b + 1 if b % 2 else b - 1) % devices
            pairs.append((((b // n_lon) * n_lat + l) * n_lon + b % n_lon, i))
        return lax.ppermute(array, ("var", "lat", "lon"), pairs)

    far = partner(pooled, "odd")
    across = partner(pooled, "lat")
    near = partner(pooled, "core")
    far, across, bias = barrier((far, across, bias))
    window = [pooled, far, near, across]
    far_late = partner(far, "lat")
    last = (nb_key, nb_value, nb_out)
    last, _ = barrier((last, far))
    last = pl.pallas_call(
        functools.partial(load_kernel, len(last)),
        in_specs=[hbm] * len(last),
        out_specs=[vmem] * len(last),
        out_shape=[weight] * len(last),
        scratch_shapes=[pltpu.SemaphoreType.DMA((len(last),))],
        compiler_params=pltpu.CompilerParams(vmem_limit_bytes=LOAD_VMEM),
        cost_estimate=pl.CostEstimate(
            flops=1000, bytes_accessed=8 * width * width, transcendentals=0
        ),
        name="load",
    )(*last)

    gain = norm_gain.reshape(1, width)
    w_agg, w_query = staged
    across, last = barrier((across, last))
    w_key, w_value, w_out = last
    late = [far_late, partner(across, "core")]
    early = len(window) * patch
    tall = jax.ShapeDtypeStruct((QROWS, width), BF16)
    side = jax.ShapeDtypeStruct((early, width), BF16)
    projected = pl.pallas_call(
        functools.partial(project_kernel, len(window)),
        in_specs=[vmem] * (len(window) + 5),
        out_specs=[vmem] * 4,
        out_shape=[tall, tall, side, side],
        scratch_shapes=[pltpu.VMEM((early, width), BF16)],
        compiler_params=pltpu.CompilerParams(vmem_limit_bytes=MERGE_VMEM),
        cost_estimate=pl.CostEstimate(
            flops=6 * early * width * width, bytes_accessed=8 * width * width, transcendentals=0
        ),
        name="project",
    )(*window, gain, w_agg, w_query, w_key, w_value)
    return pl.pallas_call(
        functools.partial(attend_kernel, heads, len(late)),
        in_specs=[vmem] * (len(late) + 10),
        out_specs=vmem,
        out_shape=jax.ShapeDtypeStruct((rows, columns, width), BF16),
        scratch_shapes=[
            pltpu.VMEM((keys - early, width), BF16),
            pltpu.VMEM((keys, width), BF16),
            pltpu.VMEM((keys, width), BF16),
            pltpu.VMEM((QROWS, width), BF16),
        ],
        compiler_params=pltpu.CompilerParams(vmem_limit_bytes=MERGE_VMEM),
        name="attend",
    )(*late, gain, w_agg, w_key, w_value, w_out, bias, *projected)


def solution(mesh):
    sizes = (mesh.shape["var"], mesh.shape["lat"], mesh.shape["lon"])
    return jax.shard_map(
        functools.partial(on_device, sizes),
        mesh=mesh,
        in_specs=(P(("var", "lon"), "lat", None, None),) + (P(),) * 11,
        out_specs=P("lat", ("var", "lon"), None),
        check_vma=False,
    )
```
